32 devices in a mesh: clip: 8 (over y, x, core), tm: 4 (over z).
Axes of the slice: x: 2, y: 2, z: 4, core: 2. Of those that a mesh axis runs over, the one named last changes fastest.
Arguments:
- latent: bfloat16 [8, 32, 8, 32, 16], P('clip', 'tm'), may hold values from -6 to 6
- offsets: int32 [8], P('clip'), may hold values from 0 to 16
- teacher: bfloat16 [8, 32, 8, 16, 384], P('clip', 'tm'), may hold values from -6 to 6
- w_in: bfloat16 [432, 384], replicated, may hold values from -0.3125 to 0.3125
- w_mid: bfloat16 [10368, 384], P('clip'), may hold values from -0.0625 to 0.0625
Outputs:
- grad_mid: float32 [10368, 384], P('clip')
- grad_in: float32 [432, 384], replicated
The draws below stay inside these ranges and needn't reach their ends.
Inputs may be any that keep to these rules, and one draw needn't show every extreme that they name: `offsets`: each clip's crop start among the latent columns.
All inputs are finite; a program needn't handle non-finite values.
Results may differ from the reference program's by a relative error of at most 0.00095.
Values may be sent and summed in bfloat16 or wider, within the bound.
No kernel may reach another device: no remote copies, remote signals or barrier semaphores. Data moves between devices by JAX's collectives and lax.ppermute only.
A program may use at most 192 MiB of HBM per device.

```python
import math
import jax
import jax.numpy as jnp
from jax import lax

C = 384
LATC = 16
HH = 8
WW = 16
SPAN = 16
CLIPS = 8
FRAMES = 32
ROWS_MID = 10368
ROWS_IN = 432


def set_ends(result, key, least, high):
    place = [jax.random.randint(jax.random.fold_in(key, axis), (), 0, length) for axis, length in enumerate(result.shape)]
    main_axis = result.shape.index(max(result.shape))
    neighbour = place[:main_axis] + [(place[main_axis] + 1) % result.shape[main_axis]] + place[main_axis + 1:]
    return result.at[tuple(place)].set(least).at[tuple(neighbour)].set(high)


def shard_levels(stream_key, shape, split, smallest, high):
    def one(dim, blocks):
        draws = jax.random.uniform(jax.random.fold_in(jax.random.fold_in(stream_key, 6), dim), (blocks,), jnp.float32, smallest / len(split), high / len(split))
        return jnp.repeat(jnp.exp(draws), shape[dim] // blocks).reshape((-1,) + (1,) * (len(shape) - dim - 1))

    level = one(*split[0])
    for cut in split[1:]:
        level = level * one(*cut)
    return level


def normal_values(rng, shape, deviation, bound, pieces=(), kind=jnp.bfloat16):
    level = shard_levels(rng, shape, pieces, -0.22, 0.18) if pieces else 1.0
    drawn = jax.random.normal(rng, shape, jnp.float32) * deviation * level
    return jnp.minimum(jnp.maximum(drawn, -bound), bound).astype(kind)


def setup_inputs(seed: int = 0) -> dict:
    key_of = jax.random.split(jax.random.key(seed), 6)
    latent = normal_values(key_of[0], (CLIPS, FRAMES, HH, WW + SPAN, LATC), 1.0, 6.0, ((0, 8), (1, 4)))
    offsets = set_ends(jax.random.randint(key_of[1], (CLIPS,), 0, SPAN + 1), jax.random.fold_in(key_of[1], 1), 0, SPAN).astype(jnp.int32)
    teacher = normal_values(key_of[2], (CLIPS, FRAMES, HH, WW, C), 1.0, 6.0, ((0, 8), (1, 4)))
    w_in = normal_values(key_of[3], (ROWS_IN, C), ROWS_IN ** -0.5, 0.3125)
    w_mid = normal_values(key_of[4], (ROWS_MID, C), ROWS_MID ** -0.5, 0.0625, ((0, 8),))
    return {"latent": latent, "offsets": offsets, "teacher": teacher, "w_in": w_in, "w_mid": w_mid}


def gather_patches(padded, frames, rows, cols):
    parts = []
    for depth in range(3):
        for row_off in range(3):
            for col_off in range(3):
                parts.append(padded[depth:depth + frames, row_off:row_off + rows, col_off:col_off + cols, :])
    return jnp.concatenate(parts, axis=-1).reshape(frames * rows * cols, -1)

def spread_back(grad_low, w_full, frames, rows, cols, chans):
    total = jnp.zeros((frames + 2, rows + 2, cols + 2, chans), jnp.float32)
    width = 9 * chans
    for depth in range(3):
        taps = w_full[depth * width:(depth + 1) * width]
        piece = lax.dot_general(grad_low, taps, (((1,), (1,)), ((), ())), preferred_element_type=jnp.float32)
        piece = piece.reshape(frames, rows, cols, 9, chans)
        for k in range(9):
            row_off = k // 3
            col_off = k % 3
            total = total + jnp.pad(piece[:, :, :, k, :], ((depth, 2 - depth), (row_off, 2 - row_off), (col_off, 2 - col_off), (0, 0)))
    return total

def cross_dot(left, right):
    return lax.dot_general(left, right, (((0,), (0,)), ((), ())), preferred_element_type=jnp.float32)

def reference(latent, offsets, teacher, w_in, w_mid):
    scale = 2.0 / math.sqrt(CLIPS * FRAMES * HH * WW)

    def one_clip(carry, items):
        lat_clip, start, target = items
        crop = lax.dynamic_slice_in_dim(lat_clip, start, WW, axis=2)
        padded = jnp.pad(crop, ((2, 0), (1, 1), (1, 1), (0, 0)))
        patch_in = gather_patches(padded, FRAMES, HH, WW)
        z_first = jnp.dot(patch_in, w_in, preferred_element_type=jnp.float32)
        act = jax.nn.silu(z_first).astype(jnp.bfloat16)
        act_pad = jnp.pad(act.reshape(FRAMES, HH, WW, C), ((2, 0), (1, 1), (1, 1), (0, 0)))
        patch_mid = gather_patches(act_pad, FRAMES, HH, WW)
        output = jnp.dot(patch_mid, w_mid, preferred_element_type=jnp.float32)
        target_rows = target.reshape(FRAMES * HH * WW, C).astype(jnp.float32)
        grad_low = ((output - target_rows) * scale).astype(jnp.bfloat16)
        gmid = cross_dot(patch_mid, grad_low)
        adjoint = spread_back(grad_low, w_mid, FRAMES, HH, WW, C)
        dact = adjoint[2:, 1:-1, 1:-1, :].reshape(FRAMES * HH * WW, C)
        sig = jax.nn.sigmoid(z_first)
        dz_first = (dact * sig * (1.0 + z_first * (1.0 - sig))).astype(jnp.bfloat16)
        gin = cross_dot(patch_in, dz_first)
        return ((carry[0] + gmid, carry[1] + gin), None)
    start_carry = (jnp.zeros((ROWS_MID, C), jnp.float32), jnp.zeros((ROWS_IN, C), jnp.float32))
    totals, _ = lax.scan(one_clip, start_carry, (latent, offsets.astype(jnp.int32), teacher))
    return (totals[0], totals[1])
```

```python
import math

import jax
import jax.numpy as jnp
from jax import lax
from jax.experimental import pallas as pl
from jax.experimental.pallas import tpu as pltpu
from jax.sharding import PartitionSpec as P

F32 = jnp.float32
BF16 = jnp.bfloat16
CHUNKS = 3
VMEM = 56 * 1024 * 1024


def passed_along(block, axis, distance):
    devices = range(lax.axis_size(axis))
    route = [(i - distance, i) for i in devices if i - distance in devices]
    return lax.ppermute(block, axis, route)


def shifted(x, row_off, col_off, rows, cols):
    lanes = x.shape[1]
    lane = lax.broadcasted_iota(jnp.int32, (1, lanes), 1)
    row = (lane // cols) % rows + row_off
    col = lane % cols + col_off
    good = (row >= 0) & (row < rows) & (col >= 0) & (col < cols)
    shift = row_off * cols + col_off
    return jnp.where(good, pltpu.roll(x, (lanes - shift) % lanes, axis=1), 0.0)


def contract(left, right, dims):
    return lax.dot_general(left, right, (dims, ((), ())), preferred_element_type=F32)


def front_kernel(crop_ref, w_ref, patch_ref, z_ref, taps_ref, full_ref, *, rows, cols):
    plane = rows * cols
    lat = crop_ref.shape[0]
    count = patch_ref.shape[1]
    ext = count + 2 * plane

    @pl.when(pl.program_id(0) == 0)
    def _():
        crop = crop_ref[...].astype(F32)
        for spot in range(9):
            moved = shifted(crop, spot // 3 - 1, spot % 3 - 1, rows, cols).astype(BF16)
            for depth in range(3):
                first = (depth * 9 + spot) * lat
                full_ref[first : first + lat, :] = moved[:, depth * plane : depth * plane + ext]
        patch_ref[...] = full_ref[:, 2 * plane :]

    z = contract(w_ref[...], full_ref[...], ((0,), (0,)))
    z_ref[...] = z[:, 2 * plane :]
    act = (z * (1.0 / (1.0 + jnp.exp(-z)))).astype(BF16).astype(F32)
    for spot in range(9):
        moved = shifted(act, spot // 3 - 1, spot % 3 - 1, rows, cols).astype(BF16)
        for depth in range(3):
            taps_ref[depth * 9 + spot] = moved[:, depth * plane : depth * plane + count]


def front(crop_t, w_in, rows, cols, count):
    chans = w_in.shape[1]
    depth_in = w_in.shape[0]
    plane = rows * cols
    block = 128
    return pl.pallas_call(
        lambda *refs: front_kernel(*refs, rows=rows, cols=cols),
        grid=(chans // block,),
        in_specs=[
            pl.BlockSpec(crop_t.shape, lambda i: (0, 0)),
            pl.BlockSpec((depth_in, block), lambda i: (0, i)),
        ],
        out_specs=[
            pl.BlockSpec((depth_in, count), lambda i: (0, 0)),
            pl.BlockSpec((block, count), lambda i: (i, 0)),
            pl.BlockSpec((27, block, count), lambda i: (0, i, 0)),
        ],
        out_shape=[
            jax.ShapeDtypeStruct((depth_in, count), BF16),
            jax.ShapeDtypeStruct((chans, count), F32),
            jax.ShapeDtypeStruct((27, chans, count), BF16),
        ],
        scratch_shapes=[pltpu.VMEM((depth_in, count + 2 * plane), BF16)],
        compiler_params=pltpu.CompilerParams(vmem_limit_bytes=VMEM),
        name="front",
    )(crop_t, w_in)


def grad_kernel(order_ref, taps_ref, g_ref, out_ref):
    out_ref[0] = contract(taps_ref[...], g_ref[...], ((1,), (1,)))


def grad_chunk(order, taps, g_t, parts, which):
    blocks = order.shape[0]
    total, count = taps.shape
    chans = g_t.shape[0]
    rows = total // blocks // parts
    return pl.pallas_call(
        grad_kernel,
        grid_spec=pltpu.PrefetchScalarGridSpec(
            num_scalar_prefetch=1,
            grid=(blocks,),
            in_specs=[
                pl.BlockSpec((rows, count), lambda i, order: (order[i] * parts + which, 0)),
                pl.BlockSpec((chans, count), lambda i, order: (0, 0)),
            ],
            out_specs=pl.BlockSpec((1, rows, chans), lambda i, order: (i, 0, 0)),
        ),
        out_shape=jax.ShapeDtypeStruct((blocks, rows, chans), F32),
        compiler_params=pltpu.CompilerParams(vmem_limit_bytes=VMEM),
        name="grad",
    )(order, taps, g_t)


def back_kernel(g_ref, w_ref, z_ref, patch_ref, out_ref, acc_ref, *, rows, cols):
    plane = rows * cols
    count = z_ref.shape[1]
    spot = pl.program_id(0)
    moved = shifted(g_ref[...].astype(F32), 1 - spot // 3, 1 - spot % 3, rows, cols).astype(BF16)
    total = contract(w_ref[0, 0], moved[:, 2 * plane : 2 * plane + count], ((1,), (0,)))
    total += contract(w_ref[1, 0], moved[:, plane : plane + count], ((1,), (0,)))
    total += contract(w_ref[2, 0], moved[:, :count], ((1,), (0,)))

    @pl.when(spot == 0)
    def _():
        acc_ref[...] = total

    @pl.when(spot > 0)
    def _():
        acc_ref[...] += total

    @pl.when(spot == 8)
    def _():
        z = z_ref[...]
        sig = 1.0 / (1.0 + jnp.exp(-z))
        dz = (acc_ref[...] * sig * (1.0 + z * (1.0 - sig))).astype(BF16)
        out_ref[...] = contract(patch_ref[...], dz, ((1,), (1,)))


def back(g_ext, w_taps, z_t, patch_t, rows, cols):
    chans, count = z_t.shape
    depth_in = patch_t.shape[0]
    return pl.pallas_call(
        lambda *refs: back_kernel(*refs, rows=rows, cols=cols),
        grid=(9,),
        in_specs=[
            pl.BlockSpec(g_ext.shape, lambda i: (0, 0)),
            pl.BlockSpec((3, 1, chans, chans), lambda i: (0, i, 0, 0)),
            pl.BlockSpec((chans, count), lambda i: (0, 0)),
            pl.BlockSpec((depth_in, count), lambda i: (0, 0)),
        ],
        out_specs=pl.BlockSpec((depth_in, chans), lambda i: (0, 0)),
        out_shape=jax.ShapeDtypeStruct((depth_in, chans), F32),
        scratch_shapes=[pltpu.VMEM((chans, count), F32)],
        compiler_params=pltpu.CompilerParams(vmem_limit_bytes=VMEM),
        name="back",
    )(g_ext, w_taps, z_t, patch_t)


def reduced(part):
    half = part.shape[0] // 2
    clips = lax.axis_size("clip")
    swap = [(i, i ^ 1) for i in range(clips)]
    mine = part[half:] + lax.ppermute(part[:half], "clip", swap)
    groups = [[2 * p + core for p in range(half)] for core in range(2)]
    block = lax.all_to_all(mine, "clip", 0, 0, axis_index_groups=groups, tiled=True).sum(axis=0)
    depth = lax.axis_size("tm")
    rows, chans = block.shape
    piece = lax.all_to_all(block.reshape(depth, rows // depth, chans), "tm", 0, 0, tiled=True).sum(axis=0)
    spread = jnp.broadcast_to(piece[None], (depth,) + piece.shape)
    return lax.all_to_all(spread, "tm", 0, 0, tiled=True).reshape(rows, chans)


def shards(latent, offsets, teacher, w_in, w_mid):
    frames = teacher.shape[1]
    rows = teacher.shape[2]
    cols = teacher.shape[3]
    chans = teacher.shape[4]
    plane = rows * cols
    count = frames * plane
    lat_chans = latent.shape[4]
    clips = lax.axis_size("clip")
    total_cells = clips * lax.axis_size("tm") * count
    scale = 2.0 / math.sqrt(total_cells)
    w_full = lax.all_gather(w_mid, "clip", axis=0, tiled=True)
    crop = lax.dynamic_slice_in_dim(latent[0], offsets[0], cols, axis=2).reshape(count, lat_chans).T
    earlier = passed_along(crop[:, count - 4 * plane :], "tm", 1)
    crop_ext = jnp.concatenate([earlier, crop], axis=1)
    patch_t, z_t, taps = front(crop_ext, w_in, rows, cols, count)
    taps = taps.reshape(27 * chans, count)
    teacher_t = teacher[0].reshape(count, chans).T.astype(F32)
    h_t = contract(w_full, taps, ((0,), (0,)))
    g_t = ((h_t - teacher_t) * scale).astype(BF16)
    later = passed_along(g_t[:, : 2 * plane], "tm", -1)
    g_ext = jnp.concatenate([g_t, later], axis=1)

    core = lax.axis_index("clip") % 2
    even = 2 * jnp.arange(clips // 2, dtype=jnp.int32)
    order = jnp.concatenate([even + 1 - core, even + core])
    parts = [grad_chunk(order, taps, g_t, CHUNKS, j) for j in range(CHUNKS)]
    in_part = back(g_ext, w_full.reshape(3, 9, chans, chans), z_t, patch_t, rows, cols)
    done = [reduced(part) for part in parts]
    grad_mid = jnp.concatenate(done, axis=0)
    grad_in = lax.psum(in_part, ("clip", "tm"))
    return (grad_mid, grad_in)


def solution(mesh):
    return jax.shard_map(
        shards,
        mesh=mesh,
        in_specs=(
            P("clip", "tm", None, None, None),
            P("clip"),
            P("clip", "tm", None, None, None),
            P(),
            P("clip", None),
        ),
        out_specs=(P("clip", None), P()),
        check_vma=False,
    )
```

```python
import math

import jax
import jax.numpy as jnp
from jax import lax
from jax.experimental import pallas as pl
from jax.experimental.pallas import tpu as pltpu
from jax.sharding import PartitionSpec as P

F32 = jnp.float32
BF16 = jnp.bfloat16
F16 = jnp.float16
VMEM = 56 * 1024 * 1024


def passed_along(block, axis, distance):
    devices = range(lax.axis_size(axis))
    route = [(i - distance, i) for i in devices if i - distance in devices]
    return lax.ppermute(block, axis, route)


def swapped(block):
    return lax.ppermute(block, "clip", [(i, i ^ 1) for i in range(lax.axis_size("clip"))])


def padded(rows):
    return (rows // 16 + 1) * 16


def shifted(x, row_off, col_off, rows, cols):
    lanes = x.shape[1]
    lane = lax.broadcasted_iota(jnp.int32, (1, lanes), 1)
    row = (lane // cols) % rows + row_off
    col = lane % cols + col_off
    good = (row >= 0) & (row < rows) & (col >= 0) & (col < cols)
    shift = row_off * cols + col_off
    return jnp.where(good, pltpu.roll(x, (lanes - shift) % lanes, axis=1), 0.0)


def contract(left, right, dims):
    return lax.dot_general(left, right, (dims, ((), ())), preferred_element_type=F32)


def front_kernel(crop_ref, w_ref, patch_ref, z_ref, taps_ref, top_ref, full_ref, *, rows, cols):
    plane = rows * cols
    lat = crop_ref.shape[0]
    count = patch_ref.shape[1]
    ext = count + 2 * plane

    @pl.when(pl.program_id(0) == 0)
    def _():
        crop = crop_ref[...].astype(F32)
        for spot in range(9):
            moved = shifted(crop, spot // 3 - 1, spot % 3 - 1, rows, cols).astype(BF16)
            for depth in range(3):
                first = (depth * 9 + spot) * lat
                full_ref[first : first + lat, :] = moved[:, depth * plane : depth * plane + ext]
        patch_ref[...] = full_ref[:, 2 * plane :]

    z = contract(w_ref[...], full_ref[...], ((0,), (0,)))
    z_ref[...] = z[:, 2 * plane :]
    act = (z * (1.0 / (1.0 + jnp.exp(-z)))).astype(BF16).astype(F32)
    top_ref[...] = jnp.broadcast_to(jnp.max(jnp.abs(act), axis=1, keepdims=True), top_ref.shape)
    for spot in range(9):
        moved = shifted(act, spot // 3 - 1, spot % 3 - 1, rows, cols).astype(BF16)
        for depth in range(3):
            taps_ref[depth * 9 + spot] = moved[:, depth * plane : depth * plane + count]


def front(crop_t, w_in, rows, cols, count):
    chans = w_in.shape[1]
    depth_in = w_in.shape[0]
    plane = rows * cols
    block = 128
    return pl.pallas_call(
        lambda *refs: front_kernel(*refs, rows=rows, cols=cols),
        grid=(chans // block,),
        in_specs=[
            pl.BlockSpec(crop_t.shape, lambda i: (0, 0)),
            pl.BlockSpec((depth_in, block), lambda i: (0, i)),
        ],
        out_specs=[
            pl.BlockSpec((depth_in, count), lambda i: (0, 0)),
            pl.BlockSpec((block, count), lambda i: (i, 0)),
            pl.BlockSpec((27, block, count), lambda i: (0, i, 0)),
            pl.BlockSpec((block, 128), lambda i: (i, 0)),
        ],
        out_shape=[
            jax.ShapeDtypeStruct((depth_in, count), BF16),
            jax.ShapeDtypeStruct((chans, count), F32),
            jax.ShapeDtypeStruct((27, chans, count), BF16),
            jax.ShapeDtypeStruct((chans, 128), F32),
        ],
        scratch_shapes=[pltpu.VMEM((depth_in, count + 2 * plane), BF16)],
        compiler_params=pltpu.CompilerParams(vmem_limit_bytes=VMEM),
        name="front",
    )(crop_t, w_in)


def grad_kernel(order_ref, *refs):
    out_ref = refs[-1]
    blocks = out_ref.shape[0]
    rows = refs[0].shape[0]
    for i in range(blocks):
        total = contract(refs[2 * i][...], refs[2 * blocks][...], ((1,), (1,)))
        total += contract(refs[2 * i + 1][...], refs[2 * blocks + 1][...], ((1,), (1,)))
        out_ref[i, :rows, :] = total


def grad_chunk(order, taps, g_t, parts, which):
    blocks = order.shape[0]
    total, count = taps[0].shape
    chans = g_t[0].shape[0]
    rows = total // (2 * blocks) // parts
    at_once = 2
    tap_specs = []
    for i in range(at_once):
        spec = pl.BlockSpec((rows, count), lambda s, order, i=i: (order[s * at_once + i] * parts + which, 0))
        tap_specs += [spec, spec]
    whole = pl.BlockSpec((chans, count), lambda s, order: (0, 0))
    return pl.pallas_call(
        grad_kernel,
        grid_spec=pltpu.PrefetchScalarGridSpec(
            num_scalar_prefetch=1,
            grid=(blocks // at_once,),
            in_specs=tap_specs + [whole, whole],
            out_specs=pl.BlockSpec((at_once, padded(rows), chans), lambda s, order: (s, 0, 0)),
        ),
        out_shape=jax.ShapeDtypeStruct((blocks, padded(rows), chans), F32),
        compiler_params=pltpu.CompilerParams(vmem_limit_bytes=VMEM),
        name="grad",
    )(order, *(list(taps) * at_once), *g_t)


def back_kernel(g_ref, w_ref, z_ref, patch_ref, out_ref, acc_ref, *, rows, cols):
    plane = rows * cols
    count = z_ref.shape[1]
    spot = pl.program_id(0)
    moved = shifted(g_ref[...].astype(F32), 1 - spot // 3, 1 - spot % 3, rows, cols).astype(BF16)
    total = contract(w_ref[0, 0], moved[:, 2 * plane : 2 * plane + count], ((1,), (0,)))
    total += contract(w_ref[1, 0], moved[:, plane : plane + count], ((1,), (0,)))
    total += contract(w_ref[2, 0], moved[:, :count], ((1,), (0,)))

    @pl.when(spot == 0)
    def _():
        acc_ref[...] = total

    @pl.when(spot > 0)
    def _():
        acc_ref[...] += total

    @pl.when(spot == 8)
    def _():
        z = z_ref[...]
        sig = 1.0 / (1.0 + jnp.exp(-z))
        dz = (acc_ref[...] * sig * (1.0 + z * (1.0 - sig))).astype(BF16)
        out_ref[...] = contract(patch_ref[...], dz, ((1,), (1,)))


def back(g_ext, w_taps, z_t, patch_t, rows, cols):
    chans, count = z_t.shape
    depth_in = patch_t.shape[0]
    return pl.pallas_call(
        lambda *refs: back_kernel(*refs, rows=rows, cols=cols),
        grid=(9,),
        in_specs=[
            pl.BlockSpec(g_ext.shape, lambda i: (0, 0)),
            pl.BlockSpec((3, 1, chans, chans), lambda i: (0, i, 0, 0)),
            pl.BlockSpec((chans, count), lambda i: (0, 0)),
            pl.BlockSpec((depth_in, count), lambda i: (0, 0)),
        ],
        out_specs=pl.BlockSpec((depth_in, chans), lambda i: (0, 0)),
        out_shape=jax.ShapeDtypeStruct((depth_in, chans), F32),
        scratch_shapes=[pltpu.VMEM((chans, count), F32)],
        compiler_params=pltpu.CompilerParams(vmem_limit_bytes=VMEM),
        name="back",
    )(g_ext, w_taps, z_t, patch_t)


def packed(x, rows, bound):
    power = jnp.ceil(jnp.log2(jnp.maximum(bound, 1e-30)))
    row = lax.broadcasted_iota(jnp.int32, x.shape, 1)
    return jnp.where(row < rows, x * jnp.exp2(14.0 - power), power).astype(F16)


def unpacked(x, rows):
    power = x[:, rows : rows + 1, :1].astype(F32)
    return x[:, :rows].astype(F32) * jnp.exp2(power - 14.0), jnp.sum(jnp.exp2(power[:, 0, 0]))


def across_plane(part, rows, bound):
    clips = lax.axis_size("clip")
    groups = [[2 * p + core for p in range(clips // 2)] for core in range(2)]
    return lax.all_to_all(packed(part, rows, bound), "clip", 0, 0, axis_index_groups=groups, tiled=True)


def to_depth(pieces, rows, bound):
    extra = padded(rows) - rows
    return lax.all_to_all(packed(jnp.pad(pieces, ((0, 0), (0, extra), (0, 0))), rows, bound), "tm", 0, 0, tiled=True)


def across_depth(got, rows):
    terms, bound = unpacked(got, rows)
    block = terms.sum(axis=0)
    depth = lax.axis_size("tm")
    chans = block.shape[1]
    small = rows // depth
    return to_depth(block.reshape(depth, small, chans), small, bound)


def spread(got, small):
    terms, bound = unpacked(got, small)
    piece = terms.sum(axis=0)
    depth = lax.axis_size("tm")
    return to_depth(jnp.broadcast_to(piece[None], (depth,) + piece.shape), small, bound)


def everywhere(part):
    clips = lax.axis_size("clip")
    depth = lax.axis_size("tm")
    rows, chans = part.shape
    mine = lax.all_to_all(part.reshape(clips, rows // clips, chans), "clip", 0, 0, tiled=True).sum(axis=0)
    mine = lax.all_to_all(jnp.broadcast_to(mine[None], (depth,) + mine.shape), "tm", 0, 0, tiled=True).sum(axis=0)
    mine = lax.all_to_all(jnp.broadcast_to(mine[None], (clips,) + mine.shape), "clip", 0, 0, tiled=True)
    return mine.reshape(rows, chans)


def shards(latent, offsets, teacher, w_in, w_mid):
    frames = teacher.shape[1]
    rows = teacher.shape[2]
    cols = teacher.shape[3]
    chans = teacher.shape[4]
    plane = rows * cols
    count = frames * plane
    lat_chans = latent.shape[4]
    clips = lax.axis_size("clip")
    total_cells = clips * lax.axis_size("tm") * count
    scale = 2.0 / math.sqrt(total_cells)
    w_full = lax.all_gather(w_mid, "clip", axis=0, tiled=True)
    crop = lax.dynamic_slice_in_dim(latent[0], offsets[0], cols, axis=2).reshape(count, lat_chans).T
    earlier = passed_along(crop[:, count - 4 * plane :], "tm", 1)
    crop_ext = jnp.concatenate([earlier, crop], axis=1)
    patch_t, z_t, taps, top = front(crop_ext, w_in, rows, cols, count)
    taps = taps.reshape(27 * chans, count)
    _, _, pair_taps, pair_top = front(swapped(crop_ext), w_in, rows, cols, count)
    pair_taps = pair_taps.reshape(27 * chans, count)
    teacher_t = teacher[0].reshape(count, chans).T.astype(F32)
    h_t = contract(w_full, taps, ((0,), (0,)))
    g_t = ((h_t - teacher_t) * scale).astype(BF16)
    pair_g = swapped(g_t)
    later = passed_along(g_t[:, : 2 * plane], "tm", -1)

    core = lax.axis_index("clip") % 2
    order = 2 * jnp.arange(clips // 2, dtype=jnp.int32) + core
    depth = lax.axis_size("tm")
    block_rows = 27 * chans // clips
    chunks = next(c for c in (2, 3, 1) if block_rows % (8 * c) == 0 and block_rows % (depth * c) == 0)
    part_rows = block_rows // chunks
    parts = [grad_chunk(order, (taps, pair_taps), (g_t, pair_g), chunks, j) for j in range(chunks)]
    size = jnp.max(jnp.sum(jnp.abs(g_t.astype(F32)), axis=1))
    pair_size = jnp.max(jnp.sum(jnp.abs(pair_g.astype(F32)), axis=1))
    bound = (jnp.max(top) * size + jnp.max(pair_top) * pair_size) * 1.01
    g_ext, _ = lax.optimization_barrier((jnp.concatenate([g_t, later], axis=1), parts[1]))
    in_part = back(g_ext, w_full.reshape(3, 9, chans, chans), z_t, patch_t, rows, cols)
    plane_got = [across_plane(part, part_rows, bound) for part in parts]
    plane_got[0], in_part = lax.optimization_barrier((plane_got[0], in_part))
    depth_got = [across_depth(got, part_rows) for got in plane_got]
    grad_in = everywhere(in_part)
    small = part_rows // depth
    last_got = [spread(got, small) for got in depth_got]
    done = [unpacked(got, small)[0].reshape(part_rows, chans) for got in last_got]
    grad_mid = jnp.concatenate(done, axis=0)
    return (grad_mid, grad_in)


def solution(mesh):
    return jax.shard_map(
        shards,
        mesh=mesh,
        in_specs=(
            P("clip", "tm", None, None, None),
            P("clip"),
            P("clip", "tm", None, None, None),
            P(),
            P("clip", None),
        ),
        out_specs=(P("clip", None), P()),
        check_vma=False,
    )
```

```python
import math

import jax
import jax.numpy as jnp
from jax import lax
from jax.experimental import pallas as pl
from jax.experimental.pallas import tpu as pltpu
from jax.sharding import PartitionSpec as P

F32 = jnp.float32
BF16 = jnp.bfloat16
F16 = jnp.float16
VMEM = 56 * 1024 * 1024


def passed_along(block, axis, distance):
    devices = range(lax.axis_size(axis))
    route = [(i - distance, i) for i in devices if i - distance in devices]
    return lax.ppermute(block, axis, route)


def swapped(block):
    return lax.ppermute(block, "clip", [(i, i ^ 1) for i in range(lax.axis_size("clip"))])


def piece_rows(rows):
    return rows // lax.axis_size("tm") // 16 * 16 + 16


def padded(rows):
    return piece_rows(rows) * lax.axis_size("tm") + 16


def shifted(x, row_off, col_off, rows, cols):
    lanes = x.shape[1]
    lane = lax.broadcasted_iota(jnp.int32, (1, lanes), 1)
    row = (lane // cols) % rows + row_off
    col = lane % cols + col_off
    good = (row >= 0) & (row < rows) & (col >= 0) & (col < cols)
    shift = row_off * cols + col_off
    return jnp.where(good, pltpu.roll(x, (lanes - shift) % lanes, axis=1), 0.0)


def contract(left, right, dims):
    return lax.dot_general(left, right, (dims, ((), ())), preferred_element_type=F32)


def front_kernel(crop_ref, w_ref, patch_ref, z_ref, taps_ref, top_ref, full_ref, *, rows, cols):
    plane = rows * cols
    lat = crop_ref.shape[0]
    count = patch_ref.shape[1]
    ext = count + 2 * plane

    @pl.when(pl.program_id(0) == 0)
    def _():
        crop = crop_ref[...].astype(F32)
        for spot in range(9):
            moved = shifted(crop, spot // 3 - 1, spot % 3 - 1, rows, cols).astype(BF16)
            for depth in range(3):
                first = (depth * 9 + spot) * lat
                full_ref[first : first + lat, :] = moved[:, depth * plane : depth * plane + ext]
        patch_ref[...] = full_ref[:, 2 * plane :]

    z = contract(w_ref[...], full_ref[...], ((0,), (0,)))
    z_ref[...] = z[:, 2 * plane :]
    act = (z * (1.0 / (1.0 + jnp.exp(-z)))).astype(BF16).astype(F32)
    top_ref[...] = jnp.broadcast_to(jnp.max(jnp.abs(act), axis=1, keepdims=True), top_ref.shape)
    for spot in range(9):
        moved = shifted(act, spot // 3 - 1, spot % 3 - 1, rows, cols).astype(BF16)
        for depth in range(3):
            taps_ref[depth * 9 + spot] = moved[:, depth * plane : depth * plane + count]


def front(crop_t, w_in, rows, cols, count):
    chans = w_in.shape[1]
    depth_in = w_in.shape[0]
    plane = rows * cols
    block = 128
    return pl.pallas_call(
        lambda *refs: front_kernel(*refs, rows=rows, cols=cols),
        grid=(chans // block,),
        in_specs=[
            pl.BlockSpec(crop_t.shape, lambda i: (0, 0)),
            pl.BlockSpec((depth_in, block), lambda i: (0, i)),
        ],
        out_specs=[
            pl.BlockSpec((depth_in, count), lambda i: (0, 0)),
            pl.BlockSpec((block, count), lambda i: (i, 0)),
            pl.BlockSpec((27, block, count), lambda i: (0, i, 0)),
            pl.BlockSpec((block, 128), lambda i: (i, 0)),
        ],
        out_shape=[
            jax.ShapeDtypeStruct((depth_in, count), BF16),
            jax.ShapeDtypeStruct((chans, count), F32),
            jax.ShapeDtypeStruct((27, chans, count), BF16),
            jax.ShapeDtypeStruct((chans, 128), F32),
        ],
        scratch_shapes=[pltpu.VMEM((depth_in, count + 2 * plane), BF16)],
        compiler_params=pltpu.CompilerParams(vmem_limit_bytes=VMEM),
        name="front",
    )(crop_t, w_in)


def grad_kernel(order_ref, *refs):
    out_ref = refs[-1]
    blocks = out_ref.shape[0]
    rows = refs[0].shape[0]
    for i in range(blocks):
        total = contract(refs[2 * i][...], refs[2 * blocks][...], ((1,), (1,)))
        total += contract(refs[2 * i + 1][...], refs[2 * blocks + 1][...], ((1,), (1,)))
        out_ref[i, :rows, :] = total
        out_ref[i, rows:, :] = jnp.zeros((out_ref.shape[1] - rows, out_ref.shape[2]), F32)


def grad_chunk(order, taps, g_t, parts, which):
    blocks = order.shape[0]
    total, count = taps[0].shape
    chans = g_t[0].shape[0]
    rows = total // (2 * blocks) // parts
    at_once = 2
    tap_specs = []
    for i in range(at_once):
        spec = pl.BlockSpec((rows, count), lambda s, order, i=i: (order[s * at_once + i] * parts + which, 0))
        tap_specs += [spec, spec]
    whole = pl.BlockSpec((chans, count), lambda s, order: (0, 0))
    return pl.pallas_call(
        grad_kernel,
        grid_spec=pltpu.PrefetchScalarGridSpec(
            num_scalar_prefetch=1,
            grid=(blocks // at_once,),
            in_specs=tap_specs + [whole, whole],
            out_specs=pl.BlockSpec((at_once, padded(rows), chans), lambda s, order: (s, 0, 0)),
        ),
        out_shape=jax.ShapeDtypeStruct((blocks, padded(rows), chans), F32),
        compiler_params=pltpu.CompilerParams(vmem_limit_bytes=VMEM),
        name="grad",
    )(order, *(list(taps) * at_once), *g_t)


def back_kernel(g_ref, w_ref, z_ref, patch_ref, out_ref, acc_ref, *, rows, cols):
    plane = rows * cols
    count = z_ref.shape[1]
    spot = pl.program_id(0)
    moved = shifted(g_ref[...].astype(F32), 1 - spot // 3, 1 - spot % 3, rows, cols).astype(BF16)
    total = contract(w_ref[0, 0], moved[:, 2 * plane : 2 * plane + count], ((1,), (0,)))
    total += contract(w_ref[1, 0], moved[:, plane : plane + count], ((1,), (0,)))
    total += contract(w_ref[2, 0], moved[:, :count], ((1,), (0,)))

    @pl.when(spot == 0)
    def _():
        acc_ref[...] = total

    @pl.when(spot > 0)
    def _():
        acc_ref[...] += total

    @pl.when(spot == 8)
    def _():
        z = z_ref[...]
        sig = 1.0 / (1.0 + jnp.exp(-z))
        dz = (acc_ref[...] * sig * (1.0 + z * (1.0 - sig))).astype(BF16)
        out_ref[...] = contract(patch_ref[...], dz, ((1,), (1,)))


def back(g_ext, w_taps, z_t, patch_t, rows, cols):
    chans, count = z_t.shape
    depth_in = patch_t.shape[0]
    return pl.pallas_call(
        lambda *refs: back_kernel(*refs, rows=rows, cols=cols),
        grid=(9,),
        in_specs=[
            pl.BlockSpec(g_ext.shape, lambda i: (0, 0)),
            pl.BlockSpec((3, 1, chans, chans), lambda i: (0, i, 0, 0)),
            pl.BlockSpec((chans, count), lambda i: (0, 0)),
            pl.BlockSpec((depth_in, count), lambda i: (0, 0)),
        ],
        out_specs=pl.BlockSpec((depth_in, chans), lambda i: (0, 0)),
        out_shape=jax.ShapeDtypeStruct((depth_in, chans), F32),
        scratch_shapes=[pltpu.VMEM((chans, count), F32)],
        compiler_params=pltpu.CompilerParams(vmem_limit_bytes=VMEM),
        name="back",
    )(g_ext, w_taps, z_t, patch_t)


def packed(x, rows, bound):
    power = jnp.ceil(jnp.log2(jnp.maximum(bound, 1e-30)))
    row = lax.broadcasted_iota(jnp.int32, x.shape, 0)
    return jnp.where(row < rows, x * jnp.exp2(14.0 - power), power).astype(F16)


def power_of(x, rows):
    return jnp.exp2(x[rows, 0].astype(F32))


def across_plane(part, rows, bound, after):
    clips = lax.axis_size("clip")
    payloads = [packed(part[q], rows, bound) for q in range(1, clips // 2)]
    payloads, after = lax.optimization_barrier((payloads, after))
    got = []
    for q in range(1, clips // 2):
        route = [(i, i ^ (2 * q)) for i in range(clips)]
        got.append(lax.ppermute(payloads[q - 1], "clip", route))
    return (part[0], got), after


def around(blocks, distance):
    depth = lax.axis_size("tm")
    return lax.ppermute(blocks, "tm", [(i, (i + distance) % depth) for i in range(depth)])


def across_depth(own, got, rows, bound):
    depth = lax.axis_size("tm")
    me = lax.axis_index("tm")
    small = piece_rows(rows)
    powers = [power_of(x, rows) for x in got]
    total = (bound + sum(powers)) * 1.01

    def piece(place):
        first = place * small
        terms = lax.dynamic_slice_in_dim(own, first, small + 16, axis=0)
        for x, power in zip(got, powers):
            terms = terms + lax.dynamic_slice_in_dim(x, first, small + 16, axis=0).astype(F32) * (power * 2.0**-14)
        return terms

    others = [around(packed(piece((me + d) % depth), small, total), d) for d in range(1, depth)]
    return piece(me), others, total


def spread(own, got, small, bound):
    depth = lax.axis_size("tm")
    powers = [power_of(x, small) for x in got]
    total = (bound + sum(powers)) * 1.01
    for x, power in zip(got, powers):
        own = own + x.astype(F32) * (power * 2.0**-14)
    payload = packed(own, small, total)
    return [payload] + [around(payload, depth - k) for k in range(1, depth)]


def assembled(pieces, small, rows):
    depth = lax.axis_size("tm")
    me = lax.axis_index("tm")
    out = []
    for place in range(depth):
        x = pieces[0]
        for k in range(1, depth):
            x = jnp.where((me + k) % depth == place, pieces[k], x)
        count = min(small, rows - place * small)
        if count <= 0:
            break
        out.append(x[:count].astype(F32) * (power_of(x, small) * 2.0**-14))
    return out


def everywhere(part):
    clips = lax.axis_size("clip")
    depth = lax.axis_size("tm")
    rows, chans = part.shape
    mine = lax.all_to_all(part.reshape(clips, rows // clips, chans), "clip", 0, 0, tiled=True).sum(axis=0)
    mine = lax.all_to_all(jnp.broadcast_to(mine[None], (depth,) + mine.shape), "tm", 0, 0, tiled=True).sum(axis=0)
    mine = lax.all_to_all(jnp.broadcast_to(mine[None], (clips,) + mine.shape), "clip", 0, 0, tiled=True)
    return mine.reshape(rows, chans)


def shards(latent, offsets, teacher, w_in, w_mid):
    frames = teacher.shape[1]
    rows = teacher.shape[2]
    cols = teacher.shape[3]
    chans = teacher.shape[4]
    plane = rows * cols
    count = frames * plane
    lat_chans = latent.shape[4]
    clips = lax.axis_size("clip")
    total_cells = clips * lax.axis_size("tm") * count
    scale = 2.0 / math.sqrt(total_cells)
    w_full = lax.all_gather(w_mid, "clip", axis=0, tiled=True)
    crop = lax.dynamic_slice_in_dim(latent[0], offsets[0], cols, axis=2).reshape(count, lat_chans).T
    earlier = passed_along(crop[:, count - 4 * plane :], "tm", 1)
    crop_ext = jnp.concatenate([earlier, crop], axis=1)
    patch_t, z_t, taps, top = front(crop_ext, w_in, rows, cols, count)
    taps = taps.reshape(27 * chans, count)
    _, _, pair_taps, pair_top = front(swapped(crop_ext), w_in, rows, cols, count)
    pair_taps = pair_taps.reshape(27 * chans, count)
    teacher_t = teacher[0].reshape(count, chans).T.astype(F32)
    w_full, pair_taps, pair_top = lax.optimization_barrier((w_full, pair_taps, pair_top))
    h_t = contract(w_full, taps, ((0,), (0,)))
    g_t = ((h_t - teacher_t) * scale).astype(BF16)
    pair_g = swapped(g_t)
    later = passed_along(g_t[:, : 2 * plane], "tm", -1)

    order = lax.axis_index("clip") ^ (2 * jnp.arange(clips // 2, dtype=jnp.int32))
    block_rows = 27 * chans // clips
    chunks = next(c for c in (2, 3, 1) if block_rows % (8 * c) == 0)
    part_rows = block_rows // chunks
    size = jnp.max(jnp.sum(jnp.abs(g_t.astype(F32)), axis=1))
    pair_size = jnp.max(jnp.sum(jnp.abs(pair_g.astype(F32)), axis=1))
    bound = (jnp.max(top) * size + jnp.max(pair_top) * pair_size) * 1.01
    plane_got = []
    g_now = g_t
    for j in range(chunks):
        part = grad_chunk(order, (taps, pair_taps), (g_now, pair_g), chunks, j)
        got, g_now = across_plane(part, part_rows, bound, g_now)
        plane_got.append(got)
    g_ext = jnp.concatenate([g_now, later], axis=1)
    in_part = back(g_ext, w_full.reshape(3, 9, chans, chans), z_t, patch_t, rows, cols)
    plane_got[0], in_part = lax.optimization_barrier((plane_got[0], in_part))
    (own, got), in_part = lax.optimization_barrier((plane_got[0], in_part))
    plane_got[0] = (own, got)
    depth_got = [across_depth(own, got, part_rows, bound) for own, got in plane_got]
    grad_in = everywhere(in_part)
    small = piece_rows(part_rows)
    pieces = []
    for own, got, total in depth_got:
        pieces += assembled(spread(own, got, small, total), small, part_rows)
    return (jnp.concatenate(pieces, axis=0), grad_in)


def solution(mesh):
    return jax.shard_map(
        shards,
        mesh=mesh,
        in_specs=(
            P("clip", "tm", None, None, None),
            P("clip"),
            P("clip", "tm", None, None, None),
            P(),
            P("clip", None),
        ),
        out_specs=(P("clip", None), P()),
        check_vma=False,
    )
```

```python
import math

import jax
import jax.numpy as jnp
from jax import lax
from jax.experimental import pallas as pl
from jax.experimental.pallas import tpu as pltpu
from jax.sharding import PartitionSpec as P

F32 = jnp.float32
BF16 = jnp.bfloat16
F16 = jnp.float16
VMEM = 56 * 1024 * 1024


def passed_along(block, axis, distance):
    devices = range(lax.axis_size(axis))
    route = [(i - distance, i) for i in devices if i - distance in devices]
    return lax.ppermute(block, axis, route)


def swapped(block):
    return lax.ppermute(block, "clip", [(i, i ^ 1) for i in range(lax.axis_size("clip"))])


def piece_rows(rows):
    return rows // lax.axis_size("tm") // 16 * 16 + 16


def padded(rows):
    return piece_rows(rows) * lax.axis_size("tm") + 16


def shifted(x, row_off, col_off, rows, cols):
    lanes = x.shape[1]
    lane = lax.broadcasted_iota(jnp.int32, (1, lanes), 1)
    row = (lane // cols) % rows + row_off
    col = lane % cols + col_off
    good = (row >= 0) & (row < rows) & (col >= 0) & (col < cols)
    shift = row_off * cols + col_off
    return jnp.where(good, pltpu.roll(x, (lanes - shift) % lanes, axis=1), 0.0)


def contract(left, right, dims):
    return lax.dot_general(left, right, (dims, ((), ())), preferred_element_type=F32)


def front_kernel(crop_ref, w_ref, patch_ref, z_ref, taps_ref, top_ref, full_ref, *, rows, cols):
    plane = rows * cols
    lat = crop_ref.shape[0]
    count = patch_ref.shape[1]
    ext = count + 2 * plane

    @pl.when(pl.program_id(0) == 0)
    def _():
        crop = crop_ref[...].astype(F32)
        for spot in range(9):
            moved = shifted(crop, spot // 3 - 1, spot % 3 - 1, rows, cols).astype(BF16)
            for depth in range(3):
                first = (depth * 9 + spot) * lat
                full_ref[first : first + lat, :] = moved[:, depth * plane : depth * plane + ext]
        patch_ref[...] = full_ref[:, 2 * plane :]

    z = contract(w_ref[...], full_ref[...], ((0,), (0,)))
    z_ref[...] = z[:, 2 * plane :]
    act = (z * (1.0 / (1.0 + jnp.exp(-z)))).astype(BF16).astype(F32)
    top_ref[...] = jnp.broadcast_to(jnp.max(jnp.abs(act), axis=1, keepdims=True), top_ref.shape)
    for spot in range(9):
        moved = shifted(act, spot // 3 - 1, spot % 3 - 1, rows, cols).astype(BF16)
        for depth in range(3):
            taps_ref[depth * 9 + spot] = moved[:, depth * plane : depth * plane + count]


def front(crop_t, w_in, rows, cols, count):
    chans = w_in.shape[1]
    depth_in = w_in.shape[0]
    plane = rows * cols
    block = 128
    return pl.pallas_call(
        lambda *refs: front_kernel(*refs, rows=rows, cols=cols),
        grid=(chans // block,),
        in_specs=[
            pl.BlockSpec(crop_t.shape, lambda i: (0, 0)),
            pl.BlockSpec((depth_in, block), lambda i: (0, i)),
        ],
        out_specs=[
            pl.BlockSpec((depth_in, count), lambda i: (0, 0)),
            pl.BlockSpec((block, count), lambda i: (i, 0)),
            pl.BlockSpec((27, block, count), lambda i: (0, i, 0)),
            pl.BlockSpec((block, 128), lambda i: (i, 0)),
        ],
        out_shape=[
            jax.ShapeDtypeStruct((depth_in, count), BF16),
            jax.ShapeDtypeStruct((chans, count), F32),
            jax.ShapeDtypeStruct((27, chans, count), BF16),
            jax.ShapeDtypeStruct((chans, 128), F32),
        ],
        scratch_shapes=[pltpu.VMEM((depth_in, count + 2 * plane), BF16)],
        compiler_params=pltpu.CompilerParams(vmem_limit_bytes=VMEM),
        name="front",
    )(crop_t, w_in)


def grad_kernel(order_ref, *refs):
    out_ref = refs[-1]
    blocks = out_ref.shape[0]
    rows = refs[0].shape[0]
    for i in range(blocks):
        total = contract(refs[2 * i][...], refs[2 * blocks][...], ((1,), (1,)))
        total += contract(refs[2 * i + 1][...], refs[2 * blocks + 1][...], ((1,), (1,)))
        out_ref[i, :rows, :] = total
        out_ref[i, rows:, :] = jnp.zeros((out_ref.shape[1] - rows, out_ref.shape[2]), F32)


def grad_chunk(order, taps, g_t, parts, which):
    blocks = order.shape[0]
    total, count = taps[0].shape
    chans = g_t[0].shape[0]
    rows = total // (2 * blocks) // parts
    at_once = 2
    tap_specs = []
    for i in range(at_once):
        spec = pl.BlockSpec((rows, count), lambda s, order, i=i: (order[s * at_once + i] * parts + which, 0))
        tap_specs += [spec, spec]
    whole = pl.BlockSpec((chans, count), lambda s, order: (0, 0))
    return pl.pallas_call(
        grad_kernel,
        grid_spec=pltpu.PrefetchScalarGridSpec(
            num_scalar_prefetch=1,
            grid=(blocks // at_once,),
            in_specs=tap_specs + [whole, whole],
            out_specs=pl.BlockSpec((at_once, padded(rows), chans), lambda s, order: (s, 0, 0)),
        ),
        out_shape=jax.ShapeDtypeStruct((blocks, padded(rows), chans), F32),
        compiler_params=pltpu.CompilerParams(vmem_limit_bytes=VMEM),
        name="grad",
    )(order, *(list(taps) * at_once), *g_t)


def back_kernel(g_ref, w_ref, z_ref, patch_ref, out_ref, acc_ref, *, rows, cols):
    plane = rows * cols
    count = z_ref.shape[1]
    spot = pl.program_id(0)
    moved = shifted(g_ref[...].astype(F32), 1 - spot // 3, 1 - spot % 3, rows, cols).astype(BF16)
    total = contract(w_ref[0, 0], moved[:, 2 * plane : 2 * plane + count], ((1,), (0,)))
    total += contract(w_ref[1, 0], moved[:, plane : plane + count], ((1,), (0,)))
    total += contract(w_ref[2, 0], moved[:, :count], ((1,), (0,)))

    @pl.when(spot == 0)
    def _():
        acc_ref[...] = total

    @pl.when(spot > 0)
    def _():
        acc_ref[...] += total

    @pl.when(spot == 8)
    def _():
        z = z_ref[...]
        sig = 1.0 / (1.0 + jnp.exp(-z))
        dz = (acc_ref[...] * sig * (1.0 + z * (1.0 - sig))).astype(BF16)
        out_ref[...] = contract(patch_ref[...], dz, ((1,), (1,)))


def back(g_ext, w_taps, z_t, patch_t, rows, cols):
    chans, count = z_t.shape
    depth_in = patch_t.shape[0]
    return pl.pallas_call(
        lambda *refs: back_kernel(*refs, rows=rows, cols=cols),
        grid=(9,),
        in_specs=[
            pl.BlockSpec(g_ext.shape, lambda i: (0, 0)),
            pl.BlockSpec((3, 1, chans, chans), lambda i: (0, i, 0, 0)),
            pl.BlockSpec((chans, count), lambda i: (0, 0)),
            pl.BlockSpec((depth_in, count), lambda i: (0, 0)),
        ],
        out_specs=pl.BlockSpec((depth_in, chans), lambda i: (0, 0)),
        out_shape=jax.ShapeDtypeStruct((depth_in, chans), F32),
        scratch_shapes=[pltpu.VMEM((chans, count), F32)],
        compiler_params=pltpu.CompilerParams(vmem_limit_bytes=VMEM),
        name="back",
    )(g_ext, w_taps, z_t, patch_t)


def packed(x, rows, bound):
    power = jnp.ceil(jnp.log2(jnp.maximum(bound, 1e-30)))
    row = lax.broadcasted_iota(jnp.int32, x.shape, 0)
    return jnp.where(row < rows, x * jnp.exp2(14.0 - power), power).astype(F16)


def across_plane(part, rows, bound, after):
    clips = lax.axis_size("clip")
    payloads = [packed(part[q], rows, bound) for q in range(1, clips // 2)]
    payloads, after = lax.optimization_barrier((payloads, after))
    got = []
    for q in range(1, clips // 2):
        route = [(i, i ^ (2 * q)) for i in range(clips)]
        got.append(lax.ppermute(payloads[q - 1], "clip", route))
    return (part[0], got), after


def around(blocks, distance):
    depth = lax.axis_size("tm")
    return lax.ppermute(blocks, "tm", [(i, (i + distance) % depth) for i in range(depth)])


def scales(got, rows, bound):
    powers = [jnp.exp2(x[rows : rows + 1].astype(F32)) for x in got]
    return [power * 2.0**-14 for power in powers], (bound + sum(powers)) * 1.01


def across_depth(own, got, rows, factors, total, after):
    depth = lax.axis_size("tm")
    me = lax.axis_index("tm")
    small = piece_rows(rows)

    def piece(place):
        first = place * small
        terms = lax.dynamic_slice_in_dim(own, first, small + 16, axis=0)
        for x, factor in zip(got, factors):
            terms = terms + lax.dynamic_slice_in_dim(x, first, small + 16, axis=0).astype(F32) * factor
        return terms

    payloads = [packed(piece((me + d) % depth), small, total) for d in range(1, depth)]
    payloads, after = lax.optimization_barrier((payloads, after))
    others = [around(payloads[d - 1], d) for d in range(1, depth)]
    return (piece(me), others), after


def spread(own, got, small, factors, total):
    depth = lax.axis_size("tm")
    for x, factor in zip(got, factors):
        own = own + x.astype(F32) * factor
    payload = packed(own, small, total)
    return [payload] + [around(payload, depth - k) for k in range(1, depth)]


def assembled(pieces, factors, small, rows):
    depth = lax.axis_size("tm")
    me = lax.axis_index("tm")
    pieces = [x[:small].astype(F32) * factor for x, factor in zip(pieces, factors)]
    out = []
    for place in range(depth):
        x = pieces[0]
        for k in range(1, depth):
            x = jnp.where((me + k) % depth == place, pieces[k], x)
        count = min(small, rows - place * small)
        if count <= 0:
            break
        out.append(x[:count])
    return out


def everywhere(part):
    clips = lax.axis_size("clip")
    depth = lax.axis_size("tm")
    rows, chans = part.shape
    mine = lax.all_to_all(part.reshape(clips, rows // clips, chans), "clip", 0, 0, tiled=True).sum(axis=0)
    mine = lax.all_to_all(jnp.broadcast_to(mine[None], (depth,) + mine.shape), "tm", 0, 0, tiled=True).sum(axis=0)
    mine = lax.all_to_all(jnp.broadcast_to(mine[None], (clips,) + mine.shape), "clip", 0, 0, tiled=True)
    return mine.reshape(rows, chans)


def shards(latent, offsets, teacher, w_in, w_mid):
    frames = teacher.shape[1]
    rows = teacher.shape[2]
    cols = teacher.shape[3]
    chans = teacher.shape[4]
    plane = rows * cols
    count = frames * plane
    lat_chans = latent.shape[4]
    clips = lax.axis_size("clip")
    total_cells = clips * lax.axis_size("tm") * count
    scale = 2.0 / math.sqrt(total_cells)
    w_full = lax.all_gather(w_mid, "clip", axis=0, tiled=True)
    crop = lax.dynamic_slice_in_dim(latent[0], offsets[0], cols, axis=2).reshape(count, lat_chans).T
    earlier = passed_along(crop[:, count - 4 * plane :], "tm", 1)
    crop_ext = jnp.concatenate([earlier, crop], axis=1)
    patch_t, z_t, taps, top = front(crop_ext, w_in, rows, cols, count)
    taps = taps.reshape(27 * chans, count)
    _, _, pair_taps, pair_top = front(swapped(crop_ext), w_in, rows, cols, count)
    pair_taps = pair_taps.reshape(27 * chans, count)
    teacher_t = teacher[0].reshape(count, chans).T.astype(F32)
    w_full, pair_taps, pair_top = lax.optimization_barrier((w_full, pair_taps, pair_top))
    h_t = contract(w_full, taps, ((0,), (0,)))
    g_t = ((h_t - teacher_t) * scale).astype(BF16)
    pair_g = swapped(g_t)
    later = passed_along(g_t[:, : 2 * plane], "tm", -1)

    order = lax.axis_index("clip") ^ (2 * jnp.arange(clips // 2, dtype=jnp.int32))
    block_rows = 27 * chans // clips
    chunks = next(c for c in (2, 3, 1) if block_rows % (8 * c) == 0)
    part_rows = block_rows // chunks
    size = jnp.max(jnp.sum(jnp.abs(g_t.astype(F32)), axis=1))
    pair_size = jnp.max(jnp.sum(jnp.abs(pair_g.astype(F32)), axis=1))
    bound = (jnp.max(top) * size + jnp.max(pair_top) * pair_size) * 1.01
    plane_got = []
    g_now = g_t
    for j in range(chunks):
        part = grad_chunk(order, (taps, pair_taps), (g_now, pair_g), chunks, j)
        got, g_now = across_plane(part, part_rows, bound, g_now)
        plane_got.append(got)
    factors, total = scales(plane_got[0][1], part_rows, bound)
    first, g_now = across_depth(*plane_got[0], part_rows, factors, total, g_now)
    depth_got = [first]
    g_ext = jnp.concatenate([g_now, later], axis=1)
    in_part = back(g_ext, w_full.reshape(3, 9, chans, chans), z_t, patch_t, rows, cols)
    for own, got in plane_got[1:]:
        got, in_part = lax.optimization_barrier((got, in_part))
        more, in_part = across_depth(own, got, part_rows, factors, total, in_part)
        depth_got.append(more)
    grad_in = everywhere(in_part)
    small = piece_rows(part_rows)
    factors, total = scales(depth_got[0][1], small, total)
    last = []
    for own, got in depth_got:
        if last:
            got, last[-1][0] = lax.optimization_barrier((got, last[-1][0]))
        last.append(spread(own, got, small, factors, total))
    factors, _ = scales(last[0], small, 0.0)
    pieces = []
    for got in last:
        pieces += assembled(got, factors, small, part_rows)
    return (jnp.concatenate(pieces, axis=0), grad_in)


def solution(mesh):
    return jax.shard_map(
        shards,
        mesh=mesh,
        in_specs=(
            P("clip", "tm", None, None, None),
            P("clip"),
            P("clip", "tm", None, None, None),
            P(),
            P("clip", None),
        ),
        out_specs=(P("clip", None), P()),
        check_vma=False,
    )
```

```python
import math

import jax
import jax.numpy as jnp
from jax import lax
from jax.experimental import pallas as pl
from jax.experimental.pallas import tpu as pltpu
from jax.sharding import PartitionSpec as P

F32 = jnp.float32
BF16 = jnp.bfloat16
F16 = jnp.float16
VMEM = 56 * 1024 * 1024


def passed_along(block, axis, distance):
    devices = range(lax.axis_size(axis))
    route = [(i - distance, i) for i in devices if i - distance in devices]
    return lax.ppermute(block, axis, route)


def swapped(block):
    return lax.ppermute(block, "clip", [(i, i ^ 1) for i in range(lax.axis_size("clip"))])


def piece_rows(rows):
    return rows // lax.axis_size("tm") // 16 * 16 + 16


def padded(rows):
    return piece_rows(rows) * lax.axis_size("tm") + 16


def shifted(x, row_off, col_off, rows, cols):
    lanes = x.shape[1]
    lane = lax.broadcasted_iota(jnp.int32, (1, lanes), 1)
    row = (lane // cols) % rows + row_off
    col = lane % cols + col_off
    good = (row >= 0) & (row < rows) & (col >= 0) & (col < cols)
    shift = row_off * cols + col_off
    return jnp.where(good, pltpu.roll(x, (lanes - shift) % lanes, axis=1), 0.0)


def contract(left, right, dims):
    return lax.dot_general(left, right, (dims, ((), ())), preferred_element_type=F32)


def fill_columns(out_ref, x, rows, cols):
    cells, chans = x.shape
    frames = cells // (rows * cols)
    zero = jnp.zeros((frames, cols, chans), BF16)
    place = lax.broadcasted_iota(jnp.int32, (cells, 1), 0) % cols
    for c in range(3):
        moved = x
        if c != 1:
            good = (place + c - 1 >= 0) & (place + c - 1 < cols)
            moved = jnp.where(good, pltpu.roll(x, (1 - c) % cells, axis=0), 0.0)
        out_ref[c, :, 0] = zero
        out_ref[c, :, rows + 1] = zero
        out_ref[c, :, 1 : rows + 1] = moved.astype(BF16).reshape(frames, rows, cols, chans)


def window(ref, column, frame, row, frames, rows):
    x = ref[column, pl.ds(frame, frames), pl.ds(row, rows)]
    return x.reshape(frames * rows * x.shape[2], x.shape[3])


def front_kernel(crop_ref, w_ref, *refs, rows, cols, first):
    if first:
        patch_ref, z_ref, cells_ref, taps_ref, top_ref, full_ref = refs
    else:
        taps_ref, top_ref, full_ref = refs
    plane = rows * cols
    lat = crop_ref.shape[0]
    ext = full_ref.shape[1]
    count = ext - 2 * plane

    @pl.when(pl.program_id(0) == 0)
    def _():
        crop = crop_ref[...].astype(F32)
        for spot in range(9):
            moved = shifted(crop, spot // 3 - 1, spot % 3 - 1, rows, cols).astype(BF16)
            for depth in range(3):
                at = (depth * 9 + spot) * lat
                full_ref[at : at + lat, :] = moved[:, depth * plane : depth * plane + ext]
        if first:
            patch_ref[...] = full_ref[:, 2 * plane :]

    z = contract(w_ref[...], full_ref[...], ((0,), (0,)))
    act = (z * (1.0 / (1.0 + jnp.exp(-z)))).astype(BF16).astype(F32)
    top_ref[...] = jnp.broadcast_to(jnp.max(jnp.abs(act), axis=1, keepdims=True), top_ref.shape)
    for spot in range(9):
        moved = shifted(act, spot // 3 - 1, spot % 3 - 1, rows, cols).astype(BF16)
        for depth in range(3):
            taps_ref[depth * 9 + spot] = moved[:, depth * plane : depth * plane + count]
    if first:
        z_ref[...] = z[:, 2 * plane :].T
        fill_columns(cells_ref, act.T, rows, cols)


def front(crop_t, w_in, rows, cols, count, first):
    chans = w_in.shape[1]
    depth_in = w_in.shape[0]
    plane = rows * cols
    block = 128
    frames = count // plane + 2
    specs = [
        pl.BlockSpec((27, block, count), lambda i: (0, i, 0)),
        pl.BlockSpec((block, 128), lambda i: (i, 0)),
    ]
    shapes = [
        jax.ShapeDtypeStruct((27, chans, count), BF16),
        jax.ShapeDtypeStruct((chans, 128), F32),
    ]
    if first:
        specs = [
            pl.BlockSpec((depth_in, count), lambda i: (0, 0)),
            pl.BlockSpec((count, block), lambda i: (0, i)),
            pl.BlockSpec((3, frames, rows + 2, cols, block), lambda i: (0, 0, 0, 0, i)),
        ] + specs
        shapes = [
            jax.ShapeDtypeStruct((depth_in, count), BF16),
            jax.ShapeDtypeStruct((count, chans), F32),
            jax.ShapeDtypeStruct((3, frames, rows + 2, cols, chans), BF16),
        ] + shapes
    return pl.pallas_call(
        lambda *refs: front_kernel(*refs, rows=rows, cols=cols, first=first),
        grid=(chans // block,),
        in_specs=[
            pl.BlockSpec(crop_t.shape, lambda i: (0, 0)),
            pl.BlockSpec((depth_in, block), lambda i: (0, i)),
        ],
        out_specs=specs,
        out_shape=shapes,
        scratch_shapes=[pltpu.VMEM((depth_in, count + 2 * plane), BF16)],
        compiler_params=pltpu.CompilerParams(vmem_limit_bytes=VMEM),
        name="front",
    )(crop_t, w_in)


def middle_kernel(cells_ref, w_ref, teacher_ref, g_ref, size_ref, acc_ref, *, scale):
    depth = pl.program_id(0)
    frames = cells_ref.shape[1] - 2
    rows = cells_ref.shape[2] - 2
    chans = w_ref.shape[2]
    left = jnp.concatenate(
        [window(cells_ref, k % 3, depth, k // 3, frames, rows) for k in range(9)], axis=1
    )
    total = contract(left, w_ref[...].reshape(9 * chans, chans), ((1,), (0,)))

    @pl.when(depth == 0)
    def _():
        acc_ref[...] = total

    @pl.when(depth == 1)
    def _():
        acc_ref[...] += total

    @pl.when(depth == 2)
    def _():
        g = ((acc_ref[...] + total - teacher_ref[...].astype(F32)) * scale).astype(BF16)
        g_ref[...] = g
        size = jnp.max(jnp.sum(jnp.abs(g.astype(F32)), axis=0, keepdims=True), axis=1, keepdims=True)
        size_ref[...] = jnp.broadcast_to(size, size_ref.shape)


def middle(cells, w_taps, teacher, scale):
    count, chans = teacher.shape
    return pl.pallas_call(
        lambda *refs: middle_kernel(*refs, scale=scale),
        grid=(3,),
        in_specs=[
            pl.BlockSpec(cells.shape, lambda i: (0,) * 5),
            pl.BlockSpec((9, chans, chans), lambda i: (i, 0, 0)),
            pl.BlockSpec((count, chans), lambda i: (0, 0)),
        ],
        out_specs=[
            pl.BlockSpec((count, chans), lambda i: (0, 0)),
            pl.BlockSpec((8, 128), lambda i: (0, 0)),
        ],
        out_shape=[
            jax.ShapeDtypeStruct((count, chans), BF16),
            jax.ShapeDtypeStruct((8, 128), F32),
        ],
        scratch_shapes=[pltpu.VMEM((count, chans), F32)],
        compiler_params=pltpu.CompilerParams(vmem_limit_bytes=VMEM),
        name="middle",
    )(cells, w_taps, teacher)


def grad_kernel(order_ref, *refs):
    own_ref, out_ref = refs[-2:]
    at_once = (len(refs) - 4) // 2
    rows = refs[0].shape[0]
    zero = jnp.zeros((own_ref.shape[0] - rows, own_ref.shape[1]), F32)
    for i in range(at_once):
        total = contract(refs[2 * i][...], refs[2 * at_once][...], ((1,), (0,)))
        total += contract(refs[2 * i + 1][...], refs[2 * at_once + 1][...], ((1,), (0,)))
        if i == 0:
            @pl.when(pl.program_id(0) == 0)
            def _():
                own_ref[:rows, :] = total
                own_ref[rows:, :] = zero

        out_ref[i, :rows, :] = total
        out_ref[i, rows:, :] = zero


def grad_chunk(order, taps, g, parts, which):
    blocks = order.shape[0]
    total, count = taps[0].shape
    chans = g[0].shape[1]
    rows = total // (2 * blocks) // parts
    at_once = 2
    tap_specs = []
    for i in range(at_once):
        spec = pl.BlockSpec((rows, count), lambda s, order, i=i: (order[s * at_once + i] * parts + which, 0))
        tap_specs += [spec, spec]
    whole = pl.BlockSpec((count, chans), lambda s, order: (0, 0))
    return pl.pallas_call(
        grad_kernel,
        grid_spec=pltpu.PrefetchScalarGridSpec(
            num_scalar_prefetch=1,
            grid=(blocks // at_once,),
            in_specs=tap_specs + [whole, whole],
            out_specs=[
                pl.BlockSpec((padded(rows), chans), lambda s, order: (0, 0)),
                pl.BlockSpec((at_once, padded(rows), chans), lambda s, order: (s, 0, 0)),
            ],
        ),
        out_shape=[
            jax.ShapeDtypeStruct((padded(rows), chans), F32),
            jax.ShapeDtypeStruct((blocks, padded(rows), chans), F32),
        ],
        compiler_params=pltpu.CompilerParams(vmem_limit_bytes=VMEM),
        name="grad",
    )(order, *(list(taps) * at_once), *g)


def back_kernel(g_ref, later_ref, w_ref, z_ref, patch_ref, out_ref, cells_ref, acc_ref, *, rows, cols):
    depth = pl.program_id(0)
    frames = cells_ref.shape[1] - 2

    @pl.when(depth == 0)
    def _():
        g = jnp.concatenate([g_ref[...], later_ref[...]], axis=0).astype(F32)
        fill_columns(cells_ref, g, rows, cols)

    left = jnp.concatenate(
        [window(cells_ref, 2 - k % 3, 2 - depth, 2 - k // 3, frames, rows) for k in range(9)], axis=1
    )
    right = jnp.concatenate([w_ref[k] for k in range(9)], axis=1)
    total = contract(left, right, ((1,), (1,)))

    @pl.when(depth == 0)
    def _():
        acc_ref[...] = total

    @pl.when(depth == 1)
    def _():
        acc_ref[...] += total

    @pl.when(depth == 2)
    def _():
        z = z_ref[...]
        sig = 1.0 / (1.0 + jnp.exp(-z))
        dz = ((acc_ref[...] + total) * sig * (1.0 + z * (1.0 - sig))).astype(BF16)
        out_ref[...] = contract(patch_ref[...], dz, ((1,), (0,)))


def back(g, later, w_taps, z, patch_t, rows, cols):
    count, chans = z.shape
    depth_in = patch_t.shape[0]
    frames = count // (rows * cols) + 2
    return pl.pallas_call(
        lambda *refs: back_kernel(*refs, rows=rows, cols=cols),
        grid=(3,),
        in_specs=[
            pl.BlockSpec(g.shape, lambda i: (0, 0)),
            pl.BlockSpec(later.shape, lambda i: (0, 0)),
            pl.BlockSpec((9, chans, chans), lambda i: (i, 0, 0)),
            pl.BlockSpec((count, chans), lambda i: (0, 0)),
            pl.BlockSpec((depth_in, count), lambda i: (0, 0)),
        ],
        out_specs=pl.BlockSpec((depth_in, chans), lambda i: (0, 0)),
        out_shape=jax.ShapeDtypeStruct((depth_in, chans), F32),
        scratch_shapes=[
            pltpu.VMEM((3, frames, rows + 2, cols, chans), BF16),
            pltpu.VMEM((count, chans), F32),
        ],
        compiler_params=pltpu.CompilerParams(vmem_limit_bytes=VMEM),
        name="back",
    )(g, later, w_taps, z, patch_t)


def packed(x, rows, bound):
    power = jnp.ceil(jnp.log2(jnp.maximum(bound, 1e-30)))
    row = lax.broadcasted_iota(jnp.int32, x.shape, 0)
    return jnp.where(row < rows, x * jnp.exp2(14.0 - power), power).astype(F16)


def across_plane(part, rows, bound, after):
    clips = lax.axis_size("clip")
    payloads = [packed(part[q], rows, bound) for q in range(1, clips // 2)]
    payloads, after = lax.optimization_barrier((payloads, after))
    got = []
    for q in range(1, clips // 2):
        route = [(i, i ^ (2 * q)) for i in range(clips)]
        got.append(lax.ppermute(payloads[q - 1], "clip", route))
    return got, after


def around(blocks, distance):
    depth = lax.axis_size("tm")
    return lax.ppermute(blocks, "tm", [(i, (i + distance) % depth) for i in range(depth)])


def scales(got, rows, bound):
    powers = [jnp.exp2(x[rows : rows + 1].astype(F32)) for x in got]
    return [power * 2.0**-14 for power in powers], (bound + sum(powers)) * 1.01


def across_depth(own, got, rows, factors, total, after, at_once):
    depth = lax.axis_size("tm")
    me = lax.axis_index("tm")
    small = piece_rows(rows)

    def piece(place):
        first = place * small
        terms = lax.dynamic_slice_in_dim(own, first, small + 16, axis=0)
        for x, factor in zip(got, factors):
            terms = terms + lax.dynamic_slice_in_dim(x, first, small + 16, axis=0).astype(F32) * factor
        return terms

    if at_once:
        payload = jnp.concatenate([packed(piece(d), small, total) for d in range(depth)], axis=0)
        payload, after = lax.optimization_barrier((payload, after))
        got = lax.all_to_all(payload, "tm", 0, 0, tiled=True)
        return (None, [got[d * (small + 16) : (d + 1) * (small + 16)] for d in range(depth)]), after
    payloads = [packed(piece((me + d) % depth), small, total) for d in range(1, depth)]
    payloads, after = lax.optimization_barrier((payloads, after))
    others = [around(payloads[d - 1], d) for d in range(1, depth)]
    return (piece(me), others), after


def spread(own, got, small, factors, total):
    depth = lax.axis_size("tm")
    terms = [x.astype(F32) * factor for x, factor in zip(got, factors)]
    own = sum(terms) if own is None else own + sum(terms)
    payload = packed(own, small, total)
    return [payload] + [around(payload, depth - k) for k in range(1, depth)]


def assembled(pieces, factors, small, rows):
    depth = lax.axis_size("tm")
    me = lax.axis_index("tm")
    pieces = [x[:small].astype(F32) * factor for x, factor in zip(pieces, factors)]
    out = []
    for place in range(depth):
        x = pieces[0]
        for k in range(1, depth):
            x = jnp.where((me + k) % depth == place, pieces[k], x)
        count = min(small, rows - place * small)
        if count <= 0:
            break
        out.append(x[:count])
    return out


def cast_to_all(block, axis):
    size = lax.axis_size(axis)
    return lax.all_to_all(jnp.broadcast_to(block[None], (size,) + block.shape), axis, 0, 0, tiled=True)


def shards(latent, offsets, teacher, w_in, w_mid):
    frames = teacher.shape[1]
    rows = teacher.shape[2]
    cols = teacher.shape[3]
    chans = teacher.shape[4]
    plane = rows * cols
    count = frames * plane
    lat_chans = latent.shape[4]
    clips = lax.axis_size("clip")
    total_cells = clips * lax.axis_size("tm") * count
    scale = 2.0 / math.sqrt(total_cells)
    w_full = lax.all_gather(w_mid, "clip", axis=0, tiled=True)
    crop = lax.dynamic_slice_in_dim(latent[0], offsets[0], cols, axis=2).reshape(count, lat_chans).T
    earlier = passed_along(crop[:, count - 4 * plane :], "tm", 1)
    crop_ext = jnp.concatenate([earlier, crop], axis=1)
    patch_t, z, cells, taps, top = front(crop_ext, w_in, rows, cols, count, True)
    pair_taps, pair_top = front(swapped(crop_ext), w_in, rows, cols, count, False)
    taps = taps.reshape(27 * chans, count)
    pair_taps = pair_taps.reshape(27 * chans, count)
    w_full, pair_taps, pair_top = lax.optimization_barrier((w_full, pair_taps, pair_top))
    w_taps = w_full.reshape(27, chans, chans)
    g, size = middle(cells, w_taps, teacher[0].reshape(count, chans), scale)
    pair_g = swapped(g)
    pair_size = swapped(size)
    later = passed_along(g[: 2 * plane], "tm", -1)

    order = lax.axis_index("clip") ^ (2 * jnp.arange(clips // 2, dtype=jnp.int32))
    block_rows = 27 * chans // clips
    chunks = next(c for c in (2, 3, 1) if block_rows % (8 * c) == 0)
    part_rows = block_rows // chunks
    bound = (jnp.max(top) * size[:1, :1] + jnp.max(pair_top) * pair_size[:1, :1]) * 1.01
    plane_got = []
    g_now = g
    for j in range(chunks):
        own, part = grad_chunk(order, (taps, pair_taps), (g_now, pair_g), chunks, j)
        got, g_now = across_plane(part, part_rows, bound, g_now)
        later, g_now = lax.optimization_barrier((later, g_now))
        plane_got.append((own, got))
    factors, total = scales(plane_got[0][1], part_rows, bound)
    first, g_now = across_depth(*plane_got[0], part_rows, factors, total, g_now, True)
    depth_got = [first]
    in_part = back(g_now, later, w_taps, z, patch_t, rows, cols)
    for own, got in plane_got[1:]:
        got, in_part = lax.optimization_barrier((got, in_part))
        more, in_part = across_depth(own, got, part_rows, factors, total, in_part, False)
        depth_got.append(more)
    in_rows = in_part.shape[0]
    in_got = lax.all_to_all(in_part.reshape(clips, in_rows // clips, chans), "clip", 0, 0, tiled=True)
    small = piece_rows(part_rows)
    factors, total = scales(depth_got[0][1], small, 0.0)
    last = []
    for own, got in depth_got:
        if last:
            in_got, got, last[-1][0] = lax.optimization_barrier((in_got, got, last[-1][0]))
            factors, _ = scales(got, small, 0.0)
        last.append(spread(own, got, small, factors, total))
        if len(last) == 2:
            in_got = cast_to_all(in_got.sum(axis=0), "tm")
    if len(last) == 1:
        in_got = cast_to_all(in_got.sum(axis=0), "tm")
    grad_in = cast_to_all(in_got.sum(axis=0), "clip").reshape(in_rows, chans)
    factors, _ = scales(last[0], small, 0.0)
    pieces = []
    for got in last:
        pieces += assembled(got, factors, small, part_rows)
    return (jnp.concatenate(pieces, axis=0), grad_in)


def solution(mesh):
    return jax.shard_map(
        shards,
        mesh=mesh,
        in_specs=(
            P("clip", "tm", None, None, None),
            P("clip"),
            P("clip", "tm", None, None, None),
            P(),
            P("clip", None),
        ),
        out_specs=(P("clip", None), P()),
        check_vma=False,
    )
```

```python
import math

import jax
import jax.numpy as jnp
from jax import lax
from jax.experimental import pallas as pl
from jax.experimental.pallas import tpu as pltpu
from jax.sharding import PartitionSpec as P

F32 = jnp.float32
BF16 = jnp.bfloat16
F16 = jnp.float16
VMEM = 56 * 1024 * 1024


def passed_along(block, axis, distance):
    devices = range(lax.axis_size(axis))
    route = [(i - distance, i) for i in devices if i - distance in devices]
    return lax.ppermute(block, axis, route)


def swapped(block):
    return lax.ppermute(block, "clip", [(i, i ^ 1) for i in range(lax.axis_size("clip"))])


def piece_rows(rows):
    return rows // lax.axis_size("tm") // 16 * 16 + 16


def padded(rows):
    return piece_rows(rows) * lax.axis_size("tm") + 16


def shifted(x, row_off, col_off, rows, cols):
    lanes = x.shape[1]
    lane = lax.broadcasted_iota(jnp.int32, (1, lanes), 1)
    row = (lane // cols) % rows + row_off
    col = lane % cols + col_off
    good = (row >= 0) & (row < rows) & (col >= 0) & (col < cols)
    shift = row_off * cols + col_off
    return jnp.where(good, pltpu.roll(x, (lanes - shift) % lanes, axis=1), 0.0)


def contract(left, right, dims):
    return lax.dot_general(left, right, (dims, ((), ())), preferred_element_type=F32)


def fill_columns(out_ref, x, rows, cols):
    cells, chans = x.shape
    frames = cells // (rows * cols)
    zero = jnp.zeros((frames, cols, chans), BF16)
    place = lax.broadcasted_iota(jnp.int32, (cells, 1), 0) % cols
    for c in range(3):
        moved = x
        if c != 1:
            good = (place + c - 1 >= 0) & (place + c - 1 < cols)
            moved = jnp.where(good, pltpu.roll(x, (1 - c) % cells, axis=0), 0.0)
        out_ref[c, :, 0] = zero
        out_ref[c, :, rows + 1] = zero
        out_ref[c, :, 1 : rows + 1] = moved.astype(BF16).reshape(frames, rows, cols, chans)


def window(ref, column, frame, row, frames, rows):
    x = ref[column, pl.ds(frame, frames), pl.ds(row, rows)]
    return x.reshape(frames * rows * x.shape[2], x.shape[3])


def front_kernel(crop_ref, w_ref, *refs, rows, cols, first):
    if first:
        patch_ref, z_ref, cells_ref, taps_ref, top_ref, full_ref = refs
    else:
        taps_ref, top_ref, full_ref = refs
    plane = rows * cols
    lat = crop_ref.shape[0]
    ext = full_ref.shape[1]
    count = ext - 2 * plane

    @pl.when(pl.program_id(0) == 0)
    def _():
        crop = crop_ref[...].astype(F32)
        for spot in range(9):
            moved = shifted(crop, spot // 3 - 1, spot % 3 - 1, rows, cols).astype(BF16)
            for depth in range(3):
                at = (depth * 9 + spot) * lat
                full_ref[at : at + lat, :] = moved[:, depth * plane : depth * plane + ext]
        if first:
            patch_ref[...] = full_ref[:, 2 * plane :]

    z = contract(w_ref[...], full_ref[...], ((0,), (0,)))
    act = (z * (1.0 / (1.0 + jnp.exp(-z)))).astype(BF16).astype(F32)
    top_ref[...] = jnp.broadcast_to(jnp.max(jnp.abs(act), axis=1, keepdims=True), top_ref.shape)
    for spot in range(9):
        moved = shifted(act, spot // 3 - 1, spot % 3 - 1, rows, cols).astype(BF16)
        for depth in range(3):
            taps_ref[depth * 9 + spot] = moved[:, depth * plane : depth * plane + count]
    if first:
        z_ref[...] = z[:, 2 * plane :].T
        fill_columns(cells_ref, act.T, rows, cols)


def front(crop_t, w_in, rows, cols, count, first):
    chans = w_in.shape[1]
    depth_in = w_in.shape[0]
    plane = rows * cols
    block = 128
    frames = count // plane + 2
    specs = [
        pl.BlockSpec((27, block, count), lambda i: (0, i, 0)),
        pl.BlockSpec((block, 128), lambda i: (i, 0)),
    ]
    shapes = [
        jax.ShapeDtypeStruct((27, chans, count), BF16),
        jax.ShapeDtypeStruct((chans, 128), F32),
    ]
    if first:
        specs = [
            pl.BlockSpec((depth_in, count), lambda i: (0, 0)),
            pl.BlockSpec((count, block), lambda i: (0, i)),
            pl.BlockSpec((3, frames, rows + 2, cols, block), lambda i: (0, 0, 0, 0, i)),
        ] + specs
        shapes = [
            jax.ShapeDtypeStruct((depth_in, count), BF16),
            jax.ShapeDtypeStruct((count, chans), F32),
            jax.ShapeDtypeStruct((3, frames, rows + 2, cols, chans), BF16),
        ] + shapes
    return pl.pallas_call(
        lambda *refs: front_kernel(*refs, rows=rows, cols=cols, first=first),
        grid=(chans // block,),
        in_specs=[
            pl.BlockSpec(crop_t.shape, lambda i: (0, 0)),
            pl.BlockSpec((depth_in, block), lambda i: (0, i)),
        ],
        out_specs=specs,
        out_shape=shapes,
        scratch_shapes=[pltpu.VMEM((depth_in, count + 2 * plane), BF16)],
        compiler_params=pltpu.CompilerParams(vmem_limit_bytes=VMEM),
        name="front",
    )(crop_t, w_in)


def middle_kernel(cells_ref, w_ref, teacher_ref, g_ref, size_ref, acc_ref, *, scale):
    depth = pl.program_id(0)
    frames = cells_ref.shape[1] - 2
    rows = cells_ref.shape[2] - 2
    chans = w_ref.shape[2]
    left = jnp.concatenate(
        [window(cells_ref, k % 3, depth, k // 3, frames, rows) for k in range(9)], axis=1
    )
    total = contract(left, w_ref[...].reshape(9 * chans, chans), ((1,), (0,)))

    @pl.when(depth == 0)
    def _():
        acc_ref[...] = total

    @pl.when(depth == 1)
    def _():
        acc_ref[...] += total

    @pl.when(depth == 2)
    def _():
        g = ((acc_ref[...] + total - teacher_ref[...].astype(F32)) * scale).astype(BF16)
        g_ref[...] = g
        size = jnp.max(jnp.sum(jnp.abs(g.astype(F32)), axis=0, keepdims=True), axis=1, keepdims=True)
        size_ref[...] = jnp.broadcast_to(size, size_ref.shape)


def middle(cells, w_taps, teacher, scale):
    count, chans = teacher.shape
    return pl.pallas_call(
        lambda *refs: middle_kernel(*refs, scale=scale),
        grid=(3,),
        in_specs=[
            pl.BlockSpec(cells.shape, lambda i: (0,) * 5),
            pl.BlockSpec((9, chans, chans), lambda i: (i, 0, 0)),
            pl.BlockSpec((count, chans), lambda i: (0, 0)),
        ],
        out_specs=[
            pl.BlockSpec((count, chans), lambda i: (0, 0)),
            pl.BlockSpec((8, 128), lambda i: (0, 0)),
        ],
        out_shape=[
            jax.ShapeDtypeStruct((count, chans), BF16),
            jax.ShapeDtypeStruct((8, 128), F32),
        ],
        scratch_shapes=[pltpu.VMEM((count, chans), F32)],
        compiler_params=pltpu.CompilerParams(vmem_limit_bytes=VMEM),
        name="middle",
    )(cells, w_taps, teacher)


def grad_kernel(order_ref, *refs, units):
    own_ref, out_ref = refs[-2:]
    g_refs = refs[-4:-2]
    at_once = out_ref.shape[0]
    rows = refs[0].shape[0]
    spare = own_ref.shape[0] - units * rows
    zero = jnp.zeros((spare, own_ref.shape[1]), F32)
    for i in range(at_once):
        for k in range(units):
            at = 2 * (i * units + k)
            total = contract(refs[at][...], g_refs[0][...], ((1,), (0,)))
            total += contract(refs[at + 1][...], g_refs[1][...], ((1,), (0,)))
            out_ref[i, k * rows : (k + 1) * rows, :] = total
        out_ref[i, units * rows :, :] = zero

    @pl.when(pl.program_id(0) == 0)
    def _():
        own_ref[...] = out_ref[0]


def grad_chunk(order, taps, g, first, units):
    blocks = order.shape[0]
    total, count = taps[0].shape
    chans = g[0].shape[1]
    rows = total // (2 * blocks) // 3
    at_once = 2 // units
    tap_specs = []
    for i in range(at_once):
        for k in range(units):
            spec = pl.BlockSpec(
                (rows, count), lambda s, order, i=i, k=k: (order[s * at_once + i] * 3 + first + k, 0)
            )
            tap_specs += [spec, spec]
    whole = pl.BlockSpec((count, chans), lambda s, order: (0, 0))
    size = padded(rows * units)
    return pl.pallas_call(
        lambda *refs: grad_kernel(*refs, units=units),
        grid_spec=pltpu.PrefetchScalarGridSpec(
            num_scalar_prefetch=1,
            grid=(blocks // at_once,),
            in_specs=tap_specs + [whole, whole],
            out_specs=[
                pl.BlockSpec((size, chans), lambda s, order: (0, 0)),
                pl.BlockSpec((at_once, size, chans), lambda s, order: (s, 0, 0)),
            ],
        ),
        out_shape=[
            jax.ShapeDtypeStruct((size, chans), F32),
            jax.ShapeDtypeStruct((blocks, size, chans), F32),
        ],
        compiler_params=pltpu.CompilerParams(vmem_limit_bytes=VMEM),
        name="grad",
    )(order, *(list(taps) * 2), *g)


def back_kernel(g_ref, later_ref, w_ref, z_ref, patch_ref, out_ref, cells_ref, acc_ref, *, rows, cols):
    depth = pl.program_id(0)
    frames = cells_ref.shape[1] - 2

    @pl.when(depth == 0)
    def _():
        g = jnp.concatenate([g_ref[...], later_ref[...]], axis=0).astype(F32)
        fill_columns(cells_ref, g, rows, cols)

    left = jnp.concatenate(
        [window(cells_ref, 2 - k % 3, 2 - depth, 2 - k // 3, frames, rows) for k in range(9)], axis=1
    )
    right = jnp.concatenate([w_ref[k] for k in range(9)], axis=1)
    total = contract(left, right, ((1,), (1,)))

    @pl.when(depth == 0)
    def _():
        acc_ref[...] = total

    @pl.when(depth == 1)
    def _():
        acc_ref[...] += total

    @pl.when(depth == 2)
    def _():
        z = z_ref[...]
        sig = 1.0 / (1.0 + jnp.exp(-z))
        dz = ((acc_ref[...] + total) * sig * (1.0 + z * (1.0 - sig))).astype(BF16)
        out_ref[...] = contract(patch_ref[...], dz, ((1,), (0,)))


def back(g, later, w_taps, z, patch_t, rows, cols):
    count, chans = z.shape
    depth_in = patch_t.shape[0]
    frames = count // (rows * cols) + 2
    return pl.pallas_call(
        lambda *refs: back_kernel(*refs, rows=rows, cols=cols),
        grid=(3,),
        in_specs=[
            pl.BlockSpec(g.shape, lambda i: (0, 0)),
            pl.BlockSpec(later.shape, lambda i: (0, 0)),
            pl.BlockSpec((9, chans, chans), lambda i: (i, 0, 0)),
            pl.BlockSpec((count, chans), lambda i: (0, 0)),
            pl.BlockSpec((depth_in, count), lambda i: (0, 0)),
        ],
        out_specs=pl.BlockSpec((depth_in, chans), lambda i: (0, 0)),
        out_shape=jax.ShapeDtypeStruct((depth_in, chans), F32),
        scratch_shapes=[
            pltpu.VMEM((3, frames, rows + 2, cols, chans), BF16),
            pltpu.VMEM((count, chans), F32),
        ],
        compiler_params=pltpu.CompilerParams(vmem_limit_bytes=VMEM),
        name="back",
    )(g, later, w_taps, z, patch_t)


def packed(x, rows, bound):
    power = jnp.ceil(jnp.log2(jnp.maximum(bound, 1e-30)))
    row = lax.broadcasted_iota(jnp.int32, x.shape, 0)
    return jnp.where(row < rows, x * jnp.exp2(14.0 - power), power).astype(F16)


def across_plane(part, rows, bound, after):
    clips = lax.axis_size("clip")
    payloads = [packed(part[q], rows, bound) for q in range(1, clips // 2)]
    payloads, after = lax.optimization_barrier((payloads, after))
    got = []
    for q in range(1, clips // 2):
        route = [(i, i ^ (2 * q)) for i in range(clips)]
        got.append(lax.ppermute(payloads[q - 1], "clip", route))
    return got, after


def around(blocks, distance):
    depth = lax.axis_size("tm")
    return lax.ppermute(blocks, "tm", [(i, (i + distance) % depth) for i in range(depth)])


def scales(got, rows, bound):
    powers = [jnp.exp2(x[rows : rows + 1].astype(F32)) for x in got]
    return [power * 2.0**-14 for power in powers], (bound + sum(powers)) * 1.01


def across_depth(own, got, rows, factors, total, after, at_once):
    depth = lax.axis_size("tm")
    me = lax.axis_index("tm")
    small = piece_rows(rows)

    def piece(place):
        first = place * small
        terms = lax.dynamic_slice_in_dim(own, first, small + 16, axis=0)
        for x, factor in zip(got, factors):
            terms = terms + lax.dynamic_slice_in_dim(x, first, small + 16, axis=0).astype(F32) * factor
        return terms

    if at_once:
        payload = jnp.concatenate([packed(piece(d), small, total) for d in range(depth)], axis=0)
        payload, after = lax.optimization_barrier((payload, after))
        got = lax.all_to_all(payload, "tm", 0, 0, tiled=True)
        return (None, [got[d * (small + 16) : (d + 1) * (small + 16)] for d in range(depth)]), after
    payloads = [packed(piece((me + d) % depth), small, total) for d in range(1, depth)]
    payloads, after = lax.optimization_barrier((payloads, after))
    others = [around(payloads[d - 1], d) for d in range(1, depth)]
    return (piece(me), others), after


def spread(own, got, small, factors, total):
    depth = lax.axis_size("tm")
    terms = [x.astype(F32) * factor for x, factor in zip(got, factors)]
    own = sum(terms) if own is None else own + sum(terms)
    payload = packed(own, small, total)
    return [payload] + [around(payload, depth - k) for k in range(1, depth)]


def assembled(pieces, factors, small, rows):
    depth = lax.axis_size("tm")
    me = lax.axis_index("tm")
    pieces = [x[:small].astype(F32) * factor for x, factor in zip(pieces, factors)]
    out = []
    for place in range(depth):
        x = pieces[0]
        for k in range(1, depth):
            x = jnp.where((me + k) % depth == place, pieces[k], x)
        count = min(small, rows - place * small)
        if count <= 0:
            break
        out.append(x[:count])
    return out


def shards(latent, offsets, teacher, w_in, w_mid):
    frames = teacher.shape[1]
    rows = teacher.shape[2]
    cols = teacher.shape[3]
    chans = teacher.shape[4]
    plane = rows * cols
    count = frames * plane
    lat_chans = latent.shape[4]
    clips = lax.axis_size("clip")
    total_cells = clips * lax.axis_size("tm") * count
    scale = 2.0 / math.sqrt(total_cells)
    w_full = lax.all_gather(w_mid, "clip", axis=0, tiled=True)
    crop = lax.dynamic_slice_in_dim(latent[0], offsets[0], cols, axis=2).reshape(count, lat_chans).T
    earlier = passed_along(crop[:, count - 4 * plane :], "tm", 1)
    crop_ext = jnp.concatenate([earlier, crop], axis=1)
    patch_t, z, cells, taps, top = front(crop_ext, w_in, rows, cols, count, True)
    pair_taps, pair_top = front(swapped(crop_ext), w_in, rows, cols, count, False)
    taps = taps.reshape(27 * chans, count)
    pair_taps = pair_taps.reshape(27 * chans, count)
    w_full, pair_taps, pair_top = lax.optimization_barrier((w_full, pair_taps, pair_top))
    w_taps = w_full.reshape(27, chans, chans)
    g, size = middle(cells, w_taps, teacher[0].reshape(count, chans), scale)
    pair_g = swapped(g)
    pair_size = swapped(size)
    later = passed_along(g[: 2 * plane], "tm", -1)

    order = lax.axis_index("clip") ^ (2 * jnp.arange(clips // 2, dtype=jnp.int32))
    third = 27 * chans // clips // 3
    bound = (jnp.max(top) * size[:1, :1] + jnp.max(pair_top) * pair_size[:1, :1]) * 1.01
    both = (taps, pair_taps)
    in_rows = patch_t.shape[0]

    own_a, part = grad_chunk(order, both, (g, pair_g), 0, 2)
    got_a, g = across_plane(part, 2 * third, bound, g)
    in_part = back(g, later, w_taps, z, patch_t, rows, cols)
    in_got = lax.all_to_all(in_part.reshape(clips, in_rows // clips, chans), "clip", 0, 0, tiled=True)
    g, in_part = lax.optimization_barrier((g, in_part))
    own_b, part = grad_chunk(order, both, (g, pair_g), 2, 1)
    got_b, got_a = across_plane(part, third, bound, got_a)

    factors, total = scales(got_a, 2 * third, bound)
    (_, depth_a), in_got = across_depth(own_a, got_a, 2 * third, factors, total, in_got, True)
    in_sum = in_got.sum(axis=0)
    got_b, _ = lax.optimization_barrier((got_b, in_sum))
    (own_b, depth_b), _ = across_depth(own_b, got_b, third, factors, total, total, False)
    in_sum, depth_a = lax.optimization_barrier((in_sum, depth_a))
    in_sum = jnp.broadcast_to(in_sum[None], (lax.axis_size("tm"),) + in_sum.shape)
    in_sum, depth_a = lax.optimization_barrier((in_sum, depth_a))
    in_got = lax.all_to_all(in_sum, "tm", 0, 0, tiled=True)
    small_a = piece_rows(2 * third)
    small_b = piece_rows(third)
    factors, total = scales(depth_a, small_a, 0.0)
    last_a = spread(None, depth_a, small_a, factors, total)
    depth_b, last_a[0] = lax.optimization_barrier((depth_b, last_a[0]))
    factors, _ = scales(depth_b, small_b, 0.0)
    last_b = spread(own_b, depth_b, small_b, factors, total)
    in_sum = in_got.sum(axis=0)
    in_sum = jnp.broadcast_to(in_sum[None], (clips,) + in_sum.shape)
    in_sum, last_a = lax.optimization_barrier((in_sum, last_a))
    grad_in = lax.all_to_all(in_sum, "clip", 0, 0, tiled=True).reshape(in_rows, chans)
    factors, _ = scales(last_a, small_a, 0.0)
    pieces = assembled(last_a, factors, small_a, 2 * third) + assembled(last_b, factors, small_b, third)
    return (jnp.concatenate(pieces, axis=0), grad_in)


def solution(mesh):
    return jax.shard_map(
        shards,
        mesh=mesh,
        in_specs=(
            P("clip", "tm", None, None, None),
            P("clip"),
            P("clip", "tm", None, None, None),
            P(),
            P("clip", None),
        ),
        out_specs=(P("clip", None), P()),
        check_vma=False,
    )
```

```python
import math

import jax
import jax.numpy as jnp
from jax import lax
from jax.experimental import pallas as pl
from jax.experimental.pallas import tpu as pltpu
from jax.sharding import PartitionSpec as P

F32 = jnp.float32
BF16 = jnp.bfloat16
F16 = jnp.float16
VMEM = 56 * 1024 * 1024


def passed_along(block, axis, distance):
    devices = range(lax.axis_size(axis))
    route = [(i - distance, i) for i in devices if i - distance in devices]
    return lax.ppermute(block, axis, route)


def swapped(block):
    return lax.ppermute(block, "clip", [(i, i ^ 1) for i in range(lax.axis_size("clip"))])


def piece_rows(rows):
    return rows // lax.axis_size("tm") // 16 * 16 + 16


def padded(rows):
    return piece_rows(rows) * lax.axis_size("tm") + 16


def shifted(x, row_off, col_off, rows, cols):
    lanes = x.shape[1]
    lane = lax.broadcasted_iota(jnp.int32, (1, lanes), 1)
    row = (lane // cols) % rows + row_off
    col = lane % cols + col_off
    good = (row >= 0) & (row < rows) & (col >= 0) & (col < cols)
    shift = row_off * cols + col_off
    return jnp.where(good, pltpu.roll(x, (lanes - shift) % lanes, axis=1), 0.0)


def contract(left, right, dims):
    return lax.dot_general(left, right, (dims, ((), ())), preferred_element_type=F32)


def fill_columns(out_ref, x, rows, cols):
    cells, chans = x.shape
    frames = cells // (rows * cols)
    zero = jnp.zeros((frames, cols, chans), BF16)
    place = lax.broadcasted_iota(jnp.int32, (cells, 1), 0) % cols
    for c in range(3):
        moved = x
        if c != 1:
            good = (place + c - 1 >= 0) & (place + c - 1 < cols)
            moved = jnp.where(good, pltpu.roll(x, (1 - c) % cells, axis=0), 0.0)
        out_ref[c, :, 0] = zero
        out_ref[c, :, rows + 1] = zero
        out_ref[c, :, 1 : rows + 1] = moved.astype(BF16).reshape(frames, rows, cols, chans)


def window(ref, column, frame, row, frames, rows):
    x = ref[column, pl.ds(frame, frames), pl.ds(row, rows)]
    return x.reshape(frames * rows * x.shape[2], x.shape[3])


def front_kernel(crop_ref, w_ref, *refs, rows, cols, first):
    if first:
        patch_ref, z_ref, cells_ref, taps_ref, top_ref, full_ref = refs
    else:
        taps_ref, top_ref, full_ref = refs
    plane = rows * cols
    lat = crop_ref.shape[0]
    ext = full_ref.shape[1]
    count = ext - 2 * plane

    @pl.when(pl.program_id(0) == 0)
    def _():
        crop = crop_ref[...].astype(F32)
        for spot in range(9):
            moved = shifted(crop, spot // 3 - 1, spot % 3 - 1, rows, cols).astype(BF16)
            for depth in range(3):
                at = (depth * 9 + spot) * lat
                full_ref[at : at + lat, :] = moved[:, depth * plane : depth * plane + ext]
        if first:
            patch_ref[...] = full_ref[:, 2 * plane :]

    z = contract(w_ref[...], full_ref[...], ((0,), (0,)))
    act = (z * (1.0 / (1.0 + jnp.exp(-z)))).astype(BF16).astype(F32)
    top_ref[...] = jnp.broadcast_to(jnp.max(jnp.abs(act), axis=1, keepdims=True), top_ref.shape)
    for spot in range(9):
        moved = shifted(act, spot // 3 - 1, spot % 3 - 1, rows, cols).astype(BF16)
        for depth in range(3):
            taps_ref[depth * 9 + spot] = moved[:, depth * plane : depth * plane + count]
    if first:
        z_ref[...] = z[:, 2 * plane :].T
        fill_columns(cells_ref, act.T, rows, cols)


def front(crop_t, w_in, rows, cols, count, first):
    chans = w_in.shape[1]
    depth_in = w_in.shape[0]
    plane = rows * cols
    block = 128
    frames = count // plane + 2
    specs = [
        pl.BlockSpec((27, block, count), lambda i: (0, i, 0)),
        pl.BlockSpec((block, 128), lambda i: (i, 0)),
    ]
    shapes = [
        jax.ShapeDtypeStruct((27, chans, count), BF16),
        jax.ShapeDtypeStruct((chans, 128), F32),
    ]
    if first:
        specs = [
            pl.BlockSpec((depth_in, count), lambda i: (0, 0)),
            pl.BlockSpec((count, block), lambda i: (0, i)),
            pl.BlockSpec((3, frames, rows + 2, cols, block), lambda i: (0, 0, 0, 0, i)),
        ] + specs
        shapes = [
            jax.ShapeDtypeStruct((depth_in, count), BF16),
            jax.ShapeDtypeStruct((count, chans), F32),
            jax.ShapeDtypeStruct((3, frames, rows + 2, cols, chans), BF16),
        ] + shapes
    return pl.pallas_call(
        lambda *refs: front_kernel(*refs, rows=rows, cols=cols, first=first),
        grid=(chans // block,),
        in_specs=[
            pl.BlockSpec(crop_t.shape, lambda i: (0, 0)),
            pl.BlockSpec((depth_in, block), lambda i: (0, i)),
        ],
        out_specs=specs,
        out_shape=shapes,
        scratch_shapes=[pltpu.VMEM((depth_in, count + 2 * plane), BF16)],
        compiler_params=pltpu.CompilerParams(vmem_limit_bytes=VMEM),
        name="front",
    )(crop_t, w_in)


def middle_kernel(cells_ref, w_ref, teacher_ref, g_ref, head_ref, acc_ref, *, scale):
    depth = pl.program_id(0)
    frames = cells_ref.shape[1] - 2
    rows = cells_ref.shape[2] - 2
    chans = w_ref.shape[2]
    left = jnp.concatenate(
        [window(cells_ref, k % 3, depth, k // 3, frames, rows) for k in range(9)], axis=1
    )
    total = contract(left, w_ref[...].reshape(9 * chans, chans), ((1,), (0,)))

    @pl.when(depth == 0)
    def _():
        acc_ref[...] = total

    @pl.when(depth == 1)
    def _():
        acc_ref[...] += total

    @pl.when(depth == 2)
    def _():
        g = ((acc_ref[...] + total - teacher_ref[...].astype(F32)) * scale).astype(BF16)
        count = g.shape[0]
        g_ref[:count, :] = g
        head_ref[...] = g[: head_ref.shape[0]]
        size = jnp.max(jnp.sum(jnp.abs(g.astype(F32)), axis=0, keepdims=True), axis=1, keepdims=True)
        g_ref[count:, :] = jnp.broadcast_to(size, (g_ref.shape[0] - count, g.shape[1])).astype(BF16)


def middle(cells, w_taps, teacher, scale, head):
    count, chans = teacher.shape
    return pl.pallas_call(
        lambda *refs: middle_kernel(*refs, scale=scale),
        grid=(3,),
        in_specs=[
            pl.BlockSpec(cells.shape, lambda i: (0,) * 5),
            pl.BlockSpec((9, chans, chans), lambda i: (i, 0, 0)),
            pl.BlockSpec((count, chans), lambda i: (0, 0)),
        ],
        out_specs=[
            pl.BlockSpec((count + 16, chans), lambda i: (0, 0)),
            pl.BlockSpec((head, chans), lambda i: (0, 0)),
        ],
        out_shape=[
            jax.ShapeDtypeStruct((count + 16, chans), BF16),
            jax.ShapeDtypeStruct((head, chans), BF16),
        ],
        scratch_shapes=[pltpu.VMEM((count, chans), F32)],
        compiler_params=pltpu.CompilerParams(vmem_limit_bytes=VMEM),
        name="middle",
    )(cells, w_taps, teacher)


def grad_kernel(order_ref, *refs, units):
    own_ref, out_ref = refs[-2:]
    g_refs = refs[-4:-2]
    at_once = out_ref.shape[0]
    rows = refs[0].shape[0]
    spare = own_ref.shape[0] - units * rows
    zero = jnp.zeros((spare, own_ref.shape[1]), F32)
    for i in range(at_once):
        for k in range(units):
            at = 2 * (i * units + k)
            total = contract(refs[at][...], g_refs[0][...], ((1,), (0,)))
            total += contract(refs[at + 1][...], g_refs[1][...], ((1,), (0,)))
            out_ref[i, k * rows : (k + 1) * rows, :] = total
        out_ref[i, units * rows :, :] = zero

    @pl.when(pl.program_id(0) == 0)
    def _():
        own_ref[...] = out_ref[0]


def grad_chunk(order, taps, g, first, units):
    blocks = order.shape[0]
    total, count = taps[0].shape
    chans = g[0].shape[1]
    rows = total // (2 * blocks) // 3
    at_once = 2 // units
    tap_specs = []
    for i in range(at_once):
        for k in range(units):
            spec = pl.BlockSpec(
                (rows, count), lambda s, order, i=i, k=k: (order[s * at_once + i] * 3 + first + k, 0)
            )
            tap_specs += [spec, spec]
    whole = pl.BlockSpec((count, chans), lambda s, order: (0, 0))
    size = padded(rows * units)
    return pl.pallas_call(
        lambda *refs: grad_kernel(*refs, units=units),
        grid_spec=pltpu.PrefetchScalarGridSpec(
            num_scalar_prefetch=1,
            grid=(blocks // at_once,),
            in_specs=tap_specs + [whole, whole],
            out_specs=[
                pl.BlockSpec((size, chans), lambda s, order: (0, 0)),
                pl.BlockSpec((at_once, size, chans), lambda s, order: (s, 0, 0)),
            ],
        ),
        out_shape=[
            jax.ShapeDtypeStruct((size, chans), F32),
            jax.ShapeDtypeStruct((blocks, size, chans), F32),
        ],
        compiler_params=pltpu.CompilerParams(vmem_limit_bytes=VMEM),
        name="grad",
    )(order, *(list(taps) * 2), *g)


def back_kernel(g_ref, later_ref, w_ref, z_ref, patch_ref, out_ref, cells_ref, acc_ref, *, rows, cols):
    depth = pl.program_id(0)
    frames = cells_ref.shape[1] - 2

    @pl.when(depth == 0)
    def _():
        g = jnp.concatenate([g_ref[...], later_ref[...]], axis=0).astype(F32)
        fill_columns(cells_ref, g, rows, cols)

    left = jnp.concatenate(
        [window(cells_ref, 2 - k % 3, 2 - depth, 2 - k // 3, frames, rows) for k in range(9)], axis=1
    )
    right = jnp.concatenate([w_ref[k] for k in range(9)], axis=1)
    total = contract(left, right, ((1,), (1,)))

    @pl.when(depth == 0)
    def _():
        acc_ref[...] = total

    @pl.when(depth == 1)
    def _():
        acc_ref[...] += total

    @pl.when(depth == 2)
    def _():
        z = z_ref[...]
        sig = 1.0 / (1.0 + jnp.exp(-z))
        dz = ((acc_ref[...] + total) * sig * (1.0 + z * (1.0 - sig))).astype(BF16)
        out_ref[...] = contract(patch_ref[...], dz, ((1,), (0,)))


def back(g, later, w_taps, z, patch_t, rows, cols):
    count, chans = z.shape
    depth_in = patch_t.shape[0]
    frames = count // (rows * cols) + 2
    return pl.pallas_call(
        lambda *refs: back_kernel(*refs, rows=rows, cols=cols),
        grid=(3,),
        in_specs=[
            pl.BlockSpec((count, chans), lambda i: (0, 0)),
            pl.BlockSpec(later.shape, lambda i: (0, 0)),
            pl.BlockSpec((9, chans, chans), lambda i: (i, 0, 0)),
            pl.BlockSpec((count, chans), lambda i: (0, 0)),
            pl.BlockSpec((depth_in, count), lambda i: (0, 0)),
        ],
        out_specs=pl.BlockSpec((depth_in, chans), lambda i: (0, 0)),
        out_shape=jax.ShapeDtypeStruct((depth_in, chans), F32),
        scratch_shapes=[
            pltpu.VMEM((3, frames, rows + 2, cols, chans), BF16),
            pltpu.VMEM((count, chans), F32),
        ],
        compiler_params=pltpu.CompilerParams(vmem_limit_bytes=VMEM),
        name="back",
    )(g, later, w_taps, z, patch_t)


def packed(x, rows, bound):
    power = jnp.ceil(jnp.log2(jnp.maximum(bound, 1e-30)))
    row = lax.broadcasted_iota(jnp.int32, x.shape, x.ndim - 2)
    return jnp.where(row < rows, x * jnp.exp2(14.0 - power), power).astype(F16)


def across_plane(part, rows, bound, after):
    clips = lax.axis_size("clip")
    payloads = [packed(part[q], rows, bound) for q in range(1, clips // 2)]
    payloads, after = lax.optimization_barrier((payloads, after))
    got = []
    for q in range(1, clips // 2):
        route = [(i, i ^ (2 * q)) for i in range(clips)]
        got.append(lax.ppermute(payloads[q - 1], "clip", route))
    return got, after


def behind(x, *first):
    return lax.optimization_barrier((x, first))[0]


def around(blocks, distance):
    depth = lax.axis_size("tm")
    return lax.ppermute(blocks, "tm", [(i, (i + distance) % depth) for i in range(depth)])


def scales(got, rows, bound):
    powers = [jnp.exp2(x[rows : rows + 1].astype(F32)) for x in got]
    return [power * 2.0**-14 for power in powers], (bound + sum(powers)) * 1.01


def across_depth(own, got, rows, factors, total, after):
    depth = lax.axis_size("tm")
    me = lax.axis_index("tm")
    small = piece_rows(rows)

    def piece(place):
        cut = lambda x: lax.dynamic_slice_in_dim(x, place * small, small + 16, axis=0)
        terms = [cut(x).astype(F32) * factor for x, factor in zip(got, factors)]
        return sum(terms) if own is None else cut(own) + sum(terms)

    payloads = [packed(piece((me + d) % depth), small, total) for d in range(1, depth)]
    after = behind(after, payloads)
    others = [around(payloads[d - 1], d) for d in range(1, depth)]
    return (piece(me), others), after


def spread(parts, smalls, factors, total):
    depth = lax.axis_size("tm")
    sums = []
    for (own, got), small in zip(parts, smalls):
        terms = [x[:small].astype(F32) * factor for x, factor in zip(got, factors)]
        sums.append(own[:small] + sum(terms))
    rows = sum(smalls)
    payload = packed(jnp.pad(jnp.concatenate(sums, axis=0), ((0, 16), (0, 0))), rows, total)
    return [payload] + [around(payload, depth - k) for k in range(1, depth)]


def assembled(pieces, factors, smalls, rows):
    depth = lax.axis_size("tm")
    me = lax.axis_index("tm")
    pieces = [x.astype(F32) * factor for x, factor in zip(pieces, factors)]
    placed = []
    for place in range(depth):
        x = pieces[0]
        for k in range(1, depth):
            x = jnp.where((me + k) % depth == place, pieces[k], x)
        placed.append(x)
    out = []
    at = 0
    for small, count in zip(smalls, rows):
        for place in range(depth):
            left = min(small, count - place * small)
            if left > 0:
                out.append(placed[place][at : at + left])
        at += small
    return out


def shards(latent, offsets, teacher, w_in, w_mid):
    frames = teacher.shape[1]
    rows = teacher.shape[2]
    cols = teacher.shape[3]
    chans = teacher.shape[4]
    plane = rows * cols
    count = frames * plane
    lat_chans = latent.shape[4]
    clips = lax.axis_size("clip")
    total_cells = clips * lax.axis_size("tm") * count
    scale = 2.0 / math.sqrt(total_cells)
    w_full = lax.all_gather(w_mid, "clip", axis=0, tiled=True)
    crop = lax.dynamic_slice_in_dim(latent[0], offsets[0], cols, axis=2).reshape(count, lat_chans).T
    earlier = passed_along(crop[:, count - 4 * plane :], "tm", 1)
    crop_ext = jnp.concatenate([earlier, crop], axis=1)
    patch_t, z, cells, taps, top = front(crop_ext, w_in, rows, cols, count, True)
    pair_taps, pair_top = front(swapped(crop_ext), w_in, rows, cols, count, False)
    taps = taps.reshape(27 * chans, count)
    pair_taps = pair_taps.reshape(27 * chans, count)
    top, pair_top = jnp.max(top), jnp.max(pair_top)
    w_full, pair_taps, top, pair_top = lax.optimization_barrier((w_full, pair_taps, top, pair_top))
    w_taps = w_full.reshape(27, chans, chans)
    g, head = middle(cells, w_taps, teacher[0].reshape(count, chans), scale, 2 * plane)
    pair_g = swapped(g)
    later = passed_along(head, "tm", -1)

    third = 27 * chans // clips // 3
    spare = slice(count, count + 1)
    bound = (top * g[spare, :1].astype(F32) + pair_top * pair_g[spare, :1].astype(F32)) * 1.03
    both = (taps, pair_taps)
    in_rows = patch_t.shape[0]

    me = lax.axis_index("clip")
    chips = jnp.arange(clips // 2, dtype=jnp.int32)
    own_a, part = grad_chunk(me ^ (2 * chips), both, (g, pair_g), 0, 2)
    part, later = lax.optimization_barrier((part, later))
    got_a, g = across_plane(part, 2 * third, bound, g)
    _, part = grad_chunk(2 * chips + me % 2, both, (g, pair_g), 2, 1)
    payload = packed(part, third, bound)
    payload, g = lax.optimization_barrier((payload, g))
    groups = [[2 * p + core for p in range(clips // 2)] for core in range(2)]
    got_b = lax.all_to_all(payload, "clip", 0, 0, axis_index_groups=groups, tiled=True)
    got_b = [got_b[p] for p in range(clips // 2)]
    in_part = back(g, later, w_taps, z, patch_t, rows, cols)

    got_a = behind(got_a, in_part)
    factors, total = scales(got_a, 2 * third, bound)
    (own_a, depth_a), got_b = across_depth(own_a, got_a, 2 * third, factors, total, got_b)
    factors, _ = scales(got_b, third, 0.0)
    (own_b, depth_b), in_part = across_depth(None, got_b, third, factors, total, in_part)
    in_got = lax.all_to_all(in_part.reshape(clips, in_rows // clips, chans), "clip", 0, 0, tiled=True)
    z_total = total
    smalls = [piece_rows(2 * third), piece_rows(third)]
    factors, total = scales(depth_a, smalls[0], z_total)
    in_sum = behind(in_got, depth_a).sum(axis=0)
    in_sum = jnp.broadcast_to(in_sum[None], (lax.axis_size("tm"),) + in_sum.shape)
    depth_b = behind(depth_b, in_sum)
    in_got = lax.all_to_all(in_sum, "tm", 0, 0, tiled=True)
    last = spread([(own_a, depth_a), (own_b, depth_b)], smalls, factors, total)
    in_sum = behind(in_got, last[0]).sum(axis=0)
    in_sum = jnp.broadcast_to(in_sum[None], (clips,) + in_sum.shape)
    last[-1] = behind(last[-1], in_sum)
    grad_in = lax.all_to_all(in_sum, "clip", 0, 0, tiled=True).reshape(in_rows, chans)
    factors, _ = scales(last, sum(smalls), 0.0)
    pieces = assembled(last, factors, smalls, [2 * third, third])
    return (jnp.concatenate(pieces, axis=0), grad_in)


def solution(mesh):
    return jax.shard_map(
        shards,
        mesh=mesh,
        in_specs=(
            P("clip", "tm", None, None, None),
            P("clip"),
            P("clip", "tm", None, None, None),
            P(),
            P("clip", None),
        ),
        out_specs=(P("clip", None), P()),
        check_vma=False,
    )
```

```python
import math

import jax
import jax.numpy as jnp
from jax import lax
from jax.experimental import pallas as pl
from jax.experimental.pallas import tpu as pltpu
from jax.sharding import PartitionSpec as P

F32 = jnp.float32
BF16 = jnp.bfloat16
F16 = jnp.float16
VMEM = 56 * 1024 * 1024


def passed_along(block, axis, distance):
    devices = range(lax.axis_size(axis))
    route = [(i - distance, i) for i in devices if i - distance in devices]
    return lax.ppermute(block, axis, route)


def swapped(block):
    return lax.ppermute(block, "clip", [(i, i ^ 1) for i in range(lax.axis_size("clip"))])


def piece_rows(rows):
    return rows // lax.axis_size("tm") // 16 * 16 + 16


def padded(rows):
    return piece_rows(rows) * lax.axis_size("tm") + 16


def shifted(x, row_off, col_off, rows, cols):
    lanes = x.shape[1]
    lane = lax.broadcasted_iota(jnp.int32, (1, lanes), 1)
    row = (lane // cols) % rows + row_off
    col = lane % cols + col_off
    good = (row >= 0) & (row < rows) & (col >= 0) & (col < cols)
    shift = row_off * cols + col_off
    return jnp.where(good, pltpu.roll(x, (lanes - shift) % lanes, axis=1), 0.0)


def contract(left, right, dims):
    return lax.dot_general(left, right, (dims, ((), ())), preferred_element_type=F32)


def fill_columns(out_ref, x, rows, cols):
    cells, chans = x.shape
    frames = cells // (rows * cols)
    zero = jnp.zeros((frames, cols, chans), BF16)
    place = lax.broadcasted_iota(jnp.int32, (cells, 1), 0) % cols
    for c in range(3):
        moved = x
        if c != 1:
            good = (place + c - 1 >= 0) & (place + c - 1 < cols)
            moved = jnp.where(good, pltpu.roll(x, (1 - c) % cells, axis=0), 0.0)
        out_ref[c, :, 0] = zero
        out_ref[c, :, rows + 1] = zero
        out_ref[c, :, 1 : rows + 1] = moved.astype(BF16).reshape(frames, rows, cols, chans)


def window(ref, column, frame, row, frames, rows):
    x = ref[column, pl.ds(frame, frames), pl.ds(row, rows)]
    return x.reshape(frames * rows * x.shape[2], x.shape[3])


def front_kernel(crop_ref, w_ref, *refs, rows, cols, first):
    if first:
        patch_ref, z_ref, cells_ref, taps_ref, top_ref, full_ref = refs
    else:
        taps_ref, top_ref, full_ref = refs
    plane = rows * cols
    lat = crop_ref.shape[0]
    ext = full_ref.shape[1]
    count = ext - 2 * plane

    @pl.when(pl.program_id(0) == 0)
    def _():
        crop = crop_ref[...].astype(F32)
        for spot in range(9):
            moved = shifted(crop, spot // 3 - 1, spot % 3 - 1, rows, cols).astype(BF16)
            for depth in range(3):
                at = (depth * 9 + spot) * lat
                full_ref[at : at + lat, :] = moved[:, depth * plane : depth * plane + ext]
        if first:
            patch_ref[...] = full_ref[:, 2 * plane :]

    z = contract(w_ref[...], full_ref[...], ((0,), (0,)))
    act = (z * (1.0 / (1.0 + jnp.exp(-z)))).astype(BF16).astype(F32)
    top_ref[...] = jnp.broadcast_to(jnp.max(jnp.abs(act), axis=1, keepdims=True), top_ref.shape)
    for spot in range(9):
        moved = shifted(act, spot // 3 - 1, spot % 3 - 1, rows, cols).astype(BF16)
        for depth in range(3):
            taps_ref[depth * 9 + spot] = moved[:, depth * plane : depth * plane + count]
    if first:
        z_ref[...] = z[:, 2 * plane :].T
        fill_columns(cells_ref, act.T, rows, cols)


def front(crop_t, w_in, rows, cols, count, first):
    chans = w_in.shape[1]
    depth_in = w_in.shape[0]
    plane = rows * cols
    block = 128
    frames = count // plane + 2
    specs = [
        pl.BlockSpec((27, block, count), lambda i: (0, i, 0)),
        pl.BlockSpec((block, 128), lambda i: (i, 0)),
    ]
    shapes = [
        jax.ShapeDtypeStruct((27, chans, count), BF16),
        jax.ShapeDtypeStruct((chans, 128), F32),
    ]
    if first:
        specs = [
            pl.BlockSpec((depth_in, count), lambda i: (0, 0)),
            pl.BlockSpec((count, block), lambda i: (0, i)),
            pl.BlockSpec((3, frames, rows + 2, cols, block), lambda i: (0, 0, 0, 0, i)),
        ] + specs
        shapes = [
            jax.ShapeDtypeStruct((depth_in, count), BF16),
            jax.ShapeDtypeStruct((count, chans), F32),
            jax.ShapeDtypeStruct((3, frames, rows + 2, cols, chans), BF16),
        ] + shapes
    return pl.pallas_call(
        lambda *refs: front_kernel(*refs, rows=rows, cols=cols, first=first),
        grid=(chans // block,),
        in_specs=[
            pl.BlockSpec(crop_t.shape, lambda i: (0, 0)),
            pl.BlockSpec((depth_in, block), lambda i: (0, i)),
        ],
        out_specs=specs,
        out_shape=shapes,
        scratch_shapes=[pltpu.VMEM((depth_in, count + 2 * plane), BF16)],
        compiler_params=pltpu.CompilerParams(vmem_limit_bytes=VMEM),
        name="front",
    )(crop_t, w_in)


def middle_kernel(cells_ref, w_ref, teacher_ref, g_ref, head_ref, acc_ref, *, scale):
    depth = pl.program_id(0)
    frames = cells_ref.shape[1] - 2
    rows = cells_ref.shape[2] - 2
    chans = w_ref.shape[2]
    left = jnp.concatenate(
        [window(cells_ref, k % 3, depth, k // 3, frames, rows) for k in range(9)], axis=1
    )
    total = contract(left, w_ref[...].reshape(9 * chans, chans), ((1,), (0,)))

    @pl.when(depth == 0)
    def _():
        acc_ref[...] = total

    @pl.when(depth == 1)
    def _():
        acc_ref[...] += total

    @pl.when(depth == 2)
    def _():
        g = ((acc_ref[...] + total - teacher_ref[...].astype(F32)) * scale).astype(BF16)
        count = g.shape[0]
        g_ref[:count, :] = g
        head_ref[...] = g[: head_ref.shape[0]]
        size = jnp.max(jnp.sum(jnp.abs(g.astype(F32)), axis=0, keepdims=True), axis=1, keepdims=True)
        g_ref[count:, :] = jnp.broadcast_to(size, (g_ref.shape[0] - count, g.shape[1])).astype(BF16)


def middle(cells, w_taps, teacher, scale, head):
    count, chans = teacher.shape
    return pl.pallas_call(
        lambda *refs: middle_kernel(*refs, scale=scale),
        grid=(3,),
        in_specs=[
            pl.BlockSpec(cells.shape, lambda i: (0,) * 5),
            pl.BlockSpec((9, chans, chans), lambda i: (i, 0, 0)),
            pl.BlockSpec((count, chans), lambda i: (0, 0)),
        ],
        out_specs=[
            pl.BlockSpec((count + 16, chans), lambda i: (0, 0)),
            pl.BlockSpec((head, chans), lambda i: (0, 0)),
        ],
        out_shape=[
            jax.ShapeDtypeStruct((count + 16, chans), BF16),
            jax.ShapeDtypeStruct((head, chans), BF16),
        ],
        scratch_shapes=[pltpu.VMEM((count, chans), F32)],
        compiler_params=pltpu.CompilerParams(vmem_limit_bytes=VMEM),
        name="middle",
    )(cells, w_taps, teacher)


def grad_kernel(order_ref, *refs, units):
    own_ref, out_ref = refs[-2:]
    g_refs = refs[-4:-2]
    at_once = out_ref.shape[0]
    rows = refs[0].shape[0]
    spare = own_ref.shape[0] - units * rows
    zero = jnp.zeros((spare, own_ref.shape[1]), F32)
    for i in range(at_once):
        for k in range(units):
            at = 2 * (i * units + k)
            total = contract(refs[at][...], g_refs[0][...], ((1,), (0,)))
            total += contract(refs[at + 1][...], g_refs[1][...], ((1,), (0,)))
            out_ref[i, k * rows : (k + 1) * rows, :] = total
        out_ref[i, units * rows :, :] = zero

    @pl.when(pl.program_id(0) == 0)
    def _():
        own_ref[...] = out_ref[0]


def grad_chunk(order, taps, g, first, units):
    blocks = order.shape[0]
    total, count = taps[0].shape
    chans = g[0].shape[1]
    rows = total // (2 * blocks) // 3
    at_once = 2 // units
    tap_specs = []
    for i in range(at_once):
        for k in range(units):
            spec = pl.BlockSpec(
                (rows, count), lambda s, order, i=i, k=k: (order[s * at_once + i] * 3 + first + k, 0)
            )
            tap_specs += [spec, spec]
    whole = pl.BlockSpec((count, chans), lambda s, order: (0, 0))
    size = padded(rows * units)
    return pl.pallas_call(
        lambda *refs: grad_kernel(*refs, units=units),
        grid_spec=pltpu.PrefetchScalarGridSpec(
            num_scalar_prefetch=1,
            grid=(blocks // at_once,),
            in_specs=tap_specs + [whole, whole],
            out_specs=[
                pl.BlockSpec((size, chans), lambda s, order: (0, 0)),
                pl.BlockSpec((at_once, size, chans), lambda s, order: (s, 0, 0)),
            ],
        ),
        out_shape=[
            jax.ShapeDtypeStruct((size, chans), F32),
            jax.ShapeDtypeStruct((blocks, size, chans), F32),
        ],
        compiler_params=pltpu.CompilerParams(vmem_limit_bytes=VMEM),
        name="grad",
    )(order, *(list(taps) * 2), *g)


def back_kernel(g_ref, later_ref, w_ref, z_ref, patch_ref, out_ref, cells_ref, acc_ref, *, rows, cols):
    depth = pl.program_id(0)
    frames = cells_ref.shape[1] - 2

    @pl.when(depth == 0)
    def _():
        g = jnp.concatenate([g_ref[...], later_ref[...]], axis=0).astype(F32)
        fill_columns(cells_ref, g, rows, cols)

    left = jnp.concatenate(
        [window(cells_ref, 2 - k % 3, 2 - depth, 2 - k // 3, frames, rows) for k in range(9)], axis=1
    )
    right = jnp.concatenate([w_ref[k] for k in range(9)], axis=1)
    total = contract(left, right, ((1,), (1,)))

    @pl.when(depth == 0)
    def _():
        acc_ref[...] = total

    @pl.when(depth == 1)
    def _():
        acc_ref[...] += total

    @pl.when(depth == 2)
    def _():
        z = z_ref[...]
        sig = 1.0 / (1.0 + jnp.exp(-z))
        dz = ((acc_ref[...] + total) * sig * (1.0 + z * (1.0 - sig))).astype(BF16)
        out_ref[...] = contract(patch_ref[...], dz, ((1,), (0,)))


def back(g, later, w_taps, z, patch_t, rows, cols):
    count, chans = z.shape
    depth_in = patch_t.shape[0]
    frames = count // (rows * cols) + 2
    return pl.pallas_call(
        lambda *refs: back_kernel(*refs, rows=rows, cols=cols),
        grid=(3,),
        in_specs=[
            pl.BlockSpec((count, chans), lambda i: (0, 0)),
            pl.BlockSpec(later.shape, lambda i: (0, 0)),
            pl.BlockSpec((9, chans, chans), lambda i: (i, 0, 0)),
            pl.BlockSpec((count, chans), lambda i: (0, 0)),
            pl.BlockSpec((depth_in, count), lambda i: (0, 0)),
        ],
        out_specs=pl.BlockSpec((depth_in, chans), lambda i: (0, 0)),
        out_shape=jax.ShapeDtypeStruct((depth_in, chans), F32),
        scratch_shapes=[
            pltpu.VMEM((3, frames, rows + 2, cols, chans), BF16),
            pltpu.VMEM((count, chans), F32),
        ],
        compiler_params=pltpu.CompilerParams(vmem_limit_bytes=VMEM),
        name="back",
    )(g, later, w_taps, z, patch_t)


def packed(x, rows, bound):
    power = jnp.ceil(jnp.log2(jnp.maximum(bound, 1e-30)))
    row = lax.broadcasted_iota(jnp.int32, x.shape, x.ndim - 2)
    return jnp.where(row < rows, x * jnp.exp2(14.0 - power), power).astype(F16)


def across_plane(part, rows, bound, after):
    clips = lax.axis_size("clip")
    payloads = [packed(part[q], rows, bound) for q in range(1, clips // 2)]
    payloads, after = lax.optimization_barrier((payloads, after))
    got = []
    for q in range(1, clips // 2):
        route = [(i, i ^ (2 * q)) for i in range(clips)]
        got.append(lax.ppermute(payloads[q - 1], "clip", route))
    return got, after


def behind(x, *first):
    return lax.optimization_barrier((x, first))[0]


def around(blocks, distance):
    depth = lax.axis_size("tm")
    return lax.ppermute(blocks, "tm", [(i, (i + distance) % depth) for i in range(depth)])


def scales(got, rows, bound):
    powers = [jnp.exp2(x[rows : rows + 1].astype(F32)) for x in got]
    return [power * 2.0**-14 for power in powers], (bound + sum(powers)) * 1.01


def across_depth(own, got, rows, factors, total, after):
    depth = lax.axis_size("tm")
    me = lax.axis_index("tm")
    small = piece_rows(rows)

    def piece(place):
        cut = lambda x: lax.dynamic_slice_in_dim(x, place * small, small + 16, axis=0)
        terms = [cut(x).astype(F32) * factor for x, factor in zip(got, factors)]
        return sum(terms) if own is None else cut(own) + sum(terms)

    payloads = [packed(piece((me + d) % depth), small, total) for d in range(1, depth)]
    after = behind(after, payloads)
    others = [around(payloads[d - 1], d) for d in range(1, depth)]
    return (piece(me), others), after


def spread(parts, smalls, factors, total):
    depth = lax.axis_size("tm")
    sums = []
    for (own, got), small in zip(parts, smalls):
        terms = [x[:small].astype(F32) * factor for x, factor in zip(got, factors)]
        sums.append(own[:small] + sum(terms))
    rows = sum(smalls)
    payload = packed(jnp.pad(jnp.concatenate(sums, axis=0), ((0, 16), (0, 0))), rows, total)
    return [payload] + [around(payload, depth - k) for k in range(1, depth)]


def assembled(pieces, factors, smalls, rows):
    depth = lax.axis_size("tm")
    me = lax.axis_index("tm")
    pieces = [x.astype(F32) * factor for x, factor in zip(pieces, factors)]
    placed = []
    for place in range(depth):
        x = pieces[0]
        for k in range(1, depth):
            x = jnp.where((me + k) % depth == place, pieces[k], x)
        placed.append(x)
    out = []
    at = 0
    for small, count in zip(smalls, rows):
        for place in range(depth):
            left = min(small, count - place * small)
            if left > 0:
                out.append(placed[place][at : at + left])
        at += small
    return out


def shards(latent, offsets, teacher, w_in, w_mid):
    frames = teacher.shape[1]
    rows = teacher.shape[2]
    cols = teacher.shape[3]
    chans = teacher.shape[4]
    plane = rows * cols
    count = frames * plane
    lat_chans = latent.shape[4]
    clips = lax.axis_size("clip")
    total_cells = clips * lax.axis_size("tm") * count
    scale = 2.0 / math.sqrt(total_cells)
    w_full = lax.all_gather(w_mid, "clip", axis=0, tiled=True)
    crop = lax.dynamic_slice_in_dim(latent[0], offsets[0], cols, axis=2).reshape(count, lat_chans).T
    earlier = passed_along(crop[:, count - 4 * plane :], "tm", 1)
    crop_ext = jnp.concatenate([earlier, crop], axis=1)
    patch_t, z, cells, taps, top = front(crop_ext, w_in, rows, cols, count, True)
    pair_taps, pair_top = front(swapped(crop_ext), w_in, rows, cols, count, False)
    taps = taps.reshape(27 * chans, count)
    pair_taps = pair_taps.reshape(27 * chans, count)
    top, pair_top = jnp.max(top), jnp.max(pair_top)
    w_full, pair_taps, top, pair_top = lax.optimization_barrier((w_full, pair_taps, top, pair_top))
    w_taps = w_full.reshape(27, chans, chans)
    g, head = middle(cells, w_taps, teacher[0].reshape(count, chans), scale, 2 * plane)
    pair_g = swapped(g)
    later = passed_along(head, "tm", -1)

    third = 27 * chans // clips // 3
    spare = slice(count, count + 1)
    bound = (top * g[spare, :1].astype(F32) + pair_top * pair_g[spare, :1].astype(F32)) * 1.03
    both = (taps, pair_taps)
    in_rows = patch_t.shape[0]

    me = lax.axis_index("clip")
    chips = jnp.arange(clips // 2, dtype=jnp.int32)
    own_a, part = grad_chunk(me ^ (2 * chips), both, (g, pair_g), 0, 2)
    part, later = lax.optimization_barrier((part, later))
    got_a, g = across_plane(part, 2 * third, bound, g)
    _, part = grad_chunk(2 * chips + me % 2, both, (g, pair_g), 2, 1)
    payload = packed(part, third, bound)
    payload, g = lax.optimization_barrier((payload, g))
    groups = [[2 * p + core for p in range(clips // 2)] for core in range(2)]
    got_b = lax.all_to_all(payload, "clip", 0, 0, axis_index_groups=groups, tiled=True)
    got_b = [got_b[p] for p in range(clips // 2)]
    in_part = back(g, later, w_taps, z, patch_t, rows, cols)

    got_a = behind(got_a, in_part)
    factors, total = scales(got_a, 2 * third, bound)
    (own_a, depth_a), got_b = across_depth(own_a, got_a, 2 * third, factors, total, got_b)
    factors, _ = scales(got_b, third, 0.0)
    (own_b, depth_b), in_part = across_depth(None, got_b, third, factors, total, in_part)
    in_got = lax.all_to_all(in_part.reshape(clips, in_rows // clips, chans), "clip", 0, 0, tiled=True)
    z_total = total
    smalls = [piece_rows(2 * third), piece_rows(third)]
    factors, total = scales(depth_a, smalls[0], z_total)
    in_sum = behind(in_got, depth_a).sum(axis=0)
    in_sum = jnp.broadcast_to(in_sum[None], (lax.axis_size("tm"),) + in_sum.shape)
    depth_b = behind(depth_b, in_sum)
    in_got = lax.all_to_all(in_sum, "tm", 0, 0, tiled=True)
    last = spread([(own_a, depth_a), (own_b, depth_b)], smalls, factors, total)
    in_sum = behind(in_got, last[0]).sum(axis=0)
    in_sum = jnp.broadcast_to(in_sum[None], (clips,) + in_sum.shape)
    last[1:] = behind(last[1:], in_sum)
    grad_in = lax.all_to_all(in_sum, "clip", 0, 0, tiled=True).reshape(in_rows, chans)
    factors, _ = scales(last, sum(smalls), 0.0)
    pieces = assembled(last, factors, smalls, [2 * third, third])
    return (jnp.concatenate(pieces, axis=0), grad_in)


def solution(mesh):
    return jax.shard_map(
        shards,
        mesh=mesh,
        in_specs=(
            P("clip", "tm", None, None, None),
            P("clip"),
            P("clip", "tm", None, None, None),
            P(),
            P("clip", None),
        ),
        out_specs=(P("clip", None), P()),
        check_vma=False,
    )
```

```python
import math

import jax
import jax.numpy as jnp
from jax import lax
from jax.experimental import pallas as pl
from jax.experimental.pallas import tpu as pltpu
from jax.sharding import PartitionSpec as P

F32 = jnp.float32
BF16 = jnp.bfloat16
F16 = jnp.float16
VMEM = 56 * 1024 * 1024


def passed_along(block, axis, distance):
    devices = range(lax.axis_size(axis))
    route = [(i - distance, i) for i in devices if i - distance in devices]
    return lax.ppermute(block, axis, route)


def swapped(block):
    return lax.ppermute(block, "clip", [(i, i ^ 1) for i in range(lax.axis_size("clip"))])


def piece_rows(rows):
    return rows // lax.axis_size("tm") // 16 * 16 + 16


def padded(rows):
    return piece_rows(rows) * lax.axis_size("tm") + 16


def shifted(x, row_off, col_off, rows, cols):
    lanes = x.shape[1]
    lane = lax.broadcasted_iota(jnp.int32, (1, lanes), 1)
    row = (lane // cols) % rows + row_off
    col = lane % cols + col_off
    good = (row >= 0) & (row < rows) & (col >= 0) & (col < cols)
    shift = row_off * cols + col_off
    return jnp.where(good, pltpu.roll(x, (lanes - shift) % lanes, axis=1), 0.0)


def contract(left, right, dims):
    return lax.dot_general(left, right, (dims, ((), ())), preferred_element_type=F32)


def fill_columns(out_ref, x, rows, cols):
    cells, chans = x.shape
    frames = cells // (rows * cols)
    zero = jnp.zeros((frames, cols, chans), BF16)
    place = lax.broadcasted_iota(jnp.int32, (cells, 1), 0) % cols
    for c in range(3):
        moved = x
        if c != 1:
            good = (place + c - 1 >= 0) & (place + c - 1 < cols)
            moved = jnp.where(good, pltpu.roll(x, (1 - c) % cells, axis=0), 0.0)
        out_ref[c, :, 0] = zero
        out_ref[c, :, rows + 1] = zero
        out_ref[c, :, 1 : rows + 1] = moved.astype(BF16).reshape(frames, rows, cols, chans)


def window(ref, column, frame, row, frames, rows):
    x = ref[column, pl.ds(frame, frames), pl.ds(row, rows)]
    return x.reshape(frames * rows * x.shape[2], x.shape[3])


def front_kernel(crop_ref, w_ref, *refs, rows, cols, first):
    if first:
        patch_ref, z_ref, cells_ref, taps_ref, top_ref, full_ref = refs
    else:
        taps_ref, top_ref, full_ref = refs
    plane = rows * cols
    lat = crop_ref.shape[0]
    ext = full_ref.shape[1]
    count = ext - 2 * plane

    @pl.when(pl.program_id(0) == 0)
    def _():
        crop = crop_ref[...].astype(F32)
        for spot in range(9):
            moved = shifted(crop, spot // 3 - 1, spot % 3 - 1, rows, cols).astype(BF16)
            for depth in range(3):
                at = (depth * 9 + spot) * lat
                full_ref[at : at + lat, :] = moved[:, depth * plane : depth * plane + ext]
        if first:
            patch_ref[...] = full_ref[:, 2 * plane :]

    z = contract(w_ref[...], full_ref[...], ((0,), (0,)))
    act = (z * (1.0 / (1.0 + jnp.exp(-z)))).astype(BF16).astype(F32)
    top_ref[...] = jnp.broadcast_to(jnp.max(jnp.abs(act), axis=1, keepdims=True), top_ref.shape)
    for spot in range(9):
        moved = shifted(act, spot // 3 - 1, spot % 3 - 1, rows, cols).astype(BF16)
        for depth in range(3):
            taps_ref[depth * 9 + spot] = moved[:, depth * plane : depth * plane + count]
    if first:
        z_ref[...] = z[:, 2 * plane :].T
        fill_columns(cells_ref, act.T, rows, cols)


def front(crop_t, w_in, rows, cols, count, first):
    chans = w_in.shape[1]
    depth_in = w_in.shape[0]
    plane = rows * cols
    block = 128
    frames = count // plane + 2
    specs = [
        pl.BlockSpec((27, block, count), lambda i: (0, i, 0)),
        pl.BlockSpec((block, 128), lambda i: (i, 0)),
    ]
    shapes = [
        jax.ShapeDtypeStruct((27, chans, count), BF16),
        jax.ShapeDtypeStruct((chans, 128), F32),
    ]
    if first:
        specs = [
            pl.BlockSpec((depth_in, count), lambda i: (0, 0)),
            pl.BlockSpec((count, block), lambda i: (0, i)),
            pl.BlockSpec((3, frames, rows + 2, cols, block), lambda i: (0, 0, 0, 0, i)),
        ] + specs
        shapes = [
            jax.ShapeDtypeStruct((depth_in, count), BF16),
            jax.ShapeDtypeStruct((count, chans), F32),
            jax.ShapeDtypeStruct((3, frames, rows + 2, cols, chans), BF16),
        ] + shapes
    return pl.pallas_call(
        lambda *refs: front_kernel(*refs, rows=rows, cols=cols, first=first),
        grid=(chans // block,),
        in_specs=[
            pl.BlockSpec(crop_t.shape, lambda i: (0, 0)),
            pl.BlockSpec((depth_in, block), lambda i: (0, i)),
        ],
        out_specs=specs,
        out_shape=shapes,
        scratch_shapes=[pltpu.VMEM((depth_in, count + 2 * plane), BF16)],
        compiler_params=pltpu.CompilerParams(vmem_limit_bytes=VMEM),
        name="front",
    )(crop_t, w_in)


def middle_kernel(cells_ref, wide_ref, thin_ref, teacher_ref, g_ref, head_ref, acc_ref, *, scale):
    depth = pl.program_id(0)
    frames = cells_ref.shape[1] - 2
    rows = cells_ref.shape[2] - 2
    left = jnp.concatenate(
        [window(cells_ref, k % 3, depth, k // 3, frames, rows) for k in range(9)], axis=1
    )
    totals = []
    for ref in (wide_ref, thin_ref):
        totals.append(contract(left, ref[...].reshape(left.shape[1], ref.shape[2]), ((1,), (0,))))
    total = jnp.concatenate(totals, axis=1)

    @pl.when(depth == 0)
    def _():
        acc_ref[...] = total

    @pl.when(depth == 1)
    def _():
        acc_ref[...] += total

    @pl.when(depth == 2)
    def _():
        g = ((acc_ref[...] + total - teacher_ref[...].astype(F32)) * scale).astype(BF16)
        count = g.shape[0]
        g_ref[:count, :] = g
        head_ref[...] = g[: head_ref.shape[0]]
        size = jnp.max(jnp.sum(jnp.abs(g.astype(F32)), axis=0, keepdims=True), axis=1, keepdims=True)
        g_ref[count:, :] = jnp.broadcast_to(size, (g_ref.shape[0] - count, g.shape[1])).astype(BF16)


def middle(cells, wide, thin, teacher, scale, head):
    count, chans = teacher.shape
    return pl.pallas_call(
        lambda *refs: middle_kernel(*refs, scale=scale),
        grid=(3,),
        in_specs=[
            pl.BlockSpec(cells.shape, lambda i: (0,) * 5),
            pl.BlockSpec((9,) + wide.shape[1:], lambda i: (i, 0, 0)),
            pl.BlockSpec((9,) + thin.shape[1:], lambda i: (i, 0, 0)),
            pl.BlockSpec((count, chans), lambda i: (0, 0)),
        ],
        out_specs=[
            pl.BlockSpec((count + 16, chans), lambda i: (0, 0)),
            pl.BlockSpec((head, chans), lambda i: (0, 0)),
        ],
        out_shape=[
            jax.ShapeDtypeStruct((count + 16, chans), BF16),
            jax.ShapeDtypeStruct((head, chans), BF16),
        ],
        scratch_shapes=[pltpu.VMEM((count, chans), F32)],
        compiler_params=pltpu.CompilerParams(vmem_limit_bytes=VMEM),
        name="middle",
    )(cells, wide, thin, teacher)


def grad_kernel(order_ref, *refs, units):
    own_ref, out_ref = refs[-2:]
    g_refs = refs[-4:-2]
    at_once = out_ref.shape[0]
    rows = refs[0].shape[0]
    spare = own_ref.shape[0] - units * rows
    zero = jnp.zeros((spare, own_ref.shape[1]), F32)
    for i in range(at_once):
        for k in range(units):
            at = 2 * (i * units + k)
            total = contract(refs[at][...], g_refs[0][...], ((1,), (0,)))
            total += contract(refs[at + 1][...], g_refs[1][...], ((1,), (0,)))
            out_ref[i, k * rows : (k + 1) * rows, :] = total
        out_ref[i, units * rows :, :] = zero

    @pl.when(pl.program_id(0) == 0)
    def _():
        own_ref[...] = out_ref[0]


def grad_chunk(order, taps, g, first, units):
    blocks = order.shape[0]
    total, count = taps[0].shape
    chans = g[0].shape[1]
    rows = total // (2 * blocks) // 3
    at_once = 2 // units
    tap_specs = []
    for i in range(at_once):
        for k in range(units):
            spec = pl.BlockSpec(
                (rows, count), lambda s, order, i=i, k=k: (order[s * at_once + i] * 3 + first + k, 0)
            )
            tap_specs += [spec, spec]
    whole = pl.BlockSpec((count, chans), lambda s, order: (0, 0))
    size = padded(rows * units)
    return pl.pallas_call(
        lambda *refs: grad_kernel(*refs, units=units),
        grid_spec=pltpu.PrefetchScalarGridSpec(
            num_scalar_prefetch=1,
            grid=(blocks // at_once,),
            in_specs=tap_specs + [whole, whole],
            out_specs=[
                pl.BlockSpec((size, chans), lambda s, order: (0, 0)),
                pl.BlockSpec((at_once, size, chans), lambda s, order: (s, 0, 0)),
            ],
        ),
        out_shape=[
            jax.ShapeDtypeStruct((size, chans), F32),
            jax.ShapeDtypeStruct((blocks, size, chans), F32),
        ],
        compiler_params=pltpu.CompilerParams(vmem_limit_bytes=VMEM),
        name="grad",
    )(order, *(list(taps) * 2), *g)


def back_kernel(g_ref, later_ref, wide_ref, thin_ref, z_ref, patch_ref, out_ref, cells_ref, acc_ref, *, rows, cols):
    depth = pl.program_id(0)
    frames = cells_ref.shape[1] - 2

    @pl.when(depth == 0)
    def _():
        g = jnp.concatenate([g_ref[...], later_ref[...]], axis=0).astype(F32)
        fill_columns(cells_ref, g, rows, cols)

    taps = [window(cells_ref, 2 - k % 3, 2 - depth, 2 - k // 3, frames, rows) for k in range(9)]
    cut = wide_ref.shape[2]
    left = jnp.concatenate([x[:, :cut] for x in taps] + [x[:, cut:] for x in taps], axis=1)
    right = jnp.concatenate([wide_ref[k] for k in range(9)] + [thin_ref[k] for k in range(9)], axis=1)
    total = contract(left, right, ((1,), (1,)))

    @pl.when(depth == 0)
    def _():
        acc_ref[...] = total

    @pl.when(depth == 1)
    def _():
        acc_ref[...] += total

    @pl.when(depth == 2)
    def _():
        z = z_ref[...]
        sig = 1.0 / (1.0 + jnp.exp(-z))
        dz = ((acc_ref[...] + total) * sig * (1.0 + z * (1.0 - sig))).astype(BF16)
        out_ref[...] = contract(patch_ref[...], dz, ((1,), (0,)))


def back(g, later, wide, thin, z, patch_t, rows, cols):
    count, chans = z.shape
    depth_in = patch_t.shape[0]
    frames = count // (rows * cols) + 2
    return pl.pallas_call(
        lambda *refs: back_kernel(*refs, rows=rows, cols=cols),
        grid=(3,),
        in_specs=[
            pl.BlockSpec((count, chans), lambda i: (0, 0)),
            pl.BlockSpec(later.shape, lambda i: (0, 0)),
            pl.BlockSpec((9,) + wide.shape[1:], lambda i: (i, 0, 0)),
            pl.BlockSpec((9,) + thin.shape[1:], lambda i: (i, 0, 0)),
            pl.BlockSpec((count, chans), lambda i: (0, 0)),
            pl.BlockSpec((depth_in, count), lambda i: (0, 0)),
        ],
        out_specs=pl.BlockSpec((depth_in, chans), lambda i: (0, 0)),
        out_shape=jax.ShapeDtypeStruct((depth_in, chans), F32),
        scratch_shapes=[
            pltpu.VMEM((3, frames, rows + 2, cols, chans), BF16),
            pltpu.VMEM((count, chans), F32),
        ],
        compiler_params=pltpu.CompilerParams(vmem_limit_bytes=VMEM),
        name="back",
    )(g, later, wide, thin, z, patch_t)


def packed(x, rows, bound):
    power = jnp.ceil(jnp.log2(jnp.maximum(bound, 1e-30)))
    row = lax.broadcasted_iota(jnp.int32, x.shape, x.ndim - 2)
    return jnp.where(row < rows, x * jnp.exp2(14.0 - power), power).astype(F16)


def across_plane(part, rows, bound, after):
    clips = lax.axis_size("clip")
    payloads = [packed(part[q], rows, bound) for q in range(1, clips // 2)]
    payloads, after = lax.optimization_barrier((payloads, after))
    got = []
    for q in range(1, clips // 2):
        route = [(i, i ^ (2 * q)) for i in range(clips)]
        got.append(lax.ppermute(payloads[q - 1], "clip", route))
    return got, after


def behind(x, *first):
    return lax.optimization_barrier((x, first))[0]


def around(blocks, distance):
    depth = lax.axis_size("tm")
    return lax.ppermute(blocks, "tm", [(i, (i + distance) % depth) for i in range(depth)])


def scales(got, rows, bound):
    powers = [jnp.exp2(x[rows : rows + 1].astype(F32)) for x in got]
    return [power * 2.0**-14 for power in powers], (bound + sum(powers)) * 1.01


def across_depth(own, got, rows, factors, total, after):
    depth = lax.axis_size("tm")
    me = lax.axis_index("tm")
    small = piece_rows(rows)

    def piece(place):
        cut = lambda x: lax.dynamic_slice_in_dim(x, place * small, small + 16, axis=0)
        terms = [cut(x).astype(F32) * factor for x, factor in zip(got, factors)]
        return sum(terms) if own is None else cut(own) + sum(terms)

    payloads = [packed(piece((me + d) % depth), small, total) for d in range(1, depth)]
    after = behind(after, payloads)
    others = [around(payloads[d - 1], d) for d in range(1, depth)]
    return (piece(me), others), after


def spread(parts, smalls, factors, total):
    depth = lax.axis_size("tm")
    sums = []
    for (own, got), small in zip(parts, smalls):
        terms = [x[:small].astype(F32) * factor for x, factor in zip(got, factors)]
        sums.append(own[:small] + sum(terms))
    rows = sum(smalls)
    payload = packed(jnp.pad(jnp.concatenate(sums, axis=0), ((0, 16), (0, 0))), rows, total)
    return [payload] + [around(payload, depth - k) for k in range(1, depth)]


def assembled(pieces, factors, smalls, rows):
    depth = lax.axis_size("tm")
    me = lax.axis_index("tm")
    pieces = [x.astype(F32) * factor for x, factor in zip(pieces, factors)]
    placed = []
    for place in range(depth):
        x = pieces[0]
        for k in range(1, depth):
            x = jnp.where((me + k) % depth == place, pieces[k], x)
        placed.append(x)
    out = []
    at = 0
    for small, count in zip(smalls, rows):
        for place in range(depth):
            left = min(small, count - place * small)
            if left > 0:
                out.append(placed[place][at : at + left])
        at += small
    return out


def shards(latent, offsets, teacher, w_in, w_mid):
    frames = teacher.shape[1]
    rows = teacher.shape[2]
    cols = teacher.shape[3]
    chans = teacher.shape[4]
    plane = rows * cols
    count = frames * plane
    lat_chans = latent.shape[4]
    clips = lax.axis_size("clip")
    total_cells = clips * lax.axis_size("tm") * count
    scale = 2.0 / math.sqrt(total_cells)
    me = lax.axis_index("clip")
    cut = chans - 128
    wide = lax.all_gather(w_mid[:, :cut], "clip", axis=0, tiled=True)
    strip = w_mid[:, cut:]
    strips = [strip]
    for q in range(1, clips // 2):
        strips.append(lax.ppermute(strip, "clip", [(i, i ^ (2 * q)) for i in range(clips)]))
    crop = lax.dynamic_slice_in_dim(latent[0], offsets[0], cols, axis=2).reshape(count, lat_chans).T
    earlier = passed_along(crop[:, count - 4 * plane :], "tm", 1)
    crop_ext = jnp.concatenate([earlier, crop], axis=1)
    patch_t, z, cells, taps, top = front(crop_ext, w_in, rows, cols, count, True)
    mine = jnp.concatenate(behind(strips, top), axis=0)
    theirs = swapped(mine)
    pair_taps, pair_top = front(behind(swapped(crop_ext), mine), w_in, rows, cols, count, False)
    taps = taps.reshape(27 * chans, count)
    pair_taps = pair_taps.reshape(27 * chans, count)
    top, pair_top = jnp.max(top), jnp.max(pair_top)
    block_rows = strip.shape[0]
    thin = jnp.zeros((clips * block_rows, 128), strip.dtype)
    for k in range(clips):
        source = theirs if k % 2 else mine
        piece = source[k // 2 * block_rows : (k // 2 + 1) * block_rows]
        thin = lax.dynamic_update_slice_in_dim(thin, piece, (me ^ k) * block_rows, axis=0)
    wide, thin, pair_taps, top, pair_top = lax.optimization_barrier((wide, thin, pair_taps, top, pair_top))
    wide = wide.reshape(27, chans, cut)
    thin = thin.reshape(27, chans, chans - cut)
    g, head = middle(cells, wide, thin, teacher[0].reshape(count, chans), scale, 2 * plane)
    pair_g = swapped(g)
    later = passed_along(head, "tm", -1)

    third = 27 * chans // clips // 3
    spare = slice(count, count + 1)
    bound = (top * g[spare, :1].astype(F32) + pair_top * pair_g[spare, :1].astype(F32)) * 1.03
    both = (taps, pair_taps)
    in_rows = patch_t.shape[0]

    chips = jnp.arange(clips // 2, dtype=jnp.int32)
    own_a, part = grad_chunk(me ^ (2 * chips), both, (g, pair_g), 0, 2)
    part, later = lax.optimization_barrier((part, later))
    got_a, g = across_plane(part, 2 * third, bound, g)
    _, part = grad_chunk(2 * chips + me % 2, both, (g, pair_g), 2, 1)
    payload = packed(part, third, bound)
    payload, g = lax.optimization_barrier((payload, g))
    groups = [[2 * p + core for p in range(clips // 2)] for core in range(2)]
    got_b = lax.all_to_all(payload, "clip", 0, 0, axis_index_groups=groups, tiled=True)
    got_b = [got_b[p] for p in range(clips // 2)]
    in_part = back(g, later, wide, thin, z, patch_t, rows, cols)

    got_a = behind(got_a, in_part)
    factors, total = scales(got_a, 2 * third, bound)
    (own_a, depth_a), got_b = across_depth(own_a, got_a, 2 * third, factors, total, got_b)
    factors, _ = scales(got_b, third, 0.0)
    (own_b, depth_b), in_part = across_depth(None, got_b, third, factors, total, in_part)
    in_got = lax.all_to_all(in_part.reshape(clips, in_rows // clips, chans), "clip", 0, 0, tiled=True)
    z_total = total
    smalls = [piece_rows(2 * third), piece_rows(third)]
    factors, total = scales(depth_a, smalls[0], z_total)
    in_sum = behind(in_got, depth_a).sum(axis=0)
    in_sum = jnp.broadcast_to(in_sum[None], (lax.axis_size("tm"),) + in_sum.shape)
    depth_b = behind(depth_b, in_sum)
    in_got = lax.all_to_all(in_sum, "tm", 0, 0, tiled=True)
    last = spread([(own_a, depth_a), (own_b, depth_b)], smalls, factors, total)
    in_sum = behind(in_got, last[0]).sum(axis=0)
    in_sum = jnp.broadcast_to(in_sum[None], (clips,) + in_sum.shape)
    last[1:] = behind(last[1:], in_sum)
    grad_in = lax.all_to_all(in_sum, "clip", 0, 0, tiled=True).reshape(in_rows, chans)
    factors, _ = scales(last, sum(smalls), 0.0)
    pieces = assembled(last, factors, smalls, [2 * third, third])
    return (jnp.concatenate(pieces, axis=0), grad_in)


def solution(mesh):
    return jax.shard_map(
        shards,
        mesh=mesh,
        in_specs=(
            P("clip", "tm", None, None, None),
            P("clip"),
            P("clip", "tm", None, None, None),
            P(),
            P("clip", None),
        ),
        out_specs=(P("clip", None), P()),
        check_vma=False,
    )
```

```python
import math

import jax
import jax.numpy as jnp
from jax import lax
from jax.experimental import pallas as pl
from jax.experimental.pallas import tpu as pltpu
from jax.sharding import PartitionSpec as P

F32 = jnp.float32
BF16 = jnp.bfloat16
F16 = jnp.float16
VMEM = 56 * 1024 * 1024


def passed_along(block, axis, distance):
    devices = range(lax.axis_size(axis))
    route = [(i - distance, i) for i in devices if i - distance in devices]
    return lax.ppermute(block, axis, route)


def swapped(block):
    return lax.ppermute(block, "clip", [(i, i ^ 1) for i in range(lax.axis_size("clip"))])


def piece_rows(rows):
    return rows // lax.axis_size("tm") // 16 * 16 + 16


def padded(rows):
    return piece_rows(rows) * lax.axis_size("tm") + 16


def shifted(x, row_off, col_off, rows, cols):
    lanes = x.shape[1]
    lane = lax.broadcasted_iota(jnp.int32, (1, lanes), 1)
    row = (lane // cols) % rows + row_off
    col = lane % cols + col_off
    good = (row >= 0) & (row < rows) & (col >= 0) & (col < cols)
    shift = row_off * cols + col_off
    return jnp.where(good, pltpu.roll(x, (lanes - shift) % lanes, axis=1), 0.0)


def contract(left, right, dims):
    return lax.dot_general(left, right, (dims, ((), ())), preferred_element_type=F32)


def fill_columns(out_ref, x, rows, cols):
    cells, chans = x.shape
    frames = cells // (rows * cols)
    zero = jnp.zeros((frames, cols, chans), BF16)
    place = lax.broadcasted_iota(jnp.int32, (cells, 1), 0) % cols
    for c in range(3):
        moved = x
        if c != 1:
            good = (place + c - 1 >= 0) & (place + c - 1 < cols)
            moved = jnp.where(good, pltpu.roll(x, (1 - c) % cells, axis=0), 0.0)
        out_ref[c, :, 0] = zero
        out_ref[c, :, rows + 1] = zero
        out_ref[c, :, 1 : rows + 1] = moved.astype(BF16).reshape(frames, rows, cols, chans)


def window(ref, column, frame, row, frames, rows):
    x = ref[column, pl.ds(frame, frames), pl.ds(row, rows)]
    return x.reshape(frames * rows * x.shape[2], x.shape[3])


def front_kernel(crop_ref, w_ref, *refs, rows, cols, first):
    if first:
        patch_ref, z_ref, cells_ref, taps_ref, top_ref, full_ref = refs
    else:
        taps_ref, top_ref, full_ref = refs
    plane = rows * cols
    lat = crop_ref.shape[0]
    ext = full_ref.shape[1]
    count = ext - 2 * plane

    @pl.when(pl.program_id(0) == 0)
    def _():
        crop = crop_ref[...].astype(F32)
        for spot in range(9):
            moved = shifted(crop, spot // 3 - 1, spot % 3 - 1, rows, cols).astype(BF16)
            for depth in range(3):
                at = (depth * 9 + spot) * lat
                full_ref[at : at + lat, :] = moved[:, depth * plane : depth * plane + ext]
        if first:
            patch_ref[...] = full_ref[:, 2 * plane :]

    z = contract(w_ref[...], full_ref[...], ((0,), (0,)))
    act = (z * (1.0 / (1.0 + jnp.exp(-z)))).astype(BF16).astype(F32)
    top_ref[...] = jnp.broadcast_to(jnp.max(jnp.abs(act), axis=1, keepdims=True), top_ref.shape)
    for spot in range(9):
        moved = shifted(act, spot // 3 - 1, spot % 3 - 1, rows, cols).astype(BF16)
        for depth in range(3):
            taps_ref[depth * 9 + spot] = moved[:, depth * plane : depth * plane + count]
    if first:
        z_ref[...] = z[:, 2 * plane :].T
        fill_columns(cells_ref, act.T, rows, cols)


def front(crop_t, w_in, rows, cols, count, first):
    chans = w_in.shape[1]
    depth_in = w_in.shape[0]
    plane = rows * cols
    block = 128
    frames = count // plane + 2
    specs = [
        pl.BlockSpec((27, block, count), lambda i: (0, i, 0)),
        pl.BlockSpec((block, 128), lambda i: (i, 0)),
    ]
    shapes = [
        jax.ShapeDtypeStruct((27, chans, count), BF16),
        jax.ShapeDtypeStruct((chans, 128), F32),
    ]
    if first:
        specs = [
            pl.BlockSpec((depth_in, count), lambda i: (0, 0)),
            pl.BlockSpec((count, block), lambda i: (0, i)),
            pl.BlockSpec((3, frames, rows + 2, cols, block), lambda i: (0, 0, 0, 0, i)),
        ] + specs
        shapes = [
            jax.ShapeDtypeStruct((depth_in, count), BF16),
            jax.ShapeDtypeStruct((count, chans), F32),
            jax.ShapeDtypeStruct((3, frames, rows + 2, cols, chans), BF16),
        ] + shapes
    return pl.pallas_call(
        lambda *refs: front_kernel(*refs, rows=rows, cols=cols, first=first),
        grid=(chans // block,),
        in_specs=[
            pl.BlockSpec(crop_t.shape, lambda i: (0, 0)),
            pl.BlockSpec((depth_in, block), lambda i: (0, i)),
        ],
        out_specs=specs,
        out_shape=shapes,
        scratch_shapes=[pltpu.VMEM((depth_in, count + 2 * plane), BF16)],
        compiler_params=pltpu.CompilerParams(vmem_limit_bytes=VMEM),
        name="front",
    )(crop_t, w_in)


def middle_kernel(cells_ref, wide_ref, thin_ref, teacher_ref, g_ref, head_ref, acc_ref, *, scale):
    depth = pl.program_id(0)
    frames = cells_ref.shape[1] - 2
    rows = cells_ref.shape[2] - 2
    left = jnp.concatenate(
        [window(cells_ref, k % 3, depth, k // 3, frames, rows) for k in range(9)], axis=1
    )
    totals = []
    for ref in (wide_ref, thin_ref):
        totals.append(contract(left, ref[...].reshape(left.shape[1], ref.shape[2]), ((1,), (0,))))
    total = jnp.concatenate(totals, axis=1)

    @pl.when(depth == 0)
    def _():
        acc_ref[...] = total

    @pl.when(depth == 1)
    def _():
        acc_ref[...] += total

    @pl.when(depth == 2)
    def _():
        g = ((acc_ref[...] + total - teacher_ref[...].astype(F32)) * scale).astype(BF16)
        count = g.shape[0]
        g_ref[:count, :] = g
        head_ref[...] = g[: head_ref.shape[0]]
        size = jnp.max(jnp.sum(jnp.abs(g.astype(F32)), axis=0, keepdims=True), axis=1, keepdims=True)
        g_ref[count:, :] = jnp.broadcast_to(size, (g_ref.shape[0] - count, g.shape[1])).astype(BF16)


def middle(cells, wide, thin, teacher, scale, head):
    count, chans = teacher.shape
    return pl.pallas_call(
        lambda *refs: middle_kernel(*refs, scale=scale),
        grid=(3,),
        in_specs=[
            pl.BlockSpec(cells.shape, lambda i: (0,) * 5),
            pl.BlockSpec((9,) + wide.shape[1:], lambda i: (i, 0, 0)),
            pl.BlockSpec((9,) + thin.shape[1:], lambda i: (i, 0, 0)),
            pl.BlockSpec((count, chans), lambda i: (0, 0)),
        ],
        out_specs=[
            pl.BlockSpec((count + 16, chans), lambda i: (0, 0)),
            pl.BlockSpec((head, chans), lambda i: (0, 0)),
        ],
        out_shape=[
            jax.ShapeDtypeStruct((count + 16, chans), BF16),
            jax.ShapeDtypeStruct((head, chans), BF16),
        ],
        scratch_shapes=[pltpu.VMEM((count, chans), F32)],
        compiler_params=pltpu.CompilerParams(vmem_limit_bytes=VMEM),
        name="middle",
    )(cells, wide, thin, teacher)


def grad_kernel(order_ref, *refs, units):
    own_ref, out_ref = refs[-2:]
    g_refs = refs[-4:-2]
    at_once = out_ref.shape[0]
    rows = refs[0].shape[0]
    spare = own_ref.shape[0] - units * rows
    zero = jnp.zeros((spare, own_ref.shape[1]), F32)
    for i in range(at_once):
        for k in range(units):
            at = 2 * (i * units + k)
            total = contract(refs[at][...], g_refs[0][...], ((1,), (0,)))
            total += contract(refs[at + 1][...], g_refs[1][...], ((1,), (0,)))
            out_ref[i, k * rows : (k + 1) * rows, :] = total
        out_ref[i, units * rows :, :] = zero

    @pl.when(pl.program_id(0) == 0)
    def _():
        own_ref[...] = out_ref[0]


def grad_chunk(order, taps, g, first, units):
    blocks = order.shape[0]
    total, count = taps[0].shape
    chans = g[0].shape[1]
    rows = total // (2 * blocks) // 3
    at_once = 2 // units
    tap_specs = []
    for i in range(at_once):
        for k in range(units):
            spec = pl.BlockSpec(
                (rows, count), lambda s, order, i=i, k=k: (order[s * at_once + i] * 3 + first + k, 0)
            )
            tap_specs += [spec, spec]
    whole = pl.BlockSpec((count, chans), lambda s, order: (0, 0))
    size = padded(rows * units)
    return pl.pallas_call(
        lambda *refs: grad_kernel(*refs, units=units),
        grid_spec=pltpu.PrefetchScalarGridSpec(
            num_scalar_prefetch=1,
            grid=(blocks // at_once,),
            in_specs=tap_specs + [whole, whole],
            out_specs=[
                pl.BlockSpec((size, chans), lambda s, order: (0, 0)),
                pl.BlockSpec((at_once, size, chans), lambda s, order: (s, 0, 0)),
            ],
        ),
        out_shape=[
            jax.ShapeDtypeStruct((size, chans), F32),
            jax.ShapeDtypeStruct((blocks, size, chans), F32),
        ],
        compiler_params=pltpu.CompilerParams(vmem_limit_bytes=VMEM),
        name="grad",
    )(order, *(list(taps) * 2), *g)


def back_kernel(g_ref, later_ref, wide_ref, thin_ref, z_ref, patch_ref, out_ref, cells_ref, acc_ref, *, rows, cols):
    depth = pl.program_id(0)
    frames = cells_ref.shape[1] - 2

    @pl.when(depth == 0)
    def _():
        g = jnp.concatenate([g_ref[...], later_ref[...]], axis=0).astype(F32)
        fill_columns(cells_ref, g, rows, cols)

    taps = [window(cells_ref, 2 - k % 3, 2 - depth, 2 - k // 3, frames, rows) for k in range(9)]
    cut = wide_ref.shape[2]
    left = jnp.concatenate([x[:, :cut] for x in taps] + [x[:, cut:] for x in taps], axis=1)
    right = jnp.concatenate([wide_ref[k] for k in range(9)] + [thin_ref[k] for k in range(9)], axis=1)
    total = contract(left, right, ((1,), (1,)))

    @pl.when(depth == 0)
    def _():
        acc_ref[...] = total

    @pl.when(depth == 1)
    def _():
        acc_ref[...] += total

    @pl.when(depth == 2)
    def _():
        z = z_ref[...]
        sig = 1.0 / (1.0 + jnp.exp(-z))
        dz = ((acc_ref[...] + total) * sig * (1.0 + z * (1.0 - sig))).astype(BF16)
        out_ref[...] = contract(patch_ref[...], dz, ((1,), (0,)))


def back(g, later, wide, thin, z, patch_t, rows, cols):
    count, chans = z.shape
    depth_in = patch_t.shape[0]
    frames = count // (rows * cols) + 2
    return pl.pallas_call(
        lambda *refs: back_kernel(*refs, rows=rows, cols=cols),
        grid=(3,),
        in_specs=[
            pl.BlockSpec((count, chans), lambda i: (0, 0)),
            pl.BlockSpec(later.shape, lambda i: (0, 0)),
            pl.BlockSpec((9,) + wide.shape[1:], lambda i: (i, 0, 0)),
            pl.BlockSpec((9,) + thin.shape[1:], lambda i: (i, 0, 0)),
            pl.BlockSpec((count, chans), lambda i: (0, 0)),
            pl.BlockSpec((depth_in, count), lambda i: (0, 0)),
        ],
        out_specs=pl.BlockSpec((depth_in, chans), lambda i: (0, 0)),
        out_shape=jax.ShapeDtypeStruct((depth_in, chans), F32),
        scratch_shapes=[
            pltpu.VMEM((3, frames, rows + 2, cols, chans), BF16),
            pltpu.VMEM((count, chans), F32),
        ],
        compiler_params=pltpu.CompilerParams(vmem_limit_bytes=VMEM),
        name="back",
    )(g, later, wide, thin, z, patch_t)


def packed(x, rows, bound):
    power = jnp.ceil(jnp.log2(jnp.maximum(bound, 1e-30)))
    row = lax.broadcasted_iota(jnp.int32, x.shape, x.ndim - 2)
    return jnp.where(row < rows, x * jnp.exp2(14.0 - power), power).astype(F16)


def across_plane(part, rows, bound, after):
    clips = lax.axis_size("clip")
    payloads = [packed(part[q], rows, bound) for q in range(1, clips // 2)]
    payloads, after = lax.optimization_barrier((payloads, after))
    got = []
    for q in range(1, clips // 2):
        route = [(i, i ^ (2 * q)) for i in range(clips)]
        got.append(lax.ppermute(payloads[q - 1], "clip", route))
    return got, after


def behind(x, *first):
    return lax.optimization_barrier((x, first))[0]


def around(blocks, distance):
    depth = lax.axis_size("tm")
    return lax.ppermute(blocks, "tm", [(i, (i + distance) % depth) for i in range(depth)])


def scales(got, rows, bound):
    powers = [jnp.exp2(x[rows : rows + 1].astype(F32)) for x in got]
    return [power * 2.0**-14 for power in powers], (bound + sum(powers)) * 1.01


def across_depth(own, got, rows, factors, total, after):
    depth = lax.axis_size("tm")
    me = lax.axis_index("tm")
    small = piece_rows(rows)

    def piece(place):
        cut = lambda x: lax.dynamic_slice_in_dim(x, place * small, small + 16, axis=0)
        terms = [cut(x).astype(F32) * factor for x, factor in zip(got, factors)]
        return sum(terms) if own is None else cut(own) + sum(terms)

    payloads = [packed(piece((me + d) % depth), small, total) for d in range(1, depth)]
    after = behind(after, payloads)
    others = [around(payloads[d - 1], d) for d in range(1, depth)]
    return (piece(me), others), after


def spread(parts, smalls, factors, total):
    depth = lax.axis_size("tm")
    sums = []
    for (own, got), small in zip(parts, smalls):
        terms = [x[:small].astype(F32) * factor for x, factor in zip(got, factors)]
        sums.append(own[:small] + sum(terms))
    rows = sum(smalls)
    payload = packed(jnp.pad(jnp.concatenate(sums, axis=0), ((0, 16), (0, 0))), rows, total)
    return [payload] + [around(payload, depth - k) for k in range(1, depth)]


def assembled(pieces, factors, smalls, rows):
    depth = lax.axis_size("tm")
    me = lax.axis_index("tm")
    pieces = [x.astype(F32) * factor for x, factor in zip(pieces, factors)]
    placed = []
    for place in range(depth):
        x = pieces[0]
        for k in range(1, depth):
            x = jnp.where((me + k) % depth == place, pieces[k], x)
        placed.append(x)
    out = []
    at = 0
    for small, count in zip(smalls, rows):
        for place in range(depth):
            left = min(small, count - place * small)
            if left > 0:
                out.append(placed[place][at : at + left])
        at += small
    return out


def shards(latent, offsets, teacher, w_in, w_mid):
    frames = teacher.shape[1]
    rows = teacher.shape[2]
    cols = teacher.shape[3]
    chans = teacher.shape[4]
    plane = rows * cols
    count = frames * plane
    lat_chans = latent.shape[4]
    clips = lax.axis_size("clip")
    total_cells = clips * lax.axis_size("tm") * count
    scale = 2.0 / math.sqrt(total_cells)
    me = lax.axis_index("clip")
    cut = chans - 128
    wide = lax.all_gather(w_mid[:, :cut], "clip", axis=0, tiled=True)
    strip = w_mid[:, cut:]
    strips = [strip]
    for q in range(1, clips // 2):
        strips.append(lax.ppermute(strip, "clip", [(i, i ^ (2 * q)) for i in range(clips)]))
    crop = lax.dynamic_slice_in_dim(latent[0], offsets[0], cols, axis=2).reshape(count, lat_chans).T
    earlier = passed_along(crop[:, count - 4 * plane :], "tm", 1)
    crop_ext = jnp.concatenate([earlier, crop], axis=1)
    patch_t, z, cells, taps, top = front(crop_ext, w_in, rows, cols, count, True)
    mine = jnp.concatenate(behind(strips, top), axis=0)
    theirs = swapped(mine)
    pair_taps, pair_top = front(behind(swapped(crop_ext), mine), w_in, rows, cols, count, False)
    taps = taps.reshape(27 * chans, count)
    pair_taps = pair_taps.reshape(27 * chans, count)
    top, pair_top = jnp.max(top), jnp.max(pair_top)
    block_rows = strip.shape[0]
    thin = jnp.zeros((clips * block_rows, 128), strip.dtype)
    for k in range(clips):
        source = theirs if k % 2 else mine
        piece = source[k // 2 * block_rows : (k // 2 + 1) * block_rows]
        thin = lax.dynamic_update_slice_in_dim(thin, piece, (me ^ k) * block_rows, axis=0)
    wide, thin, pair_taps, top, pair_top = lax.optimization_barrier((wide, thin, pair_taps, top, pair_top))
    wide = wide.reshape(27, chans, cut)
    thin = thin.reshape(27, chans, chans - cut)
    g, head = middle(cells, wide, thin, teacher[0].reshape(count, chans), scale, 2 * plane)
    pair_g = swapped(g)
    later = passed_along(head, "tm", -1)

    third = 27 * chans // clips // 3
    spare = slice(count, count + 1)
    bound = (top * g[spare, :1].astype(F32) + pair_top * pair_g[spare, :1].astype(F32)) * 1.03
    both = (taps, pair_taps)
    in_rows = patch_t.shape[0]

    chips = jnp.arange(clips // 2, dtype=jnp.int32)
    own_a, part = grad_chunk(me ^ (2 * chips), both, (g, pair_g), 0, 2)
    part, later = lax.optimization_barrier((part, later))
    got_a, g = across_plane(part, 2 * third, bound, g)
    _, part = grad_chunk(2 * chips + me % 2, both, (g, pair_g), 2, 1)
    payload = packed(part, third, bound)
    payload, g = lax.optimization_barrier((payload, g))
    groups = [[2 * p + core for p in range(clips // 2)] for core in range(2)]
    got_b = lax.all_to_all(payload, "clip", 0, 0, axis_index_groups=groups, tiled=True)
    got_b = [got_b[p] for p in range(clips // 2)]
    in_part = back(g, later, wide, thin, z, patch_t, rows, cols)

    got_a = behind(got_a, in_part)
    factors, total = scales(got_a, 2 * third, bound)
    (own_a, depth_a), got_b = across_depth(own_a, got_a, 2 * third, factors, total, got_b)
    factors, _ = scales(got_b, third, 0.0)
    (own_b, depth_b), in_part = across_depth(None, got_b, third, factors, total, in_part)
    in_got = lax.all_to_all(in_part.reshape(clips, in_rows // clips, chans), "clip", 0, 0, tiled=True)
    z_total = total
    smalls = [piece_rows(2 * third), piece_rows(third)]
    depth_a = behind(depth_a, depth_b)
    factors, total = scales(depth_a, smalls[0], z_total)
    last = spread([(own_a, depth_a), (own_b, depth_b)], smalls, factors, total)
    in_sum = behind(in_got, last[0]).sum(axis=0)
    in_sum = jnp.broadcast_to(in_sum[None], (lax.axis_size("tm"),) + in_sum.shape)
    in_got = lax.all_to_all(in_sum, "tm", 0, 0, tiled=True)
    in_sum = in_got.sum(axis=0)
    in_sum = jnp.broadcast_to(in_sum[None], (clips,) + in_sum.shape)
    last[1:] = behind(last[1:], in_sum)
    grad_in = lax.all_to_all(in_sum, "clip", 0, 0, tiled=True).reshape(in_rows, chans)
    factors, _ = scales(last, sum(smalls), 0.0)
    pieces = assembled(last, factors, smalls, [2 * third, third])
    return (jnp.concatenate(pieces, axis=0), grad_in)


def solution(mesh):
    return jax.shard_map(
        shards,
        mesh=mesh,
        in_specs=(
            P("clip", "tm", None, None, None),
            P("clip"),
            P("clip", "tm", None, None, None),
            P(),
            P("clip", None),
        ),
        out_specs=(P("clip", None), P()),
        check_vma=False,
    )
```

```python
import math

import jax
import jax.numpy as jnp
from jax import lax
from jax.experimental import pallas as pl
from jax.experimental.pallas import tpu as pltpu
from jax.sharding import PartitionSpec as P

F32 = jnp.float32
BF16 = jnp.bfloat16
F16 = jnp.float16
VMEM = 56 * 1024 * 1024


def passed_along(block, axis, distance):
    devices = range(lax.axis_size(axis))
    route = [(i - distance, i) for i in devices if i - distance in devices]
    return lax.ppermute(block, axis, route)


def swapped(block):
    return lax.ppermute(block, "clip", [(i, i ^ 1) for i in range(lax.axis_size("clip"))])


def piece_rows(rows):
    return rows // lax.axis_size("tm") // 16 * 16 + 16


def padded(rows):
    return piece_rows(rows) * lax.axis_size("tm") + 16


def shifted(x, row_off, col_off, rows, cols):
    lanes = x.shape[1]
    lane = lax.broadcasted_iota(jnp.int32, (1, lanes), 1)
    row = (lane // cols) % rows + row_off
    col = lane % cols + col_off
    good = (row >= 0) & (row < rows) & (col >= 0) & (col < cols)
    shift = row_off * cols + col_off
    return jnp.where(good, pltpu.roll(x, (lanes - shift) % lanes, axis=1), 0.0)


def contract(left, right, dims):
    return lax.dot_general(left, right, (dims, ((), ())), preferred_element_type=F32)


def fill_columns(out_ref, x, rows, cols):
    cells, chans = x.shape
    frames = cells // (rows * cols)
    zero = jnp.zeros((frames, cols, chans), BF16)
    place = lax.broadcasted_iota(jnp.int32, (cells, 1), 0) % cols
    for c in range(3):
        moved = x
        if c != 1:
            good = (place + c - 1 >= 0) & (place + c - 1 < cols)
            moved = jnp.where(good, pltpu.roll(x, (1 - c) % cells, axis=0), 0.0)
        out_ref[c, :, 0] = zero
        out_ref[c, :, rows + 1] = zero
        out_ref[c, :, 1 : rows + 1] = moved.astype(BF16).reshape(frames, rows, cols, chans)


def window(ref, column, frame, row, frames, rows):
    x = ref[column, pl.ds(frame, frames), pl.ds(row, rows)]
    return x.reshape(frames * rows * x.shape[2], x.shape[3])


def front_kernel(crop_ref, w_ref, *refs, rows, cols, first):
    if first:
        patch_ref, z_ref, cells_ref, taps_ref, top_ref, full_ref = refs
    else:
        taps_ref, top_ref, full_ref = refs
    plane = rows * cols
    lat = crop_ref.shape[0]
    ext = full_ref.shape[1]
    count = ext - 2 * plane

    @pl.when(pl.program_id(0) == 0)
    def _():
        crop = crop_ref[...].astype(F32)
        for spot in range(9):
            moved = shifted(crop, spot // 3 - 1, spot % 3 - 1, rows, cols).astype(BF16)
            for depth in range(3):
                at = (depth * 9 + spot) * lat
                full_ref[at : at + lat, :] = moved[:, depth * plane : depth * plane + ext]
        if first:
            patch_ref[...] = full_ref[:, 2 * plane :]

    z = contract(w_ref[...], full_ref[...], ((0,), (0,)))
    act = (z * (1.0 / (1.0 + jnp.exp(-z)))).astype(BF16).astype(F32)
    top_ref[...] = jnp.broadcast_to(jnp.max(jnp.abs(act), axis=1, keepdims=True), top_ref.shape)
    for spot in range(9):
        moved = shifted(act, spot // 3 - 1, spot % 3 - 1, rows, cols).astype(BF16)
        for depth in range(3):
            taps_ref[depth * 9 + spot] = moved[:, depth * plane : depth * plane + count]
    if first:
        z_ref[...] = z[:, 2 * plane :].T
        fill_columns(cells_ref, act.T, rows, cols)


def front(crop_t, w_in, rows, cols, count, first):
    chans = w_in.shape[1]
    depth_in = w_in.shape[0]
    plane = rows * cols
    block = 128
    frames = count // plane + 2
    specs = [
        pl.BlockSpec((27, block, count), lambda i: (0, i, 0)),
        pl.BlockSpec((block, 128), lambda i: (i, 0)),
    ]
    shapes = [
        jax.ShapeDtypeStruct((27, chans, count), BF16),
        jax.ShapeDtypeStruct((chans, 128), F32),
    ]
    if first:
        specs = [
            pl.BlockSpec((depth_in, count), lambda i: (0, 0)),
            pl.BlockSpec((count, block), lambda i: (0, i)),
            pl.BlockSpec((3, frames, rows + 2, cols, block), lambda i: (0, 0, 0, 0, i)),
        ] + specs
        shapes = [
            jax.ShapeDtypeStruct((depth_in, count), BF16),
            jax.ShapeDtypeStruct((count, chans), F32),
            jax.ShapeDtypeStruct((3, frames, rows + 2, cols, chans), BF16),
        ] + shapes
    return pl.pallas_call(
        lambda *refs: front_kernel(*refs, rows=rows, cols=cols, first=first),
        grid=(chans // block,),
        in_specs=[
            pl.BlockSpec(crop_t.shape, lambda i: (0, 0)),
            pl.BlockSpec((depth_in, block), lambda i: (0, i)),
        ],
        out_specs=specs,
        out_shape=shapes,
        scratch_shapes=[pltpu.VMEM((depth_in, count + 2 * plane), BF16)],
        compiler_params=pltpu.CompilerParams(vmem_limit_bytes=VMEM),
        name="front",
    )(crop_t, w_in)


def middle_kernel(cells_ref, wide_ref, thin_ref, teacher_ref, g_ref, head_ref, acc_ref, *, scale):
    depth = pl.program_id(0)
    frames = cells_ref.shape[1] - 2
    rows = cells_ref.shape[2] - 2
    left = jnp.concatenate(
        [window(cells_ref, k % 3, depth, k // 3, frames, rows) for k in range(9)], axis=1
    )
    totals = []
    for ref in (wide_ref, thin_ref):
        totals.append(contract(left, ref[...].reshape(left.shape[1], ref.shape[2]), ((1,), (0,))))
    total = jnp.concatenate(totals, axis=1)

    @pl.when(depth == 0)
    def _():
        acc_ref[...] = total

    @pl.when(depth == 1)
    def _():
        acc_ref[...] += total

    @pl.when(depth == 2)
    def _():
        g = ((acc_ref[...] + total - teacher_ref[...].astype(F32)) * scale).astype(BF16)
        count = g.shape[0]
        g_ref[:count, :] = g
        head_ref[...] = g[: head_ref.shape[0]]
        size = jnp.max(jnp.sum(jnp.abs(g.astype(F32)), axis=0, keepdims=True), axis=1, keepdims=True)
        g_ref[count:, :] = jnp.broadcast_to(size, (g_ref.shape[0] - count, g.shape[1])).astype(BF16)


def middle(cells, wide, thin, teacher, scale, head):
    count, chans = teacher.shape
    return pl.pallas_call(
        lambda *refs: middle_kernel(*refs, scale=scale),
        grid=(3,),
        in_specs=[
            pl.BlockSpec(cells.shape, lambda i: (0,) * 5),
            pl.BlockSpec((9,) + wide.shape[1:], lambda i: (i, 0, 0)),
            pl.BlockSpec((9,) + thin.shape[1:], lambda i: (i, 0, 0)),
            pl.BlockSpec((count, chans), lambda i: (0, 0)),
        ],
        out_specs=[
            pl.BlockSpec((count + 16, chans), lambda i: (0, 0)),
            pl.BlockSpec((head, chans), lambda i: (0, 0)),
        ],
        out_shape=[
            jax.ShapeDtypeStruct((count + 16, chans), BF16),
            jax.ShapeDtypeStruct((head, chans), BF16),
        ],
        scratch_shapes=[pltpu.VMEM((count, chans), F32)],
        compiler_params=pltpu.CompilerParams(vmem_limit_bytes=VMEM),
        name="middle",
    )(cells, wide, thin, teacher)


def grad_kernel(order_ref, *refs, units):
    own_ref, out_ref = refs[-2:]
    g_refs = refs[-4:-2]
    at_once = out_ref.shape[0]
    rows = refs[0].shape[0]
    spare = own_ref.shape[0] - units * rows
    zero = jnp.zeros((spare, own_ref.shape[1]), F32)
    for i in range(at_once):
        for k in range(units):
            at = 2 * (i * units + k)
            total = contract(refs[at][...], g_refs[0][...], ((1,), (0,)))
            total += contract(refs[at + 1][...], g_refs[1][...], ((1,), (0,)))
            out_ref[i, k * rows : (k + 1) * rows, :] = total
        out_ref[i, units * rows :, :] = zero

    @pl.when(pl.program_id(0) == 0)
    def _():
        own_ref[...] = out_ref[0]


def grad_chunk(order, taps, g, first, units):
    blocks = order.shape[0]
    total, count = taps[0].shape
    chans = g[0].shape[1]
    rows = total // (2 * blocks) // 3
    at_once = 2 // units
    tap_specs = []
    for i in range(at_once):
        for k in range(units):
            spec = pl.BlockSpec(
                (rows, count), lambda s, order, i=i, k=k: (order[s * at_once + i] * 3 + first + k, 0)
            )
            tap_specs += [spec, spec]
    whole = pl.BlockSpec((count, chans), lambda s, order: (0, 0))
    size = padded(rows * units)
    return pl.pallas_call(
        lambda *refs: grad_kernel(*refs, units=units),
        grid_spec=pltpu.PrefetchScalarGridSpec(
            num_scalar_prefetch=1,
            grid=(blocks // at_once,),
            in_specs=tap_specs + [whole, whole],
            out_specs=[
                pl.BlockSpec((size, chans), lambda s, order: (0, 0)),
                pl.BlockSpec((at_once, size, chans), lambda s, order: (s, 0, 0)),
            ],
        ),
        out_shape=[
            jax.ShapeDtypeStruct((size, chans), F32),
            jax.ShapeDtypeStruct((blocks, size, chans), F32),
        ],
        compiler_params=pltpu.CompilerParams(vmem_limit_bytes=VMEM),
        name="grad",
    )(order, *(list(taps) * 2), *g)


def back_kernel(g_ref, later_ref, wide_ref, thin_ref, z_ref, patch_ref, out_ref, cells_ref, acc_ref, *, rows, cols):
    depth = pl.program_id(0)
    frames = cells_ref.shape[1] - 2

    @pl.when(depth == 0)
    def _():
        g = jnp.concatenate([g_ref[...], later_ref[...]], axis=0).astype(F32)
        fill_columns(cells_ref, g, rows, cols)

    taps = [window(cells_ref, 2 - k % 3, 2 - depth, 2 - k // 3, frames, rows) for k in range(9)]
    cut = wide_ref.shape[2]
    left = jnp.concatenate([x[:, :cut] for x in taps] + [x[:, cut:] for x in taps], axis=1)
    right = jnp.concatenate([wide_ref[k] for k in range(9)] + [thin_ref[k] for k in range(9)], axis=1)
    total = contract(left, right, ((1,), (1,)))

    @pl.when(depth == 0)
    def _():
        acc_ref[...] = total

    @pl.when(depth == 1)
    def _():
        acc_ref[...] += total

    @pl.when(depth == 2)
    def _():
        z = z_ref[...]
        sig = 1.0 / (1.0 + jnp.exp(-z))
        dz = ((acc_ref[...] + total) * sig * (1.0 + z * (1.0 - sig))).astype(BF16)
        out_ref[...] = contract(patch_ref[...], dz, ((1,), (0,)))


def back(g, later, wide, thin, z, patch_t, rows, cols):
    count, chans = z.shape
    depth_in = patch_t.shape[0]
    frames = count // (rows * cols) + 2
    return pl.pallas_call(
        lambda *refs: back_kernel(*refs, rows=rows, cols=cols),
        grid=(3,),
        in_specs=[
            pl.BlockSpec((count, chans), lambda i: (0, 0)),
            pl.BlockSpec(later.shape, lambda i: (0, 0)),
            pl.BlockSpec((9,) + wide.shape[1:], lambda i: (i, 0, 0)),
            pl.BlockSpec((9,) + thin.shape[1:], lambda i: (i, 0, 0)),
            pl.BlockSpec((count, chans), lambda i: (0, 0)),
            pl.BlockSpec((depth_in, count), lambda i: (0, 0)),
        ],
        out_specs=pl.BlockSpec((depth_in, chans), lambda i: (0, 0)),
        out_shape=jax.ShapeDtypeStruct((depth_in, chans), F32),
        scratch_shapes=[
            pltpu.VMEM((3, frames, rows + 2, cols, chans), BF16),
            pltpu.VMEM((count, chans), F32),
        ],
        compiler_params=pltpu.CompilerParams(vmem_limit_bytes=VMEM),
        name="back",
    )(g, later, wide, thin, z, patch_t)


def packed(x, rows, bound):
    power = jnp.ceil(jnp.log2(jnp.maximum(bound, 1e-30)))
    row = lax.broadcasted_iota(jnp.int32, x.shape, x.ndim - 2)
    return jnp.where(row < rows, x * jnp.exp2(14.0 - power), power).astype(F16)


def across_plane(part, rows, bound, after):
    clips = lax.axis_size("clip")
    payloads = [packed(part[q], rows, bound) for q in range(1, clips // 2)]
    payloads, after = lax.optimization_barrier((payloads, after))
    got = []
    for q in range(1, clips // 2):
        route = [(i, i ^ (2 * q)) for i in range(clips)]
        got.append(lax.ppermute(payloads[q - 1], "clip", route))
    return got, after


def behind(x, *first):
    return lax.optimization_barrier((x, first))[0]


def around(blocks, distance):
    depth = lax.axis_size("tm")
    return lax.ppermute(blocks, "tm", [(i, (i + distance) % depth) for i in range(depth)])


def scales(got, rows, bound):
    powers = [jnp.exp2(x[rows : rows + 1].astype(F32)) for x in got]
    return [power * 2.0**-14 for power in powers], (bound + sum(powers)) * 1.01


def across_depth(own, got, rows, factors, total, after):
    depth = lax.axis_size("tm")
    me = lax.axis_index("tm")
    small = piece_rows(rows)

    def piece(place):
        cut = lambda x: lax.dynamic_slice_in_dim(x, place * small, small + 16, axis=0)
        terms = [cut(x).astype(F32) * factor for x, factor in zip(got, factors)]
        return sum(terms) if own is None else cut(own) + sum(terms)

    payloads = [packed(piece((me + d) % depth), small, total) for d in range(1, depth)]
    after = behind(after, payloads)
    others = [around(payloads[d - 1], d) for d in range(1, depth)]
    return (piece(me), others), after


def spread(parts, smalls, factors, total):
    depth = lax.axis_size("tm")
    sums = []
    for (own, got), small in zip(parts, smalls):
        terms = [x[:small].astype(F32) * factor for x, factor in zip(got, factors)]
        sums.append(own[:small] + sum(terms))
    rows = sum(smalls)
    payload = packed(jnp.pad(jnp.concatenate(sums, axis=0), ((0, 16), (0, 0))), rows, total)
    return [payload] + [around(payload, depth - k) for k in range(1, depth)]


def assembled(pieces, factors, smalls, rows):
    depth = lax.axis_size("tm")
    me = lax.axis_index("tm")
    pieces = [x.astype(F32) * factor for x, factor in zip(pieces, factors)]
    placed = []
    for place in range(depth):
        x = pieces[0]
        for k in range(1, depth):
            x = jnp.where((me + k) % depth == place, pieces[k], x)
        placed.append(x)
    out = []
    at = 0
    for small, count in zip(smalls, rows):
        for place in range(depth):
            left = min(small, count - place * small)
            if left > 0:
                out.append(placed[place][at : at + left])
        at += small
    return out


def shards(latent, offsets, teacher, w_in, w_mid):
    frames = teacher.shape[1]
    rows = teacher.shape[2]
    cols = teacher.shape[3]
    chans = teacher.shape[4]
    plane = rows * cols
    count = frames * plane
    lat_chans = latent.shape[4]
    clips = lax.axis_size("clip")
    total_cells = clips * lax.axis_size("tm") * count
    scale = 2.0 / math.sqrt(total_cells)
    me = lax.axis_index("clip")
    cut = chans - 128
    wide = lax.all_gather(w_mid[:, :cut], "clip", axis=0, tiled=True)
    strip = w_mid[:, cut:]
    strips = [strip]
    for q in range(1, clips // 2):
        strips.append(lax.ppermute(strip, "clip", [(i, i ^ (2 * q)) for i in range(clips)]))
    crop = lax.dynamic_slice_in_dim(latent[0], offsets[0], cols, axis=2).reshape(count, lat_chans).T
    earlier = passed_along(crop[:, count - 4 * plane :], "tm", 1)
    crop_ext = jnp.concatenate([earlier, crop], axis=1)
    patch_t, z, cells, taps, top = front(crop_ext, w_in, rows, cols, count, True)
    mine = jnp.concatenate(behind(strips, top), axis=0)
    theirs = swapped(mine)
    pair_taps, pair_top = front(behind(swapped(crop_ext), mine), w_in, rows, cols, count, False)
    taps = taps.reshape(27 * chans, count)
    pair_taps = pair_taps.reshape(27 * chans, count)
    top, pair_top = jnp.max(top), jnp.max(pair_top)
    block_rows = strip.shape[0]
    thin = jnp.zeros((clips * block_rows, 128), strip.dtype)
    for k in range(clips):
        source = theirs if k % 2 else mine
        piece = source[k // 2 * block_rows : (k // 2 + 1) * block_rows]
        thin = lax.dynamic_update_slice_in_dim(thin, piece, (me ^ k) * block_rows, axis=0)
    wide, thin, pair_taps, top, pair_top = lax.optimization_barrier((wide, thin, pair_taps, top, pair_top))
    wide = wide.reshape(27, chans, cut)
    thin = thin.reshape(27, chans, chans - cut)
    g, head = middle(cells, wide, thin, teacher[0].reshape(count, chans), scale, 2 * plane)
    pair_g = swapped(g)
    later = passed_along(head, "tm", -1)

    third = 27 * chans // clips // 3
    spare = slice(count, count + 1)
    bound = (top * g[spare, :1].astype(F32) + pair_top * pair_g[spare, :1].astype(F32)) * 1.03
    both = (taps, pair_taps)
    in_rows = patch_t.shape[0]

    chips = jnp.arange(clips // 2, dtype=jnp.int32)
    own_a, part = grad_chunk(me ^ (2 * chips), both, (g, pair_g), 0, 1)
    part, later = lax.optimization_barrier((part, later))
    got_a, g = across_plane(part, third, bound, g)
    _, part = grad_chunk(2 * chips + me % 2, both, (g, pair_g), 1, 2)
    payload = packed(behind(part, got_a), 2 * third, bound)
    payload, g = lax.optimization_barrier((payload, g))
    groups = [[2 * p + core for p in range(clips // 2)] for core in range(2)]
    got_b = lax.all_to_all(payload, "clip", 0, 0, axis_index_groups=groups, tiled=True)
    got_b = [got_b[p] for p in range(clips // 2)]
    got_a = behind(got_a, payload)
    factors, total = scales(got_a, third, bound)
    (own_a, depth_a), g = across_depth(own_a, got_a, third, factors, total, g)
    in_part = back(g, later, wide, thin, z, patch_t, rows, cols)
    got_b = behind(got_b, in_part)
    factors, _ = scales(got_b, 2 * third, 0.0)
    (own_b, depth_b), in_part = across_depth(None, got_b, 2 * third, factors, total, in_part)
    in_got = lax.all_to_all(in_part.reshape(clips, in_rows // clips, chans), "clip", 0, 0, tiled=True)
    z_total = total
    smalls = [piece_rows(third), piece_rows(2 * third)]
    factors, total = scales(depth_a, smalls[0], z_total)
    in_sum = behind(in_got, depth_a).sum(axis=0)
    in_sum = jnp.broadcast_to(in_sum[None], (lax.axis_size("tm"),) + in_sum.shape)
    depth_b = behind(depth_b, in_sum)
    in_got = lax.all_to_all(in_sum, "tm", 0, 0, tiled=True)
    last = spread([(own_a, depth_a), (own_b, depth_b)], smalls, factors, total)
    in_sum = behind(in_got, last[0]).sum(axis=0)
    in_sum = jnp.broadcast_to(in_sum[None], (clips,) + in_sum.shape)
    last[1:] = behind(last[1:], in_sum)
    grad_in = lax.all_to_all(in_sum, "clip", 0, 0, tiled=True).reshape(in_rows, chans)
    factors, _ = scales(last, sum(smalls), 0.0)
    pieces = assembled(last, factors, smalls, [third, 2 * third])
    return (jnp.concatenate(pieces, axis=0), grad_in)


def solution(mesh):
    return jax.shard_map(
        shards,
        mesh=mesh,
        in_specs=(
            P("clip", "tm", None, None, None),
            P("clip"),
            P("clip", "tm", None, None, None),
            P(),
            P("clip", None),
        ),
        out_specs=(P("clip", None), P()),
        check_vma=False,
    )
```

```python
import math

import jax
import jax.numpy as jnp
from jax import lax
from jax.experimental import pallas as pl
from jax.experimental.pallas import tpu as pltpu
from jax.sharding import PartitionSpec as P

F32 = jnp.float32
BF16 = jnp.bfloat16
F16 = jnp.float16
VMEM = 56 * 1024 * 1024


def passed_along(block, axis, distance):
    devices = range(lax.axis_size(axis))
    route = [(i - distance, i) for i in devices if i - distance in devices]
    return lax.ppermute(block, axis, route)


def swapped(block):
    return lax.ppermute(block, "clip", [(i, i ^ 1) for i in range(lax.axis_size("clip"))])


def piece_rows(rows):
    return rows // lax.axis_size("tm") // 16 * 16 + 16


def padded(rows):
    return piece_rows(rows) * lax.axis_size("tm") + 16


def shifted(x, row_off, col_off, rows, cols):
    lanes = x.shape[1]
    lane = lax.broadcasted_iota(jnp.int32, (1, lanes), 1)
    row = (lane // cols) % rows + row_off
    col = lane % cols + col_off
    good = (row >= 0) & (row < rows) & (col >= 0) & (col < cols)
    shift = row_off * cols + col_off
    return jnp.where(good, pltpu.roll(x, (lanes - shift) % lanes, axis=1), 0.0)


def contract(left, right, dims):
    return lax.dot_general(left, right, (dims, ((), ())), preferred_element_type=F32)


def fill_columns(out_ref, x, rows, cols):
    cells, chans = x.shape
    frames = cells // (rows * cols)
    zero = jnp.zeros((frames, cols, chans), BF16)
    place = lax.broadcasted_iota(jnp.int32, (cells, 1), 0) % cols
    for c in range(3):
        moved = x
        if c != 1:
            good = (place + c - 1 >= 0) & (place + c - 1 < cols)
            moved = jnp.where(good, pltpu.roll(x, (1 - c) % cells, axis=0), 0.0)
        out_ref[c, :, 0] = zero
        out_ref[c, :, rows + 1] = zero
        out_ref[c, :, 1 : rows + 1] = moved.astype(BF16).reshape(frames, rows, cols, chans)


def window(ref, column, frame, row, frames, rows):
    x = ref[column, pl.ds(frame, frames), pl.ds(row, rows)]
    return x.reshape(frames * rows * x.shape[2], x.shape[3])


def front_kernel(crop_ref, w_ref, *refs, rows, cols, first):
    if first:
        patch_ref, z_ref, cells_ref, taps_ref, top_ref, full_ref = refs
    else:
        taps_ref, top_ref, full_ref = refs
    plane = rows * cols
    lat = crop_ref.shape[0]
    ext = full_ref.shape[1]
    count = ext - 2 * plane

    @pl.when(pl.program_id(0) == 0)
    def _():
        crop = crop_ref[...].astype(F32)
        for spot in range(9):
            moved = shifted(crop, spot // 3 - 1, spot % 3 - 1, rows, cols).astype(BF16)
            for depth in range(3):
                at = (depth * 9 + spot) * lat
                full_ref[at : at + lat, :] = moved[:, depth * plane : depth * plane + ext]
        if first:
            patch_ref[...] = full_ref[:, 2 * plane :]

    z = contract(w_ref[...], full_ref[...], ((0,), (0,)))
    act = (z * (1.0 / (1.0 + jnp.exp(-z)))).astype(BF16).astype(F32)
    top_ref[...] = jnp.broadcast_to(jnp.max(jnp.abs(act), axis=1, keepdims=True), top_ref.shape)
    for spot in range(9):
        moved = shifted(act, spot // 3 - 1, spot % 3 - 1, rows, cols).astype(BF16)
        for depth in range(3):
            taps_ref[depth * 9 + spot] = moved[:, depth * plane : depth * plane + count]
    if first:
        z_ref[...] = z[:, 2 * plane :].T
        fill_columns(cells_ref, act.T, rows, cols)


def front(crop_t, w_in, rows, cols, count, first):
    chans = w_in.shape[1]
    depth_in = w_in.shape[0]
    plane = rows * cols
    block = 128
    frames = count // plane + 2
    specs = [
        pl.BlockSpec((27, block, count), lambda i: (0, i, 0)),
        pl.BlockSpec((block, 128), lambda i: (i, 0)),
    ]
    shapes = [
        jax.ShapeDtypeStruct((27, chans, count), BF16),
        jax.ShapeDtypeStruct((chans, 128), F32),
    ]
    if first:
        specs = [
            pl.BlockSpec((depth_in, count), lambda i: (0, 0)),
            pl.BlockSpec((count, block), lambda i: (0, i)),
            pl.BlockSpec((3, frames, rows + 2, cols, block), lambda i: (0, 0, 0, 0, i)),
        ] + specs
        shapes = [
            jax.ShapeDtypeStruct((depth_in, count), BF16),
            jax.ShapeDtypeStruct((count, chans), F32),
            jax.ShapeDtypeStruct((3, frames, rows + 2, cols, chans), BF16),
        ] + shapes
    return pl.pallas_call(
        lambda *refs: front_kernel(*refs, rows=rows, cols=cols, first=first),
        grid=(chans // block,),
        in_specs=[
            pl.BlockSpec(crop_t.shape, lambda i: (0, 0)),
            pl.BlockSpec((depth_in, block), lambda i: (0, i)),
        ],
        out_specs=specs,
        out_shape=shapes,
        scratch_shapes=[pltpu.VMEM((depth_in, count + 2 * plane), BF16)],
        compiler_params=pltpu.CompilerParams(vmem_limit_bytes=VMEM),
        name="front",
    )(crop_t, w_in)


def middle_kernel(cells_ref, wide_ref, thin_ref, teacher_ref, g_ref, head_ref, acc_ref, *, scale):
    depth = pl.program_id(0)
    frames = cells_ref.shape[1] - 2
    rows = cells_ref.shape[2] - 2
    left = jnp.concatenate(
        [window(cells_ref, k % 3, depth, k // 3, frames, rows) for k in range(9)], axis=1
    )
    totals = []
    for ref in (wide_ref, thin_ref):
        totals.append(contract(left, ref[...].reshape(left.shape[1], ref.shape[2]), ((1,), (0,))))
    total = jnp.concatenate(totals, axis=1)

    @pl.when(depth == 0)
    def _():
        acc_ref[...] = total

    @pl.when(depth == 1)
    def _():
        acc_ref[...] += total

    @pl.when(depth == 2)
    def _():
        g = ((acc_ref[...] + total - teacher_ref[...].astype(F32)) * scale).astype(BF16)
        count = g.shape[0]
        g_ref[:count, :] = g
        head_ref[...] = g[: head_ref.shape[0]]
        size = jnp.max(jnp.sum(jnp.abs(g.astype(F32)), axis=0, keepdims=True), axis=1, keepdims=True)
        g_ref[count:, :] = jnp.broadcast_to(size, (g_ref.shape[0] - count, g.shape[1])).astype(BF16)


def middle(cells, wide, thin, teacher, scale, head):
    count, chans = teacher.shape
    return pl.pallas_call(
        lambda *refs: middle_kernel(*refs, scale=scale),
        grid=(3,),
        in_specs=[
            pl.BlockSpec(cells.shape, lambda i: (0,) * 5),
            pl.BlockSpec((9,) + wide.shape[1:], lambda i: (i, 0, 0)),
            pl.BlockSpec((9,) + thin.shape[1:], lambda i: (i, 0, 0)),
            pl.BlockSpec((count, chans), lambda i: (0, 0)),
        ],
        out_specs=[
            pl.BlockSpec((count + 16, chans), lambda i: (0, 0)),
            pl.BlockSpec((head, chans), lambda i: (0, 0)),
        ],
        out_shape=[
            jax.ShapeDtypeStruct((count + 16, chans), BF16),
            jax.ShapeDtypeStruct((head, chans), BF16),
        ],
        scratch_shapes=[pltpu.VMEM((count, chans), F32)],
        compiler_params=pltpu.CompilerParams(vmem_limit_bytes=VMEM),
        name="middle",
    )(cells, wide, thin, teacher)


def grad_kernel(order_ref, *refs, units, apart):
    out_ref = refs[-1]
    g_refs = refs[-4:-2] if apart else refs[-3:-1]
    at_once = out_ref.shape[0]
    rows = refs[0].shape[0]
    zero = jnp.zeros((out_ref.shape[1] - units * rows, out_ref.shape[2]), F32)
    for i in range(at_once):
        totals = []
        for k in range(units):
            at = 2 * (i * units + k)
            total = contract(refs[at][...], g_refs[0][...], ((1,), (0,)))
            total += contract(refs[at + 1][...], g_refs[1][...], ((1,), (0,)))
            totals.append(total)
        block = jnp.concatenate(totals + [zero], axis=0)
        if apart:
            @pl.when(pl.program_id(0) == 0)
            def _():
                refs[-2][...] = block

            @pl.when(pl.program_id(0) > 0)
            def _():
                out_ref[0] = block

        else:
            out_ref[i] = block


def grad_chunk(order, taps, g, first, units, apart):
    blocks = order.shape[0]
    total, count = taps[0].shape
    chans = g[0].shape[1]
    rows = total // (2 * blocks) // 3
    at_once = 2 // units
    tap_specs = []
    for i in range(at_once):
        for k in range(units):
            spec = pl.BlockSpec(
                (rows, count), lambda s, order, i=i, k=k: (order[s * at_once + i] * 3 + first + k, 0)
            )
            tap_specs += [spec, spec]
    whole = pl.BlockSpec((count, chans), lambda s, order: (0, 0))
    size = padded(rows * units)
    out_specs = [pl.BlockSpec((at_once, size, chans), lambda s, order: (jnp.maximum(s - apart, 0), 0, 0))]
    out_shape = [jax.ShapeDtypeStruct((blocks - apart, size, chans), F32)]
    if apart:
        out_specs = [pl.BlockSpec((size, chans), lambda s, order: (0, 0))] + out_specs
        out_shape = [jax.ShapeDtypeStruct((size, chans), F32)] + out_shape
    return pl.pallas_call(
        lambda *refs: grad_kernel(*refs, units=units, apart=apart),
        grid_spec=pltpu.PrefetchScalarGridSpec(
            num_scalar_prefetch=1,
            grid=(blocks // at_once,),
            in_specs=tap_specs + [whole, whole],
            out_specs=out_specs,
        ),
        out_shape=out_shape,
        compiler_params=pltpu.CompilerParams(vmem_limit_bytes=VMEM),
        name="grad",
    )(order, *(list(taps) * 2), *g)


def back_kernel(g_ref, later_ref, wide_ref, thin_ref, z_ref, patch_ref, out_ref, cells_ref, acc_ref, *, rows, cols):
    depth = pl.program_id(0)
    frames = cells_ref.shape[1] - 2

    @pl.when(depth == 0)
    def _():
        g = jnp.concatenate([g_ref[...], later_ref[...]], axis=0).astype(F32)
        fill_columns(cells_ref, g, rows, cols)

    taps = [window(cells_ref, 2 - k % 3, 2 - depth, 2 - k // 3, frames, rows) for k in range(9)]
    cut = wide_ref.shape[2]
    left = jnp.concatenate([x[:, :cut] for x in taps] + [x[:, cut:] for x in taps], axis=1)
    right = jnp.concatenate([wide_ref[k] for k in range(9)] + [thin_ref[k] for k in range(9)], axis=1)
    total = contract(left, right, ((1,), (1,)))

    @pl.when(depth == 0)
    def _():
        acc_ref[...] = total

    @pl.when(depth == 1)
    def _():
        acc_ref[...] += total

    @pl.when(depth == 2)
    def _():
        z = z_ref[...]
        sig = 1.0 / (1.0 + jnp.exp(-z))
        dz = ((acc_ref[...] + total) * sig * (1.0 + z * (1.0 - sig))).astype(BF16)
        out_ref[...] = contract(patch_ref[...], dz, ((1,), (0,)))


def back(g, later, wide, thin, z, patch_t, rows, cols):
    count, chans = z.shape
    depth_in = patch_t.shape[0]
    frames = count // (rows * cols) + 2
    return pl.pallas_call(
        lambda *refs: back_kernel(*refs, rows=rows, cols=cols),
        grid=(3,),
        in_specs=[
            pl.BlockSpec((count, chans), lambda i: (0, 0)),
            pl.BlockSpec(later.shape, lambda i: (0, 0)),
            pl.BlockSpec((9,) + wide.shape[1:], lambda i: (i, 0, 0)),
            pl.BlockSpec((9,) + thin.shape[1:], lambda i: (i, 0, 0)),
            pl.BlockSpec((count, chans), lambda i: (0, 0)),
            pl.BlockSpec((depth_in, count), lambda i: (0, 0)),
        ],
        out_specs=pl.BlockSpec((depth_in, chans), lambda i: (0, 0)),
        out_shape=jax.ShapeDtypeStruct((depth_in, chans), F32),
        scratch_shapes=[
            pltpu.VMEM((3, frames, rows + 2, cols, chans), BF16),
            pltpu.VMEM((count, chans), F32),
        ],
        compiler_params=pltpu.CompilerParams(vmem_limit_bytes=VMEM),
        name="back",
    )(g, later, wide, thin, z, patch_t)


def packed(x, rows, bound):
    power = jnp.ceil(jnp.log2(jnp.maximum(bound, 1e-30)))
    row = lax.broadcasted_iota(jnp.int32, x.shape, x.ndim - 2)
    return jnp.where(row < rows, x * jnp.exp2(14.0 - power), power).astype(F16)


def across_plane(part, rows, bound, after):
    clips = lax.axis_size("clip")
    payloads = [packed(part[q - 1], rows, bound) for q in range(1, clips // 2)]
    payloads, after = lax.optimization_barrier((payloads, after))
    got = []
    for q in range(1, clips // 2):
        route = [(i, i ^ (2 * q)) for i in range(clips)]
        got.append(lax.ppermute(payloads[q - 1], "clip", route))
    return got, after


def behind(x, *first):
    return lax.optimization_barrier((x, first))[0]


def around(blocks, distance):
    depth = lax.axis_size("tm")
    return lax.ppermute(blocks, "tm", [(i, (i + distance) % depth) for i in range(depth)])


def scales(got, rows, bound):
    powers = [jnp.exp2(x[rows : rows + 1].astype(F32)) for x in got]
    return [power * 2.0**-14 for power in powers], (bound + sum(powers)) * 1.01


def across_depth(own, got, rows, factors, total, after):
    depth = lax.axis_size("tm")
    me = lax.axis_index("tm")
    small = piece_rows(rows)

    def piece(place):
        cut = lambda x: lax.dynamic_slice_in_dim(x, place * small, small + 16, axis=0)
        terms = [cut(x).astype(F32) * factor for x, factor in zip(got, factors)]
        return sum(terms) if own is None else cut(own) + sum(terms)

    payloads = [packed(piece((me + d) % depth), small, total) for d in range(1, depth)]
    after = behind(after, payloads)
    others = [around(payloads[d - 1], d) for d in range(1, depth)]
    return (piece(me), others), after


def spread(parts, smalls, factors, total):
    depth = lax.axis_size("tm")
    sums = []
    for (own, got), small in zip(parts, smalls):
        terms = [x[:small].astype(F32) * factor for x, factor in zip(got, factors)]
        sums.append(own[:small] + sum(terms))
    rows = sum(smalls)
    payload = packed(jnp.pad(jnp.concatenate(sums, axis=0), ((0, 16), (0, 0))), rows, total)
    return [payload] + [around(payload, depth - k) for k in range(1, depth)]


def assembled(pieces, factors, smalls, rows):
    depth = lax.axis_size("tm")
    me = lax.axis_index("tm")
    pieces = [x.astype(F32) * factor for x, factor in zip(pieces, factors)]
    placed = []
    for place in range(depth):
        x = pieces[0]
        for k in range(1, depth):
            x = jnp.where((me + k) % depth == place, pieces[k], x)
        placed.append(x)
    out = []
    at = 0
    for small, count in zip(smalls, rows):
        for place in range(depth):
            left = min(small, count - place * small)
            if left > 0:
                out.append(placed[place][at : at + left])
        at += small
    return out


def shards(latent, offsets, teacher, w_in, w_mid):
    frames = teacher.shape[1]
    rows = teacher.shape[2]
    cols = teacher.shape[3]
    chans = teacher.shape[4]
    plane = rows * cols
    count = frames * plane
    lat_chans = latent.shape[4]
    clips = lax.axis_size("clip")
    total_cells = clips * lax.axis_size("tm") * count
    scale = 2.0 / math.sqrt(total_cells)
    me = lax.axis_index("clip")
    cut = chans - 128
    wide = lax.all_gather(w_mid[:, :cut], "clip", axis=0, tiled=True)
    strip = w_mid[:, cut:]
    strips = [strip]
    for q in range(1, clips // 2):
        strips.append(lax.ppermute(strip, "clip", [(i, i ^ (2 * q)) for i in range(clips)]))
    crop = lax.dynamic_slice_in_dim(latent[0], offsets[0], cols, axis=2).reshape(count, lat_chans).T
    earlier = passed_along(crop[:, count - 4 * plane :], "tm", 1)
    crop_ext = jnp.concatenate([earlier, crop], axis=1)
    patch_t, z, cells, taps, top = front(crop_ext, w_in, rows, cols, count, True)
    mine = jnp.concatenate(behind(strips, top), axis=0)
    theirs = swapped(mine)
    pair_taps, pair_top = front(behind(swapped(crop_ext), mine), w_in, rows, cols, count, False)
    taps = taps.reshape(27 * chans, count)
    pair_taps = pair_taps.reshape(27 * chans, count)
    top, pair_top = jnp.max(top), jnp.max(pair_top)
    block_rows = strip.shape[0]
    thin = jnp.zeros((clips * block_rows, 128), strip.dtype)
    for k in range(clips):
        source = theirs if k % 2 else mine
        piece = source[k // 2 * block_rows : (k // 2 + 1) * block_rows]
        thin = lax.dynamic_update_slice_in_dim(thin, piece, (me ^ k) * block_rows, axis=0)
    wide, thin, pair_taps, top, pair_top = lax.optimization_barrier((wide, thin, pair_taps, top, pair_top))
    wide = wide.reshape(27, chans, cut)
    thin = thin.reshape(27, chans, chans - cut)
    g, head = middle(cells, wide, thin, teacher[0].reshape(count, chans), scale, 2 * plane)
    pair_g = swapped(g)
    later = passed_along(head, "tm", -1)

    third = 27 * chans // clips // 3
    spare = slice(count, count + 1)
    bound = (top * g[spare, :1].astype(F32) + pair_top * pair_g[spare, :1].astype(F32)) * 1.03
    both = (taps, pair_taps)
    in_rows = patch_t.shape[0]

    chips = jnp.arange(clips // 2, dtype=jnp.int32)
    own_a, part = grad_chunk(me ^ (2 * chips), both, (g, pair_g), 0, 2, 1)
    part, later = lax.optimization_barrier((part, later))
    got_a, g = across_plane(part, 2 * third, bound, g)
    (part,) = grad_chunk(2 * chips + me % 2, both, (g, pair_g), 2, 1, 0)
    payload = packed(part, third, bound)
    payload, g = lax.optimization_barrier((payload, g))
    groups = [[2 * p + core for p in range(clips // 2)] for core in range(2)]
    got_b = lax.all_to_all(payload, "clip", 0, 0, axis_index_groups=groups, tiled=True)
    got_b = [got_b[p] for p in range(clips // 2)]
    in_part = back(g, later, wide, thin, z, patch_t, rows, cols)

    got_a = behind(got_a, in_part)
    factors, total = scales(got_a, 2 * third, bound)
    (own_a, depth_a), got_b = across_depth(own_a, got_a, 2 * third, factors, total, got_b)
    factors, _ = scales(got_b, third, 0.0)
    (own_b, depth_b), in_part = across_depth(None, got_b, third, factors, total, in_part)
    in_got = lax.all_to_all(in_part.reshape(clips, in_rows // clips, chans), "clip", 0, 0, tiled=True)
    z_total = total
    smalls = [piece_rows(2 * third), piece_rows(third)]
    factors, total = scales(depth_a, smalls[0], z_total)
    in_sum = behind(in_got, depth_a).sum(axis=0)
    in_sum = jnp.broadcast_to(in_sum[None], (lax.axis_size("tm"),) + in_sum.shape)
    depth_b = behind(depth_b, in_sum)
    in_got = lax.all_to_all(in_sum, "tm", 0, 0, tiled=True)
    last = spread([(own_a, depth_a), (own_b, depth_b)], smalls, factors, total)
    in_sum = behind(in_got, last[0]).sum(axis=0)
    in_sum = jnp.broadcast_to(in_sum[None], (clips,) + in_sum.shape)
    last[1:] = behind(last[1:], in_sum)
    grad_in = lax.all_to_all(in_sum, "clip", 0, 0, tiled=True).reshape(in_rows, chans)
    factors, _ = scales(last, sum(smalls), 0.0)
    pieces = assembled(last, factors, smalls, [2 * third, third])
    return (jnp.concatenate(pieces, axis=0), grad_in)


def solution(mesh):
    return jax.shard_map(
        shards,
        mesh=mesh,
        in_specs=(
            P("clip", "tm", None, None, None),
            P("clip"),
            P("clip", "tm", None, None, None),
            P(),
            P("clip", None),
        ),
        out_specs=(P("clip", None), P()),
        check_vma=False,
    )
```
